32 devices in a mesh: trc: 4 (over z), lat: 4 (over y, x), lon: 2 (over core).
Axes of the slice: x: 2, y: 2, z: 4, core: 2. Of those that a mesh axis runs over, the one named last changes fastest.
Arguments:
- tracers: float32 [8, 16, 128, 128], P('trc', 'lat', 'lon'), may hold values from -6 to 6
- land_mask: int32 [16, 128], P('lat', 'lon'), may hold values 0 or 1
- bottom_level: int32 [16, 128], P('lat', 'lon'), may hold values from 1 to 128
- bottom_part: float32 [16, 128], P('lat', 'lon'), may hold values from 0.05 to 1
- velocity: float32 [2, 2, 8, 32768], P(None, None, ('lat', 'lon'), 'trc'), may hold values from -0.45 to 0.45
- upwelling: float32 [2, 8, 32768], P(None, ('lat', 'lon'), 'trc'), may hold values from -0.3 to 0.3
- diffusivity: float32 [2, 8, 32768], P(None, ('lat', 'lon'), 'trc'), may hold values from 0.08 to 0.32
Outputs:
- tracers_out: float32 [8, 16, 128, 128], P('trc', 'lat', 'lon')
The draws below stay inside these ranges and needn't reach their ends.
All inputs are finite; a program needn't handle non-finite values. No bound on the sum of `land_mask` on one device may be relied on, other than what follows from the above.
Results may differ from the reference program's by a relative error of at most 0.0003.
Values sent between devices are 32-bit elements; how exact they have to be, the bound alone decides.
A program may use at most 64 MiB of HBM per device.

```python
import math
import jax
import jax.numpy as jnp
from jax import lax

ROWS = 4
COLS = 64
LEVELS = 128
STEPS = 2
NLAT = 16
NLON = 128
TRACERS = 8
BLOCKS = 8
CELLS_DEV = 32768
N_LAT = 4
N_LON = 2


def set_ends(drawn, own_key, least, high):
    spot = [jax.random.randint(jax.random.fold_in(own_key, axis), (), 0, length) for axis, length in enumerate(drawn.shape)]
    main_axis = drawn.shape.index(max(drawn.shape))
    neighbour = spot[:main_axis] + [(spot[main_axis] + 1) % drawn.shape[main_axis]] + spot[main_axis + 1:]
    return drawn.at[tuple(spot)].set(least).at[tuple(neighbour)].set(high)


def level_of(own_key, dims, shards, low, high):
    factor_of, own = 1.0, jax.random.fold_in(own_key, 6)
    for position, shards_of in shards:
        draws = jnp.exp(jax.random.uniform(jax.random.fold_in(own, position), (shards_of,), jnp.float32, low / len(shards), high / len(shards)))
        factor_of = factor_of * jnp.repeat(draws, dims[position] // shards_of).reshape([-1 if axis == position else 1 for axis in range(len(dims))])
    return factor_of


def noise(rng, shape, deviation, reach, split=(), dtype=jnp.bfloat16):
    values = deviation * jax.random.normal(rng, shape, jnp.float32)
    if split:
        values = values * level_of(rng, shape, split, -0.22, 0.18)
    return jnp.clip(values, -reach, reach).astype(dtype)


def setup_inputs(seed: int = 0) -> dict:
    key_list = jax.random.split(jax.random.key(seed), 8)
    tracers = noise(key_list[0], (TRACERS, NLAT, NLON, LEVELS), 1.0, 6.0, ((0, 4), (1, 4), (2, 2)), jnp.float32)
    land_mask = set_ends((jax.random.randint(key_list[1], (NLAT, NLON), 0, 8) < 7).astype(jnp.int32), jax.random.fold_in(key_list[1], 1), 0, 1)
    bottom_level = set_ends(jax.random.randint(key_list[2], (NLAT, NLON), 1, LEVELS + 1), jax.random.fold_in(key_list[2], 1), 1, LEVELS).astype(jnp.int32)
    bottom_part = jnp.clip(0.05 + 0.95 * jax.random.uniform(key_list[3], (NLAT, NLON), jnp.float32) ** level_of(key_list[3], (NLAT, NLON), ((0, 4), (1, 2)), -0.2, 0.2), 0.05, 1.0)
    velocity = jnp.clip(jax.random.uniform(key_list[4], (STEPS, 2, BLOCKS, CELLS_DEV), jnp.float32, -0.45, 0.45) * level_of(key_list[4], (STEPS, 2, BLOCKS, CELLS_DEV), ((2, 8), (3, 4)), -0.4, 0.0), -0.45, 0.45)
    upwelling = jnp.clip(jax.random.uniform(key_list[5], (STEPS, BLOCKS, CELLS_DEV), jnp.float32, -0.3, 0.3) * level_of(key_list[5], (STEPS, BLOCKS, CELLS_DEV), ((1, 8), (2, 4)), -0.4, 0.0), -0.3, 0.3)
    diffusivity = jnp.clip(jnp.exp(math.log(0.32) - 1.3862944 * jax.random.uniform(key_list[6], (STEPS, BLOCKS, CELLS_DEV), jnp.float32) ** level_of(key_list[6], (STEPS, BLOCKS, CELLS_DEV), ((1, 8), (2, 4)), -0.2, 0.2)), 0.08, 0.32)
    return {"tracers": tracers, "land_mask": land_mask, "bottom_level": bottom_level, "bottom_part": bottom_part, "velocity": velocity, "upwelling": upwelling, "diffusivity": diffusivity}


fraction_floor = 0.25


def minmod(first, second):
    return 0.5 * (jnp.sign(first) + jnp.sign(second)) * jnp.minimum(jnp.abs(first), jnp.abs(second))


def window(array, start, stop, offset):
    return lax.slice_in_dim(array, start, stop, axis=array.ndim + offset)


def face_divergence(field, speed, mixing, fraction, offset):
    extent = field.shape[field.ndim + offset]
    before = window(field, 0, extent - 3, offset)
    lower = window(field, 1, extent - 2, offset)
    upper = window(field, 2, extent - 1, offset)
    after = window(field, 3, extent, offset)
    face_speed = 0.5 * (window(speed, 1, extent - 2, offset) + window(speed, 2, extent - 1, offset))
    face_area = jnp.minimum(window(fraction, 1, extent - 2, offset), window(fraction, 2, extent - 1, offset))
    face_mixing = 0.5 * (window(mixing, 1, extent - 2, offset) + window(mixing, 2, extent - 1, offset))
    jump = upper - lower
    damping = 0.5 * (1.0 - jnp.abs(face_speed))
    from_lower = lower + damping * minmod(lower - before, jump)
    from_upper = upper - damping * minmod(jump, after - upper)
    face_value = jnp.where(face_speed >= 0.0, from_lower, from_upper)
    face_flux = face_area * (face_speed * face_value - face_mixing * jump)
    return window(face_flux, 1, extent - 3, offset) - window(face_flux, 0, extent - 4, offset)


def substep(field, fraction, eastward, northward, mixing, rising):
    across_rows = face_divergence(field, northward, mixing, fraction, -3)[..., 2:-2, :]
    across_cols = face_divergence(field, eastward, mixing, fraction, -2)[..., 2:-2, :, :]
    centre = field[..., 2:-2, 2:-2, :]
    wet_share = fraction[2:-2, 2:-2, :]
    top_area = jnp.minimum(wet_share[:, :, :-1], wet_share[:, :, 1:])
    lifting = rising[:, :, :-1]
    carried = jnp.where(lifting >= 0.0, centre[..., :-1], centre[..., 1:])
    vertical = top_area * lifting * carried
    closed = jnp.zeros(vertical.shape[:-1] + (1,), jnp.float32)
    across_levels = jnp.concatenate([vertical, closed], axis=-1) - jnp.concatenate([closed, vertical], axis=-1)
    return centre - (across_rows + across_cols + across_levels) / jnp.maximum(wet_share, fraction_floor)


def cell_fraction(land_mask, bottom_level, bottom_part, levels):
    level_index = lax.broadcasted_iota(jnp.int32, land_mask.shape + (levels,), 2)
    deepest = bottom_level[:, :, None].astype(jnp.int32) - 1
    full_cell = (level_index < deepest).astype(jnp.float32)
    last_cell = (level_index == deepest).astype(jnp.float32) * bottom_part[:, :, None]
    return land_mask.astype(jnp.float32)[:, :, None] * (full_cell + last_cell)


def unblock(array):
    leading = array.shape[:-2]
    array = array.reshape(leading + (N_LAT, N_LON, ROWS, COLS, LEVELS))
    array = jnp.swapaxes(array, -4, -3)
    return array.reshape(leading + (N_LAT * ROWS, N_LON * COLS, LEVELS))


def widen(array):
    return jnp.pad(array, ((2, 2), (2, 2), (0, 0)))


def reference(tracers, land_mask, bottom_level, bottom_part, velocity, upwelling, diffusivity):
    fraction = cell_fraction(land_mask, bottom_level, bottom_part, LEVELS)
    speeds = unblock(velocity)
    rises = unblock(upwelling)
    mixes = unblock(diffusivity)
    wide_frac = widen(fraction)

    def advance(field):
        for number in range(STEPS):
            field = substep(widen(field), wide_frac, widen(speeds[number, 0]), widen(speeds[number, 1]),
                            widen(mixes[number]), rises[number])
        return field

    return lax.map(advance, tracers)
```

```python
import functools

import jax
import jax.numpy as jnp
from jax import lax
from jax.experimental import pallas as pl
from jax.experimental.pallas import tpu as pltpu
from jax.sharding import PartitionSpec as P

STEPS = 2
MESH = pl.DeviceIdType.MESH


fraction_floor = 0.25


def with_halo(block, sides, width):
    for axis, dim in sides:
        count = lax.axis_size(axis)
        forward = [(i, i + 1) for i in range(count - 1)]
        backward = [(target, source) for source, target in forward]
        low = lax.ppermute(
            lax.slice_in_dim(block, block.shape[dim] - width, None, axis=dim), axis, forward
        )
        high = lax.ppermute(lax.slice_in_dim(block, 0, width, axis=dim), axis, backward)
        block = jnp.concatenate([low, block, high], axis=dim)
    return block


def minmod(first, second):
    return 0.5 * (jnp.sign(first) + jnp.sign(second)) * jnp.minimum(jnp.abs(first), jnp.abs(second))


def window(array, start, stop, offset):
    return lax.slice_in_dim(array, start, stop, axis=array.ndim + offset)


def face_divergence(field, speed, mixing, fraction, offset):
    extent = field.shape[field.ndim + offset]
    before = window(field, 0, extent - 3, offset)
    lower = window(field, 1, extent - 2, offset)
    upper = window(field, 2, extent - 1, offset)
    after = window(field, 3, extent, offset)
    face_speed = 0.5 * (window(speed, 1, extent - 2, offset) + window(speed, 2, extent - 1, offset))
    face_area = jnp.minimum(
        window(fraction, 1, extent - 2, offset), window(fraction, 2, extent - 1, offset)
    )
    face_mixing = 0.5 * (
        window(mixing, 1, extent - 2, offset) + window(mixing, 2, extent - 1, offset)
    )
    jump = upper - lower
    damping = 0.5 * (1.0 - jnp.abs(face_speed))
    from_lower = lower + damping * minmod(lower - before, jump)
    from_upper = upper - damping * minmod(jump, after - upper)
    face_value = jnp.where(face_speed >= 0.0, from_lower, from_upper)
    face_flux = face_area * (face_speed * face_value - face_mixing * jump)
    return window(face_flux, 1, extent - 3, offset) - window(face_flux, 0, extent - 4, offset)


def substep(field, fraction, eastward, northward, mixing, rising):
    across_rows = face_divergence(field, northward, mixing, fraction, -3)[..., 2:-2, :]
    across_cols = face_divergence(field, eastward, mixing, fraction, -2)[..., 2:-2, :, :]
    centre = field[..., 2:-2, 2:-2, :]
    wet_share = fraction[2:-2, 2:-2, :]
    top_area = jnp.minimum(wet_share[:, :, :-1], wet_share[:, :, 1:])
    lifting = rising[:, :, :-1]
    carried = jnp.where(lifting >= 0.0, centre[..., :-1], centre[..., 1:])
    vertical = top_area * lifting * carried
    closed = jnp.zeros(vertical.shape[:-1] + (1,), jnp.float32)
    across_levels = jnp.concatenate([vertical, closed], axis=-1) - jnp.concatenate(
        [closed, vertical], axis=-1
    )
    return centre - (across_rows + across_cols + across_levels) / jnp.maximum(
        wet_share, fraction_floor
    )


def cell_fraction(land_mask, bottom_level, bottom_part, levels):
    level_index = lax.broadcasted_iota(jnp.int32, land_mask.shape + (levels,), 2)
    deepest = bottom_level[:, :, None] - 1
    full_cell = (level_index < deepest).astype(jnp.float32)
    last_cell = (level_index == deepest).astype(jnp.float32) * bottom_part[:, :, None]
    return land_mask.astype(jnp.float32)[:, :, None] * (full_cell + last_cell)


def gathered_body(tracers, land_mask, bottom_level, bottom_part, velocity, upwelling, diffusivity):
    levels = tracers.shape[3]
    block_shape = (tracers.shape[1], tracers.shape[2], levels)
    fraction = cell_fraction(land_mask, bottom_level, bottom_part, levels)
    tracer_count = tracers.shape[0]
    moved = (
        lax.all_gather(velocity, "trc", axis=3, tiled=True),
        lax.all_gather(upwelling, "trc", axis=2, tiled=True),
        lax.all_gather(diffusivity, "trc", axis=2, tiled=True),
    )
    speeds = moved[0].reshape((STEPS, 2) + block_shape)
    rises = moved[1].reshape((STEPS,) + block_shape)
    mixes = moved[2].reshape((STEPS,) + block_shape)
    field = tracers
    wide_frac = fraction
    for number in range(STEPS):
        extras = [fraction[None]] if number == 0 else []
        stack = jnp.concatenate(
            [field] + extras + [jnp.stack([speeds[number, 0], speeds[number, 1], mixes[number]])],
            axis=0,
        )
        widened = with_halo(stack, (("lat", 1), ("lon", 2)), 2)
        if number == 0:
            wide_frac = widened[tracer_count]
        flows = widened[-3:]
        field = substep(
            widened[:tracer_count], wide_frac, flows[0], flows[1], flows[2], rises[number]
        )
    return field


U, K, V, W = range(4)
PAD = 8
CHUNK = 16


def limited_flux(before, lower, upper, after, east, scale, area_speed, area_mix):
    jump = upper - lower
    base = jnp.where(east, lower, upper)
    slope = jnp.where(east, lower - before, after - upper)
    limited = jnp.maximum(jnp.minimum(slope, jump), 0.0) + jnp.minimum(
        jnp.maximum(slope, jump), 0.0
    )
    return area_speed * (base + scale * limited) - area_mix * jump


def face_terms(speed_p, speed_q, mix_p, mix_q, frac_p, frac_q):
    speed = 0.5 * (speed_p + speed_q)
    area = jnp.minimum(frac_p, frac_q)
    east = speed >= 0.0
    damping = 0.5 * (1.0 - jnp.abs(speed))
    return east, jnp.where(east, damping, -damping), area * speed, area * (0.5 * (mix_p + mix_q))


def transport_kernel(
    counts, tr_hbm, vel_hbm, up_hbm, dif_hbm, mask_hbm, level_hbm, part_hbm, out_ref,
    c0, c1, flow, frac, rflux, xflux, mask_ref, level_ref, part_ref,
    own_sem, in_sem, column_sem, zs, zr, fs, cs, cr, fls, flr, frs, frr,
):
    n, n_lat, n_lon = counts
    tracer_count, rows, cols, levels = tr_hbm.shape
    t, la, lo = lax.axis_index("trc"), lax.axis_index("lat"), lax.axis_index("lon")
    inner = pl.ds(PAD, cols)
    left_halo, right_halo = pl.ds(0, PAD), pl.ds(PAD + cols, PAD)
    left_edge, right_edge = pl.ds(PAD, PAD), pl.ds(cols, PAD)

    sides = (
        (la > 0, {"lat": la - 1}),
        (la < n_lat - 1, {"lat": la + 1}),
        (lo > 0, {"lon": lo - 1}),
        (lo < n_lon - 1, {"lon": lo + 1}),
    )
    shifts = (2, -2, 1, -1)
    groups = (
        (t < n - 2, {"trc": t + 2}), (t >= 2, {"trc": t - 2}),
        (t < n - 1, {"trc": t + 1}), (t > 0, {"trc": t - 1}),
    )
    relays = ((t == n - 2, n - 1, (0,)), (t == 1, 0, (n - 1,)))

    columns = [
        pltpu.make_async_copy(src, dst, column_sem.at[i])
        for i, (src, dst) in enumerate(
            ((mask_hbm, mask_ref), (level_hbm, level_ref), (part_hbm, part_ref)))
    ]
    for copy in columns:
        copy.start()
    barrier = pltpu.get_barrier_semaphore()
    partners = sides + groups
    for there, device in partners:
        @pl.when(there)
        def _(device=device):
            pl.semaphore_signal(barrier, inc=1, device_id=device, device_id_type=MESH)

    def source(s, f):
        return {
            U: lambda: vel_hbm.at[s, 0], V: lambda: vel_hbm.at[s, 1],
            K: lambda: dif_hbm.at[s], W: lambda: up_hbm.at[s],
        }[f]()

    def group_copy(s, f, i):
        return pltpu.make_async_remote_copy(
            src_ref=source(s, f), dst_ref=flow.at[s, f, 1 + t, inner],
            send_sem=zs.at[s, f, i], recv_sem=zr.at[s, f, t],
            device_id=groups[i][1], device_id_type=MESH,
        )

    def forward_copy(s, f, r, target, slot=0):
        return pltpu.make_async_remote_copy(
            src_ref=flow.at[s, f, 1 + r, inner], dst_ref=flow.at[s, f, 1 + r, inner],
            send_sem=fs.at[s, f, slot], recv_sem=zr.at[s, f, r],
            device_id={"trc": target}, device_id_type=MESH,
        )

    def own_copy(s, f):
        return pltpu.make_async_copy(
            source(s, f), flow.at[s, f, 1 + t, inner], own_sem.at[s, f]
        )

    def side_copy(src, dst, send, recv, i):
        return pltpu.make_async_remote_copy(
            src_ref=src, dst_ref=dst, send_sem=send.at[i], recv_sem=recv.at[i],
            device_id=sides[i][1], device_id_type=MESH,
        )

    def field_copy(s, i):
        dst = c0 if s == 0 else c1
        if s == 0:
            srcs = (
                tr_hbm.at[:, pl.ds(0, 2)], tr_hbm.at[:, pl.ds(rows - 2, 2)],
                tr_hbm.at[:, :, pl.ds(0, PAD)], tr_hbm.at[:, :, pl.ds(cols - PAD, PAD)],
            )
        else:
            srcs = (
                c1.at[:, pl.ds(2, 2), inner], c1.at[:, pl.ds(rows, 2), inner],
                c1.at[:, pl.ds(2, rows), left_edge], c1.at[:, pl.ds(2, rows), right_edge],
            )
        dsts = (
            dst.at[:, pl.ds(rows + 2, 2), inner], dst.at[:, pl.ds(0, 2), inner],
            dst.at[:, pl.ds(2, rows), right_halo], dst.at[:, pl.ds(2, rows), left_halo],
        )
        return side_copy(srcs[i], dsts[i], cs.at[s], cr.at[s], i)

    def frac_copy(i):
        body = pl.ds(1, rows)
        srcs = (frac.at[1, inner], frac.at[rows, inner],
                frac.at[body, left_edge], frac.at[body, right_edge])
        dsts = (frac.at[rows + 1, inner], frac.at[0, inner],
                frac.at[body, right_halo], frac.at[body, left_halo])
        return side_copy(srcs[i], dsts[i], frs, frr, i)

    def flow_copy(s, i):
        body = pl.ds(1, rows)
        kv, uk = pl.ds(K, 2), pl.ds(U, 2)
        srcs = (flow.at[s, kv, 1, inner], flow.at[s, kv, rows, inner],
                flow.at[s, uk, body, left_edge], flow.at[s, uk, body, right_edge])
        dsts = (flow.at[s, kv, rows + 1, inner], flow.at[s, kv, 0, inner],
                flow.at[s, uk, body, right_halo], flow.at[s, uk, body, left_halo])
        return side_copy(srcs[i], dsts[i], fls.at[s], flr.at[s], i)

    opposite = (1, 0, 3, 2)

    def on_sides(make, which, act):
        for i in which:
            @pl.when(sides[i][0])
            def _(i=i):
                getattr(make(i), act)()

    def receive(make, which):
        for i in which:
            @pl.when(sides[opposite[i]][0])
            def _(i=i):
                make(i).wait_recv()

    def send_rows(s, fields, slots, when=None):
        for f in fields:
            for i in slots:
                @pl.when(groups[i][0] if when is None else groups[i][0] & when)
                def _(f=f, i=i):
                    group_copy(s, f, i).start()

    far, near = (0, 1), (2, 3)
    ends = (t == 0) | (t == n - 1)
    middle = jnp.logical_not(ends)
    own_field = pltpu.make_async_copy(tr_hbm, c0.at[:, pl.ds(2, rows), inner], in_sem)
    own_field.start()
    for f in (K, V, U, W):
        own_copy(0, f).start()
    for f in (K, V, U, W):
        own_copy(1, f).start()

    square = (cols, cols)
    eye = lax.broadcasted_iota(jnp.int32, square, 0) == lax.broadcasted_iota(jnp.int32, square, 1)
    level = lax.broadcasted_iota(jnp.int32, (cols, levels), 1).astype(jnp.float32)

    def upright(row):
        return jnp.sum(jnp.where(eye, jnp.broadcast_to(row, square), 0.0), axis=1, keepdims=True)

    for copy in columns:
        copy.wait()
    for r in range(rows):
        wet = mask_ref[r:r + 1, :].astype(jnp.float32)
        deepest = upright(level_ref[r:r + 1, :].astype(jnp.float32) - 1.0)
        share = upright(wet * part_ref[r:r + 1, :])
        wet = upright(wet)
        frac[1 + r, inner, :] = jnp.where(
            level < deepest, wet, jnp.where(level == deepest, share, 0.0)
        )

    @pl.when(la == 0)
    def _():
        for field in (c0, c1):
            field[:, 0:2] = jnp.zeros((tracer_count, 2) + field.shape[2:], jnp.float32)
        frac[0] = jnp.zeros(frac.shape[1:], jnp.float32)
        flow[:, :, 0] = jnp.zeros((STEPS, 4) + flow.shape[3:], jnp.float32)

    @pl.when(la == n_lat - 1)
    def _():
        for field in (c0, c1):
            field[:, rows + 2:] = jnp.zeros((tracer_count, 2) + field.shape[2:], jnp.float32)
        frac[rows + 1] = jnp.zeros(frac.shape[1:], jnp.float32)
        flow[:, :, rows + 1] = jnp.zeros((STEPS, 4) + flow.shape[3:], jnp.float32)

    for at_edge, strip in ((lo == 0, left_halo), (lo == n_lon - 1, right_halo)):
        @pl.when(at_edge)
        def _(strip=strip):
            for field in (c0, c1):
                field[:, 2:2 + rows, strip] = jnp.zeros(
                    (tracer_count, rows, PAD, levels), jnp.float32)
            frac[1:1 + rows, strip] = jnp.zeros((rows, PAD, levels), jnp.float32)
            flow[:, :, 1:1 + rows, strip] = jnp.zeros((STEPS, 4, rows, PAD, levels), jnp.float32)

    total = 0
    for there, _ in partners:
        total = total + jnp.where(there, 1, 0)
    pl.semaphore_wait(barrier, total)

    on_sides(frac_copy, range(4), "start")
    send_rows(0, (K, V), far + near)
    send_rows(1, (K, V), far + near, ends)
    on_sides(functools.partial(field_copy, 0), range(4), "start")
    send_rows(0, (U, W), far + near)
    send_rows(1, (U, W), far + near, ends)

    own_field.wait()
    receive(frac_copy, range(4))

    def arrive(s, f, r):
        @pl.when(t == r)
        def _():
            own_copy(s, f).wait()

        relayed = ((t == n - 2) & (r == 0)) | ((t == 1) & (r == n - 1))

        @pl.when((t != r) & jnp.logical_not(relayed))
        def _():
            forward_copy(s, f, r, t).wait_recv()

    def relay(s, f):
        for here, target, sources in relays:
            @pl.when(here)
            def _(target=target, sources=sources):
                for slot, r in enumerate(sources):
                    forward_copy(s, f, r, t).wait_recv()
                    forward_copy(s, f, r, target, slot).start()

    def edge_rows(s):
        for f in (K, V):
            for r in (0, n - 1):
                arrive(s, f, r)
        on_sides(functools.partial(flow_copy, s), (0, 1), "start")

    def mixed_columns(s):
        for f, those in ((K, (1, 2)), (V, (1, 2)), (U, (1, 2, 0, 3))):
            for r in those:
                arrive(s, f, r)
        on_sides(functools.partial(flow_copy, s), (2, 3), "start")
        for r in range(n):
            arrive(s, W, r)

    def collect_halos(s):
        receive(functools.partial(field_copy, s), range(4))
        receive(functools.partial(flow_copy, s), range(4))

    last_level = lax.broadcasted_iota(jnp.int32, (CHUNK, levels), 1) == levels - 1

    def advance(s, src, write):
        @pl.loop(0, rows + 1)
        def _(i):
            for c in range(0, cols, CHUNK):
                at = pl.ds(PAD + c, CHUNK)
                terms = face_terms(
                    flow[s, V, i, at], flow[s, V, i + 1, at],
                    flow[s, K, i, at], flow[s, K, i + 1, at], frac[i, at], frac[i + 1, at],
                )
                for a in range(tracer_count):
                    rflux[a, i, pl.ds(c, CHUNK)] = limited_flux(
                        src[a, i, at], src[a, i + 1, at], src[a, i + 2, at], src[a, i + 3, at],
                        *terms,
                    )

        @pl.loop(0, rows)
        def _(r):
            for c, size in [(c, CHUNK) for c in range(0, cols, CHUNK)] + [(cols - 7, 8)]:
                p, q = pl.ds(PAD + c - 1, size), pl.ds(PAD + c, size)
                terms = face_terms(
                    flow[s, U, r + 1, p], flow[s, U, r + 1, q],
                    flow[s, K, r + 1, p], flow[s, K, r + 1, q], frac[r + 1, p], frac[r + 1, q],
                )
                for a in range(tracer_count):
                    xflux[a, pl.ds(c, size)] = limited_flux(
                        src[a, r + 2, pl.ds(PAD + c - 2, size)], src[a, r + 2, p],
                        src[a, r + 2, q], src[a, r + 2, pl.ds(PAD + c + 1, size)], *terms,
                    )
            for c in range(0, cols, CHUNK):
                at = pl.ds(PAD + c, CHUNK)
                share = frac[r + 1, at]
                rise = flow[s, W, r + 1, at]
                area = jnp.where(
                    last_level, 0.0, jnp.minimum(share, pltpu.roll(share, levels - 1, 1))
                )
                lifted = area * rise
                upward = rise >= 0.0
                inverse = 1.0 / jnp.maximum(share, fraction_floor)
                for a in range(tracer_count):
                    centre = src[a, r + 2, at]
                    vertical = lifted * jnp.where(
                        upward, centre, pltpu.roll(centre, levels - 1, 1)
                    )
                    net = (
                        (rflux[a, r + 1, pl.ds(c, CHUNK)] - rflux[a, r, pl.ds(c, CHUNK)])
                        + (xflux[a, pl.ds(c + 1, CHUNK)] - xflux[a, pl.ds(c, CHUNK)])
                        + (vertical - pltpu.roll(vertical, 1, 1))
                    )
                    write(a, r, c, centre - net * inverse)

    def write_middle(a, r, c, value):
        c1[a, r + 2, pl.ds(PAD + c, CHUNK)] = value

    def write_out(a, r, c, value):
        out_ref[a, r, pl.ds(c, CHUNK)] = value

    for f in (K, V):
        relay(0, f)
    edge_rows(0)
    for f in (K, V):
        relay(1, f)
    relay(0, U)
    relay(0, W)
    send_rows(1, (K, V), near + far, middle)
    edge_rows(1)
    mixed_columns(0)
    collect_halos(0)
    advance(0, c0, write_middle)
    send_rows(1, (U, W), far + near, middle)
    on_sides(functools.partial(field_copy, 1), range(4), "start")
    for f in (U, W):
        relay(1, f)
    mixed_columns(1)
    collect_halos(1)
    advance(1, c1, write_out)

    for s in range(STEPS):
        for f in range(4):
            for i in range(len(shifts)):
                @pl.when(groups[i][0])
                def _(s=s, f=f, i=i):
                    group_copy(s, f, i).wait_send()

            @pl.when((t == 1) | (t == n - 2))
            def _(s=s, f=f):
                for slot in range(1):
                    forward_copy(s, f, 0, t, slot).wait_send()
        on_sides(functools.partial(field_copy, s), range(4), "wait_send")
        on_sides(functools.partial(flow_copy, s), range(4), "wait_send")
    on_sides(frac_copy, range(4), "wait_send")


def fused_body(counts, tracers, land_mask, bottom_level, bottom_part, velocity, upwelling,
               diffusivity):
    tracer_count, rows, cols, levels = tracers.shape
    wide = cols + 2 * PAD
    row = (cols, levels)
    dma = pltpu.SemaphoreType.DMA
    hbm, vmem = pl.BlockSpec(memory_space=pltpu.HBM), pl.BlockSpec(memory_space=pltpu.VMEM)
    return pl.pallas_call(
        functools.partial(transport_kernel, counts),
        out_shape=pltpu.VMEM(tracers.shape, jnp.float32),
        in_specs=[hbm] * 7,
        out_specs=vmem,
        scratch_shapes=[
            pltpu.VMEM((tracer_count, rows + 4, wide, levels), jnp.float32),
            pltpu.VMEM((tracer_count, rows + 4, wide, levels), jnp.float32),
            pltpu.VMEM((STEPS, 4, rows + 2, wide, levels), jnp.float32),
            pltpu.VMEM((rows + 2, wide, levels), jnp.float32),
            pltpu.VMEM((tracer_count, rows + 1, cols, levels), jnp.float32),
            pltpu.VMEM((tracer_count, cols + 8, levels), jnp.float32),
            pltpu.VMEM((rows, cols), jnp.int32),
            pltpu.VMEM((rows, cols), jnp.int32),
            pltpu.VMEM((rows, cols), jnp.float32),
            dma((STEPS, 4)), dma, dma((3,)),
            dma((STEPS, 4, 4)), dma((STEPS, 4, counts[0])), dma((STEPS, 4, 2)),
            dma((STEPS, 4)), dma((STEPS, 4)),
            dma((STEPS, 4)), dma((STEPS, 4)),
            dma((4,)), dma((4,)),
        ],
        compiler_params=pltpu.CompilerParams(
            collective_id=0, has_side_effects=True, vmem_limit_bytes=60 * 1024 * 1024
        ),
    )(
        tracers,
        velocity.reshape((STEPS, 2) + row),
        upwelling.reshape((STEPS,) + row),
        diffusivity.reshape((STEPS,) + row),
        land_mask, bottom_level, bottom_part,
    )


def solution(mesh):
    placed = (
        P("trc", "lat", "lon", None),
        P("lat", "lon"),
        P("lat", "lon"),
        P("lat", "lon"),
        P(None, None, ("lat", "lon"), "trc"),
        P(None, ("lat", "lon"), "trc"),
        P(None, ("lat", "lon"), "trc"),
    )
    counts = tuple(mesh.shape[axis] for axis in ("trc", "lat", "lon"))

    def body(*arrays):
        tracers, velocity = arrays[0], arrays[4]
        one_row = velocity.shape[3] == tracers.shape[2] * tracers.shape[3]
        if counts[0] == 4 and tracers.shape[1] == 4 and one_row:
            return fused_body(counts, *arrays)
        return gathered_body(*arrays)

    return jax.shard_map(
        body, mesh=mesh, in_specs=placed, out_specs=P("trc", "lat", "lon", None), check_vma=False
    )
```

```python
import functools

import jax
import jax.numpy as jnp
from jax import lax
from jax.experimental import pallas as pl
from jax.experimental.pallas import tpu as pltpu
from jax.sharding import PartitionSpec as P

STEPS = 2
MESH = pl.DeviceIdType.MESH


fraction_floor = 0.25


def with_halo(block, sides, width):
    for axis, dim in sides:
        count = lax.axis_size(axis)
        forward = [(i, i + 1) for i in range(count - 1)]
        backward = [(target, source) for source, target in forward]
        low = lax.ppermute(
            lax.slice_in_dim(block, block.shape[dim] - width, None, axis=dim), axis, forward
        )
        high = lax.ppermute(lax.slice_in_dim(block, 0, width, axis=dim), axis, backward)
        block = jnp.concatenate([low, block, high], axis=dim)
    return block


def minmod(first, second):
    return 0.5 * (jnp.sign(first) + jnp.sign(second)) * jnp.minimum(jnp.abs(first), jnp.abs(second))


def window(array, start, stop, offset):
    return lax.slice_in_dim(array, start, stop, axis=array.ndim + offset)


def face_divergence(field, speed, mixing, fraction, offset):
    extent = field.shape[field.ndim + offset]
    before = window(field, 0, extent - 3, offset)
    lower = window(field, 1, extent - 2, offset)
    upper = window(field, 2, extent - 1, offset)
    after = window(field, 3, extent, offset)
    face_speed = 0.5 * (window(speed, 1, extent - 2, offset) + window(speed, 2, extent - 1, offset))
    face_area = jnp.minimum(
        window(fraction, 1, extent - 2, offset), window(fraction, 2, extent - 1, offset)
    )
    face_mixing = 0.5 * (
        window(mixing, 1, extent - 2, offset) + window(mixing, 2, extent - 1, offset)
    )
    jump = upper - lower
    damping = 0.5 * (1.0 - jnp.abs(face_speed))
    from_lower = lower + damping * minmod(lower - before, jump)
    from_upper = upper - damping * minmod(jump, after - upper)
    face_value = jnp.where(face_speed >= 0.0, from_lower, from_upper)
    face_flux = face_area * (face_speed * face_value - face_mixing * jump)
    return window(face_flux, 1, extent - 3, offset) - window(face_flux, 0, extent - 4, offset)


def substep(field, fraction, eastward, northward, mixing, rising):
    across_rows = face_divergence(field, northward, mixing, fraction, -3)[..., 2:-2, :]
    across_cols = face_divergence(field, eastward, mixing, fraction, -2)[..., 2:-2, :, :]
    centre = field[..., 2:-2, 2:-2, :]
    wet_share = fraction[2:-2, 2:-2, :]
    top_area = jnp.minimum(wet_share[:, :, :-1], wet_share[:, :, 1:])
    lifting = rising[:, :, :-1]
    carried = jnp.where(lifting >= 0.0, centre[..., :-1], centre[..., 1:])
    vertical = top_area * lifting * carried
    closed = jnp.zeros(vertical.shape[:-1] + (1,), jnp.float32)
    across_levels = jnp.concatenate([vertical, closed], axis=-1) - jnp.concatenate(
        [closed, vertical], axis=-1
    )
    return centre - (across_rows + across_cols + across_levels) / jnp.maximum(
        wet_share, fraction_floor
    )


def cell_fraction(land_mask, bottom_level, bottom_part, levels):
    level_index = lax.broadcasted_iota(jnp.int32, land_mask.shape + (levels,), 2)
    deepest = bottom_level[:, :, None] - 1
    full_cell = (level_index < deepest).astype(jnp.float32)
    last_cell = (level_index == deepest).astype(jnp.float32) * bottom_part[:, :, None]
    return land_mask.astype(jnp.float32)[:, :, None] * (full_cell + last_cell)


def gathered_body(tracers, land_mask, bottom_level, bottom_part, velocity, upwelling, diffusivity):
    levels = tracers.shape[3]
    block_shape = (tracers.shape[1], tracers.shape[2], levels)
    fraction = cell_fraction(land_mask, bottom_level, bottom_part, levels)
    tracer_count = tracers.shape[0]
    moved = (
        lax.all_gather(velocity, "trc", axis=3, tiled=True),
        lax.all_gather(upwelling, "trc", axis=2, tiled=True),
        lax.all_gather(diffusivity, "trc", axis=2, tiled=True),
    )
    speeds = moved[0].reshape((STEPS, 2) + block_shape)
    rises = moved[1].reshape((STEPS,) + block_shape)
    mixes = moved[2].reshape((STEPS,) + block_shape)
    field = tracers
    wide_frac = fraction
    for number in range(STEPS):
        extras = [fraction[None]] if number == 0 else []
        stack = jnp.concatenate(
            [field] + extras + [jnp.stack([speeds[number, 0], speeds[number, 1], mixes[number]])],
            axis=0,
        )
        widened = with_halo(stack, (("lat", 1), ("lon", 2)), 2)
        if number == 0:
            wide_frac = widened[tracer_count]
        flows = widened[-3:]
        field = substep(
            widened[:tracer_count], wide_frac, flows[0], flows[1], flows[2], rises[number]
        )
    return field


W, U, K, V = range(4)
PAD = 8
TILE = 8
PARTS = 4
LEAD = 12
LAG = 1
AHEAD = 3
DIRECT = 2
PASSES = {0: (0,), 1: (1,), 2: (2, 3)}
WINDOWS = (1, 2, 2, 3)


def limited_flux(before, lower, upper, after, east, scale, area_speed, area_mix):
    jump = upper - lower
    base = jnp.where(east, lower, upper)
    slope = jnp.where(east, lower - before, after - upper)
    limited = jnp.maximum(jnp.minimum(slope, jump), 0.0) + jnp.minimum(
        jnp.maximum(slope, jump), 0.0
    )
    return area_speed * (base + scale * limited) - area_mix * jump


def face_terms(speed_p, speed_q, mix_p, mix_q, frac_p, frac_q):
    speed = 0.5 * (speed_p + speed_q)
    area = jnp.minimum(frac_p, frac_q)
    east = speed >= 0.0
    damping = 0.5 * (1.0 - jnp.abs(speed))
    return east, jnp.where(east, damping, -damping), area * speed, area * (0.5 * (mix_p + mix_q))


def arrival_order():
    flat = [(s, k) for s in range(STEPS) for k in range(PARTS)]
    order = [(0, K, 0)]
    ahead = 1
    for i, (s, k) in enumerate(flat):
        while ahead < len(flat) and ahead <= i + (AHEAD if flat[ahead][0] else 1):
            order.append((flat[ahead][0], K, flat[ahead][1]))
            ahead += 1
        order.append((s, W, k))
    return order


def transport_kernel(
    counts, tr_hbm, vel_hbm, up_hbm, dif_hbm, mask_hbm, level_hbm, part_hbm, out_ref,
    c0, c1, flow, frac, xflux, info, mask_ref, level_ref, part_ref,
    own_sem, in_sem, column_sem, zs, zr, c0s, c0r, c1s, c1r, ss, sr, kvs, kvr, uks, ukr,
    frs, frr, ifs, ifr, rbs, rbr, ready, passing,
):
    n, n_lat, n_lon = counts
    tracer_count, rows, cols, levels = tr_hbm.shape
    width = cols // PARTS
    tiles = cols // TILE
    t, la, lo = lax.axis_index("trc"), lax.axis_index("lat"), lax.axis_index("lon")
    west = lo == 0
    inner = pl.ds(PAD, cols)
    body = pl.ds(1, rows)
    left_halo, right_halo = pl.ds(0, PAD), pl.ds(PAD + cols, PAD)
    left_edge, right_edge = pl.ds(PAD, PAD), pl.ds(cols, PAD)
    middle = (t == 1) | (t == n - 2)
    ends = jnp.logical_not(middle)
    far_end = jnp.where(t == 1, 0, n - 1)
    far_row = jnp.where(t == 1, n - 1, 0)
    far_pair = jnp.where(t < 2, 2, 0)

    sides = (
        (la > 0, {"lat": la - 1}),
        (la < n_lat - 1, {"lat": la + 1}),
        (lo > 0, {"lon": lo - 1}),
        (lo < n_lon - 1, {"lon": lo + 1}),
    )
    opposite = (1, 0, 3, 2)
    NORTH, SOUTH, WEST, EAST = range(4)
    later = (sides[SOUTH], sides[EAST], (t < n - 1, {"trc": t + 1}), (t < n - 2, {"trc": t + 2}),
             (la < n_lat - 2, {"lat": la + 2}))
    earlier = (sides[NORTH], sides[WEST], (t > 0, {"trc": t - 1}), (t == 2, {"trc": t - 2}),
               (la == n_lat - 1, {"lat": la - 2}))
    awaited = (la > 0, lo > 0, t > 0, t > 1, la > 1)

    columns = [
        pltpu.make_async_copy(src, dst, column_sem.at[i])
        for i, (src, dst) in enumerate(
            ((mask_hbm, mask_ref), (level_hbm, level_ref), (part_hbm, part_ref)))
    ]
    barrier = pltpu.get_barrier_semaphore()
    for there, device in later:
        @pl.when(there)
        def _(device=device):
            pl.semaphore_signal(barrier, inc=1, device_id=device, device_id_type=MESH)

    def source(s, f):
        return {
            U: lambda: vel_hbm.at[s, 0], V: lambda: vel_hbm.at[s, 1],
            K: lambda: dif_hbm.at[s], W: lambda: up_hbm.at[s],
        }[f]()

    def own_copy(s, f):
        return pltpu.make_async_copy(
            source(s, f), flow.at[s, f, 1 + t, inner], own_sem.at[s, f]
        )

    for s in range(STEPS):
        for f in (K, V, W, U):
            own_copy(s, f).start()
    for copy in columns:
        copy.start()
    own_field = pltpu.make_async_copy(tr_hbm, c0.at[:, pl.ds(2, rows), inner], in_sem)
    own_field.start()

    def part(k, base):
        at = width * jnp.where(west, PARTS - 1 - k, k)
        return pl.ds(pl.multiple_of(base + at, TILE), width)

    first_tile = [
        jnp.where(west, tiles - sum(WINDOWS[:k + 1]), sum(WINDOWS[:k])) for k in range(PARTS)
    ]

    def window_columns(k):
        return pl.ds(pl.multiple_of(PAD + TILE * first_tile[k], TILE), TILE * WINDOWS[k])

    def group_copy(item, row, count, target, sent, landed, wide=False):
        s, f, k = item
        at = inner if wide else part(k, PAD)
        ref = flow.at[s, pl.ds(f, 2), pl.ds(1 + row, count), at]
        return pltpu.make_async_remote_copy(
            src_ref=ref, dst_ref=ref, send_sem=zs.at[s, f // 2, sent],
            recv_sem=zr.at[s, f // 2, k, landed],
            device_id={"trc": target}, device_id_type=MESH,
        )

    def up_copy(item, **kw):
        return group_copy(item, t, 1, t + 1, 0, 1, **kw)

    def down_copy(item, **kw):
        return group_copy(item, t, 1, t - 1, 1, 0, **kw)

    def far_copy(item, **kw):
        return group_copy(item, t, 1, jnp.where(t == 0, 2, 1), 2, 2, **kw)

    def relay_copy(item, **kw):
        return group_copy(item, far_pair, 2, far_end, 2, 2, **kw)

    def side_copy(src, dst, send, recv, i):
        return pltpu.make_async_remote_copy(
            src_ref=src, dst_ref=dst, send_sem=send, recv_sem=recv,
            device_id=sides[i][1], device_id_type=MESH,
        )

    def start_rows(k, i):
        src = pl.ds(0 if i == NORTH else rows - 2, 2)
        dst = pl.ds(rows + 2 if i == NORTH else 0, 2)
        return side_copy(
            tr_hbm.at[:, src, part(k, 0)], c0.at[:, dst, part(k, PAD)],
            c0s.at[i], c0r.at[i, k], i)

    def detour(k, i):
        src = pl.ds(0 if i == NORTH else rows - 2, 2)
        return pltpu.make_async_remote_copy(
            src_ref=tr_hbm.at[:, src, part(k, 0)], dst_ref=passing.at[:, :, part(k, 0)],
            send_sem=c0s.at[i], recv_sem=rbr.at[k],
            device_id={"lat": 0 if i == NORTH else n_lat - 1}, device_id_type=MESH,
        )

    def pass_on(k, i):
        dst = pl.ds(rows + 2 if i == NORTH else 0, 2)
        return pltpu.make_async_remote_copy(
            src_ref=passing.at[:, :, part(k, 0)], dst_ref=c0.at[:, dst, part(k, PAD)],
            send_sem=rbs, recv_sem=c0r.at[i, k],
            device_id={"lat": 1 if i == NORTH else n_lat - 2}, device_id_type=MESH,
        )

    def pass_all(ks):
        for at, i in ((0, NORTH), (n_lat - 1, SOUTH)):
            @pl.when(la == at)
            def _(i=i):
                for k in ks:
                    detour(k, i).wait_recv()
                    pass_on(k, i).start()

    def step_rows(k, i):
        src = pl.ds(2 if i == NORTH else rows, 2)
        dst = pl.ds(rows + 2 if i == NORTH else 0, 2)
        at = window_columns(k)
        return side_copy(c1.at[:, src, at], c1.at[:, dst, at], c1s.at[i], c1r.at[i, k], i)

    def strip(s, i):
        if s == 0:
            edge = pl.ds(0, PAD) if i == WEST else pl.ds(cols - PAD, PAD)
            src = tr_hbm.at[:, :, edge]
        else:
            src = c1.at[:, pl.ds(2, rows), left_edge if i == WEST else right_edge]
        halo = right_halo if i == WEST else left_halo
        dst = (c0, c1)[s].at[:, pl.ds(2, rows), halo]
        return side_copy(src, dst, ss.at[s, i - 2], sr.at[s, i - 2], i)

    def flow_rows(s, k, i):
        kv = pl.ds(K, 2)
        src, dst = (1, rows + 1) if i == NORTH else (rows, 0)
        at = part(k, PAD)
        return side_copy(flow.at[s, kv, src, at], flow.at[s, kv, dst, at],
                         kvs.at[s, i], kvr.at[s, i, k], i)

    def flow_strip(s, i):
        uk = pl.ds(U, 2)
        src, dst = (left_edge, right_halo) if i == WEST else (right_edge, left_halo)
        return side_copy(flow.at[s, uk, body, src], flow.at[s, uk, body, dst],
                         uks.at[s, i - 2], ukr.at[s, i - 2], i)

    def frac_strip(i):
        src, dst = (left_edge, right_halo) if i == WEST else (right_edge, left_halo)
        return side_copy(frac.at[body, src], frac.at[body, dst], frs.at[i - 2], frr.at[i - 2], i)

    def info_copy(i):
        return side_copy(info.at[0], info.at[1 + i], ifs.at[i], ifr.at[i], i)

    lat_sides, lon_sides = (NORTH, SOUTH), (WEST, EAST)

    def on_sides(make, which, act="start"):
        for i in which:
            @pl.when(sides[i][0])
            def _(i=i):
                getattr(make(i), act)()

    def receive(make, which):
        for i in which:
            @pl.when(sides[opposite[i]][0])
            def _(i=i):
                make(i).wait_recv()

    order = arrival_order()

    total = 0
    for there in awaited:
        total = total + jnp.where(there, 1, 0)
    pl.when(total > 0)(lambda: pl.semaphore_wait(barrier, total))
    for i, (there, device) in enumerate(earlier):
        @pl.when(there)
        def _(i=i, device=device):
            pl.semaphore_signal(ready.at[i], inc=1, device_id=device, device_id_type=MESH)

    def greet(i, there):
        @pl.when(there)
        def _():
            pl.semaphore_wait(ready.at[i], 1)

    def first_copies(item, target, sent, landed):
        s, f, k = item
        for field in (f, f + 1):
            pltpu.make_async_remote_copy(
                src_ref=source(s, field).at[part(k, 0)],
                dst_ref=flow.at[s, field, 1 + t, part(k, PAD)],
                send_sem=zs.at[s, f // 2, sent], recv_sem=zr.at[s, f // 2, k, landed],
                device_id={"trc": target}, device_id_type=MESH,
            ).start()

    @pl.when(t > 0)
    def _():
        for item in order[:DIRECT]:
            @pl.when(t == n - 1)
            def _(item=item):
                first_copies(item, 1, 2, 2)
            first_copies(item, t - 1, 1, 0)

    for s in range(STEPS):
        for f in (K, V, W, U):
            own_copy(s, f).wait()

    @pl.when(t > 0)
    def _():
        for item in order[DIRECT:LEAD]:
            @pl.when(t == n - 1)
            def _(item=item):
                far_copy(item).start()
            down_copy(item).start()

    def outward(make, i):
        for k in range(PARTS):
            make(k, i).start()

    greet(2, t < n - 1)
    greet(3, t == 0)

    @pl.when(t < n - 1)
    def _():
        for item in order[:LEAD]:
            @pl.when(t == 0)
            def _(item=item):
                far_copy(item).start()
            up_copy(item).start()

    pl.when((la > 0) & (la != 2))(lambda: outward(start_rows, NORTH))
    pl.when(la == 2)(lambda: outward(detour, NORTH))
    greet(4, la == 1)
    pl.when(la == 1)(lambda: outward(detour, SOUTH))
    greet(0, la < n_lat - 1)
    pl.when((la < n_lat - 1) & (la != 1))(lambda: outward(start_rows, SOUTH))
    pl.when(lo > 0)(lambda: strip(0, WEST).start())
    greet(1, lo < n_lon - 1)
    pl.when(lo < n_lon - 1)(lambda: strip(0, EAST).start())

    def send_own(item):
        @pl.when(t > 0)
        def _():
            down_copy(item).start()

        @pl.when(t < n - 1)
        def _():
            up_copy(item).start()

    @pl.when(ends)
    def _():
        for item in order[LEAD:]:
            far_copy(item).start()
            send_own(item)

    square = (cols, cols)
    eye = lax.broadcasted_iota(jnp.int32, square, 0) == lax.broadcasted_iota(jnp.int32, square, 1)
    level = lax.broadcasted_iota(jnp.int32, (cols, levels), 1).astype(jnp.float32)

    def upright(row):
        return jnp.sum(jnp.where(eye, jnp.broadcast_to(row, square), 0.0), axis=1, keepdims=True)

    def fill_fraction(slot, r, row):
        wet, share, deepest = (
            upright(info[slot, 8 * i + r:8 * i + r + 1, 0:cols]) for i in range(3)
        )
        frac[row, inner, :] = jnp.where(
            level < deepest, wet, jnp.where(level == deepest, share, 0.0)
        )

    for copy in columns:
        copy.wait()
    wet = mask_ref[...].astype(jnp.float32)
    info[0] = jnp.zeros(info.shape[1:], jnp.float32)
    info[0, 0:rows, 0:cols] = wet
    info[0, 8:8 + rows, 0:cols] = wet * part_ref[...]
    info[0, 16:16 + rows, 0:cols] = level_ref[...].astype(jnp.float32) - 1.0
    on_sides(info_copy, lat_sides)
    for r in range(rows):
        fill_fraction(0, r, 1 + r)
    on_sides(frac_strip, lon_sides)

    @pl.when(la == 0)
    def _():
        for field in (c0, c1):
            field[:, 0:2] = jnp.zeros((tracer_count, 2) + field.shape[2:], jnp.float32)
        frac[0] = jnp.zeros(frac.shape[1:], jnp.float32)
        flow[:, K:, 0] = jnp.zeros((STEPS, 2) + flow.shape[3:], jnp.float32)

    @pl.when(la == n_lat - 1)
    def _():
        for field in (c0, c1):
            field[:, rows + 2:] = jnp.zeros((tracer_count, 2) + field.shape[2:], jnp.float32)
        frac[rows + 1] = jnp.zeros(frac.shape[1:], jnp.float32)
        flow[:, K:, rows + 1] = jnp.zeros((STEPS, 2) + flow.shape[3:], jnp.float32)

    for at_edge, halo in ((lo == 0, left_halo), (lo == n_lon - 1, right_halo)):
        @pl.when(at_edge)
        def _(halo=halo):
            for field in (c0, c1):
                field[:, 2:2 + rows, halo] = jnp.zeros(
                    (tracer_count, rows, PAD, levels), jnp.float32)
            frac[1:1 + rows, halo] = jnp.zeros((rows, PAD, levels), jnp.float32)
            flow[:, U:U + 2, 1:1 + rows, halo] = jnp.zeros(
                (STEPS, 2, rows, PAD, levels), jnp.float32)

    def prepare():
        receive(info_copy, lat_sides)
        for side, r, row in ((SOUTH, rows - 1, 0), (NORTH, 0, rows + 1)):
            @pl.when(sides[opposite[side]][0])
            def _(side=side, r=r, row=row):
                fill_fraction(1 + side, r, row)
        own_field.wait()
        receive(frac_strip, lon_sides)
        receive(functools.partial(strip, 0), lon_sides)

    last_level = lax.broadcasted_iota(jnp.int32, (TILE, levels), 1) == levels - 1

    def faces(s, src, first, count):
        @pl.loop(0, count)
        def _(i):
            base = pl.multiple_of(TILE * (first + i), TILE)
            p, q = pl.ds(base + PAD - 1, TILE), pl.ds(base + PAD, TILE)
            for r in range(rows):
                terms = face_terms(
                    flow[s, U, r + 1, p], flow[s, U, r + 1, q],
                    flow[s, K, r + 1, p], flow[s, K, r + 1, q], frac[r + 1, p], frac[r + 1, q],
                )
                for a in range(tracer_count):
                    xflux[a, r, pl.ds(base, TILE)] = limited_flux(
                        src[a, r + 2, pl.ds(base + PAD - 2, TILE)], src[a, r + 2, p],
                        src[a, r + 2, q], src[a, r + 2, pl.ds(base + PAD + 1, TILE)], *terms,
                    )

    def cells(s, src, dst, row_shift, shift, first, count):
        @pl.loop(0, count)
        def _(i):
            base = pl.multiple_of(TILE * (first + i), TILE)
            at = pl.ds(base + PAD, TILE)

            def row_flux(r):
                terms = face_terms(
                    flow[s, V, r, at], flow[s, V, r + 1, at],
                    flow[s, K, r, at], flow[s, K, r + 1, at], frac[r, at], frac[r + 1, at],
                )
                return [
                    limited_flux(
                        src[a, r, at], src[a, r + 1, at], src[a, r + 2, at], src[a, r + 3, at],
                        *terms)
                    for a in range(tracer_count)
                ]

            lower = row_flux(0)
            for r in range(rows):
                upper = row_flux(r + 1)
                share = frac[r + 1, at]
                rise = flow[s, W, r + 1, at]
                area = jnp.where(
                    last_level, 0.0, jnp.minimum(share, pltpu.roll(share, levels - 1, 1))
                )
                lifted = area * rise
                upward = rise >= 0.0
                inverse = 1.0 / jnp.maximum(share, fraction_floor)
                for a in range(tracer_count):
                    centre = src[a, r + 2, at]
                    vertical = lifted * jnp.where(
                        upward, centre, pltpu.roll(centre, levels - 1, 1)
                    )
                    net = (
                        (upper[a] - lower[a])
                        + (xflux[a, r, pl.ds(base + 1, TILE)] - xflux[a, r, pl.ds(base, TILE)])
                        + (vertical - pltpu.roll(vertical, 1, 1))
                    )
                    dst[a, r + row_shift, pl.ds(base + shift, TILE)] = centre - net * inverse
                lower = upper

    def arrive(item):
        @pl.when(t > 0)
        def _():
            group_copy(item, t - 1, 1, t, 0, 1).wait_recv()

        @pl.when(t < n - 1)
        def _():
            group_copy(item, t + 1, 1, t, 0, 0).wait_recv()

        @pl.when(middle)
        def _():
            group_copy(item, far_row, 1, t, 0, 2).wait_recv()
            relay_copy(item).start()

        @pl.when(ends)
        def _():
            group_copy(item, far_pair, 2, t, 0, 2).wait_recv()

    def after(i):
        s, f, k = order[i]
        if i + LEAD < len(order):
            pl.when(middle)(lambda: send_own(order[i + LEAD]))
        if f == K:
            on_sides(functools.partial(flow_rows, s, k), lat_sides)
        elif k == 0:
            on_sides(functools.partial(flow_strip, s), lon_sides)

    def window(s, k):
        src = (c0, c1)[s]
        if s == 0 and k == 0:
            prepare()
        if k == 0:
            receive(functools.partial(flow_strip, s), lon_sides)
            if s == 1:
                receive(functools.partial(strip, 1), lon_sides)
        at = first_tile[k]
        low = jnp.where(west, at, at + (1 if k > 0 else 0))
        count = WINDOWS[k] + (1 if k == 0 else 0)
        faces(s, src, low, count)
        receive(functools.partial(start_rows if s == 0 else step_rows, k), lat_sides)
        receive(functools.partial(flow_rows, s, k), lat_sides)
        if s == 0:
            cells(s, src, c1, 2, PAD, at, WINDOWS[k])
            on_sides(functools.partial(step_rows, k), lat_sides)
            if k == 0:
                on_sides(functools.partial(strip, 1), lon_sides)
        else:
            cells(s, src, out_ref, 0, 0, at, WINDOWS[k])

    due = {}
    for s in range(STEPS):
        for k in range(PARTS):
            i = order.index((s, W, k)) + LAG
            due.setdefault(min(i, len(order) - 1), []).append((s, k))
    for i, item in enumerate(order):
        arrive(item)
        after(i)
        pass_all(PASSES.get(i, ()))
        for s, k in due.get(i, ()):
            window(s, k)

    for s in range(STEPS):
        for f in (K, W):
            item = (s, f, 0)

            @pl.when(t < n - 1)
            def _(item=item):
                up_copy(item, wide=True).wait_send()

            @pl.when(t > 0)
            def _(item=item):
                down_copy(item, wide=True).wait_send()

            @pl.when(ends)
            def _(item=item):
                far_copy(item, wide=True).wait_send()

            @pl.when(middle)
            def _(item=item):
                relay_copy(item, wide=True).wait_send()

        on_sides(functools.partial(strip, s), lon_sides, "wait_send")
        on_sides(functools.partial(flow_strip, s), lon_sides, "wait_send")
        for i in lat_sides:
            @pl.when(sides[i][0])
            def _(i=i, s=s):
                kv, two = pl.ds(K, 2), pl.ds(0, 2)
                field = (c0, c1)[s].at[:, two, inner]
                side_copy(flow.at[s, kv, 1, inner], flow.at[s, kv, 1, inner],
                          kvs.at[s, i], kvr.at[s, i, 0], i).wait_send()
                side_copy(field, field, (c0s, c1s)[s].at[i], (c0r, c1r)[s].at[i, 0], i).wait_send()
    on_sides(frac_strip, lon_sides, "wait_send")
    on_sides(info_copy, lat_sides, "wait_send")

    @pl.when((la == 0) | (la == n_lat - 1))
    def _():
        pltpu.make_async_copy(passing, passing, rbs).wait()


def fused_body(counts, tracers, land_mask, bottom_level, bottom_part, velocity, upwelling,
               diffusivity):
    tracer_count, rows, cols, levels = tracers.shape
    wide = cols + 2 * PAD
    row = (cols, levels)
    dma = pltpu.SemaphoreType.DMA
    hbm, vmem = pl.BlockSpec(memory_space=pltpu.HBM), pl.BlockSpec(memory_space=pltpu.VMEM)
    return pl.pallas_call(
        functools.partial(transport_kernel, counts),
        out_shape=pltpu.VMEM(tracers.shape, jnp.float32),
        in_specs=[hbm] * 7,
        out_specs=vmem,
        scratch_shapes=[
            pltpu.VMEM((tracer_count, rows + 4, wide + PAD, levels), jnp.float32),
            pltpu.VMEM((tracer_count, rows + 4, wide + PAD, levels), jnp.float32),
            pltpu.VMEM((STEPS, 4, rows + 2, wide, levels), jnp.float32),
            pltpu.VMEM((rows + 2, wide, levels), jnp.float32),
            pltpu.VMEM((tracer_count, rows, cols + 16, levels), jnp.float32),
            pltpu.VMEM((3, 24, 128), jnp.float32),
            pltpu.VMEM((rows, cols), jnp.int32),
            pltpu.VMEM((rows, cols), jnp.int32),
            pltpu.VMEM((rows, cols), jnp.float32),
            dma((STEPS, 4)), dma, dma((3,)),
            dma((STEPS, 2, 3)), dma((STEPS, 2, PARTS, 3)),
            dma((2,)), dma((2, PARTS)), dma((2,)), dma((2, PARTS)),
            dma((STEPS, 2)), dma((STEPS, 2)),
            dma((STEPS, 2)), dma((STEPS, 2, PARTS)),
            dma((STEPS, 2)), dma((STEPS, 2)),
            dma((2,)), dma((2,)), dma((2,)), dma((2,)),
            dma, dma((PARTS,)), pltpu.SemaphoreType.REGULAR((5,)),
            pltpu.VMEM((tracer_count, 2, cols, levels), jnp.float32),
        ],
        compiler_params=pltpu.CompilerParams(
            collective_id=0, has_side_effects=True, vmem_limit_bytes=60 * 1024 * 1024
        ),
    )(
        tracers,
        velocity.reshape((STEPS, 2) + row),
        upwelling.reshape((STEPS,) + row),
        diffusivity.reshape((STEPS,) + row),
        land_mask, bottom_level, bottom_part,
    )


def solution(mesh):
    placed = (
        P("trc", "lat", "lon", None),
        P("lat", "lon"),
        P("lat", "lon"),
        P("lat", "lon"),
        P(None, None, ("lat", "lon"), "trc"),
        P(None, ("lat", "lon"), "trc"),
        P(None, ("lat", "lon"), "trc"),
    )
    counts = tuple(mesh.shape[axis] for axis in ("trc", "lat", "lon"))

    def body(*arrays):
        tracers, velocity = arrays[0], arrays[4]
        one_row = velocity.shape[3] == tracers.shape[2] * tracers.shape[3]
        blocks = tracers.shape[1] == 4 and tracers.shape[2] == 64 and tracers.shape[3] == 128
        if counts == (4, 4, 2) and blocks and one_row:
            return fused_body(counts, *arrays)
        return gathered_body(*arrays)

    return jax.shard_map(
        body, mesh=mesh, in_specs=placed, out_specs=P("trc", "lat", "lon", None), check_vma=False
    )
```

```python
import functools

import jax
import jax.numpy as jnp
from jax import lax
from jax.experimental import pallas as pl
from jax.experimental.pallas import tpu as pltpu
from jax.sharding import PartitionSpec as P

STEPS = 2
MESH = pl.DeviceIdType.MESH


fraction_floor = 0.25


def with_halo(block, sides, width):
    for axis, dim in sides:
        count = lax.axis_size(axis)
        forward = [(i, i + 1) for i in range(count - 1)]
        backward = [(target, source) for source, target in forward]
        low = lax.ppermute(
            lax.slice_in_dim(block, block.shape[dim] - width, None, axis=dim), axis, forward
        )
        high = lax.ppermute(lax.slice_in_dim(block, 0, width, axis=dim), axis, backward)
        block = jnp.concatenate([low, block, high], axis=dim)
    return block


def minmod(first, second):
    return 0.5 * (jnp.sign(first) + jnp.sign(second)) * jnp.minimum(jnp.abs(first), jnp.abs(second))


def window(array, start, stop, offset):
    return lax.slice_in_dim(array, start, stop, axis=array.ndim + offset)


def face_divergence(field, speed, mixing, fraction, offset):
    extent = field.shape[field.ndim + offset]
    before = window(field, 0, extent - 3, offset)
    lower = window(field, 1, extent - 2, offset)
    upper = window(field, 2, extent - 1, offset)
    after = window(field, 3, extent, offset)
    face_speed = 0.5 * (window(speed, 1, extent - 2, offset) + window(speed, 2, extent - 1, offset))
    face_area = jnp.minimum(
        window(fraction, 1, extent - 2, offset), window(fraction, 2, extent - 1, offset)
    )
    face_mixing = 0.5 * (
        window(mixing, 1, extent - 2, offset) + window(mixing, 2, extent - 1, offset)
    )
    jump = upper - lower
    damping = 0.5 * (1.0 - jnp.abs(face_speed))
    from_lower = lower + damping * minmod(lower - before, jump)
    from_upper = upper - damping * minmod(jump, after - upper)
    face_value = jnp.where(face_speed >= 0.0, from_lower, from_upper)
    face_flux = face_area * (face_speed * face_value - face_mixing * jump)
    return window(face_flux, 1, extent - 3, offset) - window(face_flux, 0, extent - 4, offset)


def substep(field, fraction, eastward, northward, mixing, rising):
    across_rows = face_divergence(field, northward, mixing, fraction, -3)[..., 2:-2, :]
    across_cols = face_divergence(field, eastward, mixing, fraction, -2)[..., 2:-2, :, :]
    centre = field[..., 2:-2, 2:-2, :]
    wet_share = fraction[2:-2, 2:-2, :]
    top_area = jnp.minimum(wet_share[:, :, :-1], wet_share[:, :, 1:])
    lifting = rising[:, :, :-1]
    carried = jnp.where(lifting >= 0.0, centre[..., :-1], centre[..., 1:])
    vertical = top_area * lifting * carried
    closed = jnp.zeros(vertical.shape[:-1] + (1,), jnp.float32)
    across_levels = jnp.concatenate([vertical, closed], axis=-1) - jnp.concatenate(
        [closed, vertical], axis=-1
    )
    return centre - (across_rows + across_cols + across_levels) / jnp.maximum(
        wet_share, fraction_floor
    )


def cell_fraction(land_mask, bottom_level, bottom_part, levels):
    level_index = lax.broadcasted_iota(jnp.int32, land_mask.shape + (levels,), 2)
    deepest = bottom_level[:, :, None] - 1
    full_cell = (level_index < deepest).astype(jnp.float32)
    last_cell = (level_index == deepest).astype(jnp.float32) * bottom_part[:, :, None]
    return land_mask.astype(jnp.float32)[:, :, None] * (full_cell + last_cell)


def gathered_body(tracers, land_mask, bottom_level, bottom_part, velocity, upwelling, diffusivity):
    levels = tracers.shape[3]
    block_shape = (tracers.shape[1], tracers.shape[2], levels)
    fraction = cell_fraction(land_mask, bottom_level, bottom_part, levels)
    tracer_count = tracers.shape[0]
    moved = (
        lax.all_gather(velocity, "trc", axis=3, tiled=True),
        lax.all_gather(upwelling, "trc", axis=2, tiled=True),
        lax.all_gather(diffusivity, "trc", axis=2, tiled=True),
    )
    speeds = moved[0].reshape((STEPS, 2) + block_shape)
    rises = moved[1].reshape((STEPS,) + block_shape)
    mixes = moved[2].reshape((STEPS,) + block_shape)
    field = tracers
    wide_frac = fraction
    for number in range(STEPS):
        extras = [fraction[None]] if number == 0 else []
        stack = jnp.concatenate(
            [field] + extras + [jnp.stack([speeds[number, 0], speeds[number, 1], mixes[number]])],
            axis=0,
        )
        widened = with_halo(stack, (("lat", 1), ("lon", 2)), 2)
        if number == 0:
            wide_frac = widened[tracer_count]
        flows = widened[-3:]
        field = substep(
            widened[:tracer_count], wide_frac, flows[0], flows[1], flows[2], rises[number]
        )
    return field


W, U, K, V = range(4)
PAD = 8
TILE = 8
SHARES = (2, 2, 2, 2)
PARTS = len(SHARES)
LEAD = 12
LAG = 1
AHEAD = 2
DIRECT = 2
EARLY = 2
PASSES = {0: (0,), 1: (1,), 2: tuple(range(2, PARTS))}
WINDOWS = tuple(share - (k == 0) + (k == PARTS - 1) for k, share in enumerate(SHARES))


def limited_flux(before, lower, upper, after, east, scale, area_speed, area_mix):
    jump = upper - lower
    base = jnp.where(east, lower, upper)
    slope = jnp.where(east, lower - before, after - upper)
    limited = jnp.maximum(jnp.minimum(slope, jump), 0.0) + jnp.minimum(
        jnp.maximum(slope, jump), 0.0
    )
    return area_speed * (base + scale * limited) - area_mix * jump


def face_terms(speed_p, speed_q, mix_p, mix_q, frac_p, frac_q):
    speed = 0.5 * (speed_p + speed_q)
    area = jnp.minimum(frac_p, frac_q)
    east = speed >= 0.0
    damping = 0.5 * (1.0 - jnp.abs(speed))
    return east, jnp.where(east, damping, -damping), area * speed, area * (0.5 * (mix_p + mix_q))


def arrival_order():
    flat = [(s, k) for s in range(STEPS) for k in range(PARTS)]
    order = [(0, K, 0)]
    ahead = 1
    for i, (s, k) in enumerate(flat):
        while ahead < len(flat) and ahead <= i + (AHEAD if flat[ahead][0] else 1):
            order.append((flat[ahead][0], K, flat[ahead][1]))
            ahead += 1
        order.append((s, W, k))
    return order


def transport_kernel(
    counts, tr_hbm, vel_hbm, up_hbm, dif_hbm, mask_hbm, level_hbm, part_hbm, out_ref,
    c0, c1, flow, frac, xflux, info, mask_ref, level_ref, part_ref,
    own_sem, in_sem, column_sem, zs, zr, c0s, c0r, c1s, c1r, ss, sr, kvs, kvr, uks, ukr,
    frs, frr, ifs, ifr, rbs, rbr, ready, passing,
):
    n, n_lat, n_lon = counts
    tracer_count, rows, cols, levels = tr_hbm.shape
    tiles = cols // TILE
    t, la, lo = lax.axis_index("trc"), lax.axis_index("lat"), lax.axis_index("lon")
    west = lo == 0
    inner = pl.ds(PAD, cols)
    body = pl.ds(1, rows)
    left_halo, right_halo = pl.ds(0, PAD), pl.ds(PAD + cols, PAD)
    left_edge, right_edge = pl.ds(PAD, PAD), pl.ds(cols, PAD)
    middle = (t == 1) | (t == n - 2)
    ends = jnp.logical_not(middle)
    far_end = jnp.where(t == 1, 0, n - 1)
    far_row = jnp.where(t == 1, n - 1, 0)
    far_pair = jnp.where(t < 2, 2, 0)

    sides = (
        (la > 0, {"lat": la - 1}),
        (la < n_lat - 1, {"lat": la + 1}),
        (lo > 0, {"lon": lo - 1}),
        (lo < n_lon - 1, {"lon": lo + 1}),
    )
    opposite = (1, 0, 3, 2)
    NORTH, SOUTH, WEST, EAST = range(4)
    later = (sides[SOUTH], sides[EAST], (t < n - 1, {"trc": t + 1}), (t < n - 2, {"trc": t + 2}),
             (la < n_lat - 2, {"lat": la + 2}))
    earlier = (sides[NORTH], sides[WEST], (t > 0, {"trc": t - 1}), (t == 2, {"trc": t - 2}),
               (la == n_lat - 1, {"lat": la - 2}))
    awaited = (la > 0, lo > 0, t > 0, t > 1, la > 1)

    columns = [
        pltpu.make_async_copy(src, dst, column_sem.at[i])
        for i, (src, dst) in enumerate(
            ((mask_hbm, mask_ref), (level_hbm, level_ref), (part_hbm, part_ref)))
    ]
    barrier = pltpu.get_barrier_semaphore()
    for there, device in later:
        @pl.when(there)
        def _(device=device):
            pl.semaphore_signal(barrier, inc=1, device_id=device, device_id_type=MESH)

    def source(s, f):
        return {
            U: lambda: vel_hbm.at[s, 0], V: lambda: vel_hbm.at[s, 1],
            K: lambda: dif_hbm.at[s], W: lambda: up_hbm.at[s],
        }[f]()

    def own_copy(s, f):
        return pltpu.make_async_copy(
            source(s, f), flow.at[s, f, 1 + t, inner], own_sem.at[s, f]
        )

    for s in range(STEPS):
        for f in (K, V, W, U):
            own_copy(s, f).start()
    for copy in columns:
        copy.start()
    own_field = pltpu.make_async_copy(tr_hbm, c0.at[:, pl.ds(2, rows), inner], in_sem)
    own_field.start()

    def part(k, base):
        before, share = sum(SHARES[:k]), SHARES[k]
        at = TILE * jnp.where(west, tiles - before - share, before)
        return pl.ds(pl.multiple_of(base + at, TILE), TILE * share)

    first_tile = [
        jnp.where(west, tiles - sum(WINDOWS[:k + 1]), sum(WINDOWS[:k])) for k in range(PARTS)
    ]

    def window_columns(k):
        return pl.ds(pl.multiple_of(PAD + TILE * first_tile[k], TILE), TILE * WINDOWS[k])

    def group_copy(item, row, count, target, sent, landed, wide=False):
        s, f, k = item
        at = inner if wide else part(k, PAD)
        ref = flow.at[s, pl.ds(f, 2), pl.ds(1 + row, count), at]
        return pltpu.make_async_remote_copy(
            src_ref=ref, dst_ref=ref, send_sem=zs.at[s, f // 2, sent],
            recv_sem=zr.at[s, f // 2, k, landed],
            device_id={"trc": target}, device_id_type=MESH,
        )

    def up_copy(item, **kw):
        return group_copy(item, t, 1, t + 1, 0, 1, **kw)

    def down_copy(item, **kw):
        return group_copy(item, t, 1, t - 1, 1, 0, **kw)

    def far_copy(item, **kw):
        return group_copy(item, t, 1, jnp.where(t == 0, 2, 1), 2, 2, **kw)

    def relay_copy(item, **kw):
        return group_copy(item, far_pair, 2, far_end, 2, 2, **kw)

    def side_copy(src, dst, send, recv, i):
        return pltpu.make_async_remote_copy(
            src_ref=src, dst_ref=dst, send_sem=send, recv_sem=recv,
            device_id=sides[i][1], device_id_type=MESH,
        )

    def start_rows(k, i):
        src = pl.ds(0 if i == NORTH else rows - 2, 2)
        dst = pl.ds(rows + 2 if i == NORTH else 0, 2)
        return side_copy(
            tr_hbm.at[:, src, part(k, 0)], c0.at[:, dst, part(k, PAD)],
            c0s.at[i], c0r.at[i, k], i)

    def detour(k, i):
        src = pl.ds(0 if i == NORTH else rows - 2, 2)
        return pltpu.make_async_remote_copy(
            src_ref=tr_hbm.at[:, src, part(k, 0)], dst_ref=passing.at[:, :, part(k, 0)],
            send_sem=c0s.at[i], recv_sem=rbr.at[k],
            device_id={"lat": 0 if i == NORTH else n_lat - 1}, device_id_type=MESH,
        )

    def pass_on(k, i):
        dst = pl.ds(rows + 2 if i == NORTH else 0, 2)
        return pltpu.make_async_remote_copy(
            src_ref=passing.at[:, :, part(k, 0)], dst_ref=c0.at[:, dst, part(k, PAD)],
            send_sem=rbs, recv_sem=c0r.at[i, k],
            device_id={"lat": 1 if i == NORTH else n_lat - 2}, device_id_type=MESH,
        )

    def pass_all(ks):
        for at, i in ((0, NORTH), (n_lat - 1, SOUTH)):
            @pl.when(la == at)
            def _(i=i):
                for k in ks:
                    detour(k, i).wait_recv()
                    pass_on(k, i).start()

    def step_rows(k, i):
        src = pl.ds(2 if i == NORTH else rows, 2)
        dst = pl.ds(rows + 2 if i == NORTH else 0, 2)
        at = window_columns(k)
        return side_copy(c1.at[:, src, at], c1.at[:, dst, at], c1s.at[i], c1r.at[i, k], i)

    def strip(s, i):
        if s == 0:
            edge = pl.ds(0, PAD) if i == WEST else pl.ds(cols - PAD, PAD)
            src = tr_hbm.at[:, :, edge]
        else:
            src = c1.at[:, pl.ds(2, rows), left_edge if i == WEST else right_edge]
        halo = right_halo if i == WEST else left_halo
        dst = (c0, c1)[s].at[:, pl.ds(2, rows), halo]
        return side_copy(src, dst, ss.at[s, i - 2], sr.at[s, i - 2], i)

    def flow_rows(s, k, i):
        kv = pl.ds(K, 2)
        src, dst = (1, rows + 1) if i == NORTH else (rows, 0)
        at = part(k, PAD)
        return side_copy(flow.at[s, kv, src, at], flow.at[s, kv, dst, at],
                         kvs.at[s, i], kvr.at[s, i, k], i)

    def flow_strip(s, i):
        uk = pl.ds(U, 2)
        src, dst = (left_edge, right_halo) if i == WEST else (right_edge, left_halo)
        return side_copy(flow.at[s, uk, body, src], flow.at[s, uk, body, dst],
                         uks.at[s, i - 2], ukr.at[s, i - 2], i)

    def frac_strip(i):
        src, dst = (left_edge, right_halo) if i == WEST else (right_edge, left_halo)
        return side_copy(frac.at[body, src], frac.at[body, dst], frs.at[i - 2], frr.at[i - 2], i)

    def info_copy(i):
        return side_copy(info.at[0], info.at[1 + i], ifs.at[i], ifr.at[i], i)

    lat_sides, lon_sides = (NORTH, SOUTH), (WEST, EAST)

    def on_sides(make, which, act="start"):
        for i in which:
            @pl.when(sides[i][0])
            def _(i=i):
                getattr(make(i), act)()

    def receive(make, which):
        for i in which:
            @pl.when(sides[opposite[i]][0])
            def _(i=i):
                make(i).wait_recv()

    order = arrival_order()

    total = 0
    for there in awaited:
        total = total + jnp.where(there, 1, 0)
    pl.when(total > 0)(lambda: pl.semaphore_wait(barrier, total))
    for i, (there, device) in enumerate(earlier):
        @pl.when(there)
        def _(i=i, device=device):
            pl.semaphore_signal(ready.at[i], inc=1, device_id=device, device_id_type=MESH)

    def greet(i, there):
        @pl.when(there)
        def _():
            pl.semaphore_wait(ready.at[i], 1)

    def first_copies(item, target, sent, landed):
        s, f, k = item
        for field in (f, f + 1):
            pltpu.make_async_remote_copy(
                src_ref=source(s, field).at[part(k, 0)],
                dst_ref=flow.at[s, field, 1 + t, part(k, PAD)],
                send_sem=zs.at[s, f // 2, sent], recv_sem=zr.at[s, f // 2, k, landed],
                device_id={"trc": target}, device_id_type=MESH,
            ).start()

    @pl.when(t > 0)
    def _():
        for item in order[:DIRECT]:
            @pl.when(t == n - 1)
            def _(item=item):
                first_copies(item, 1, 2, 2)
            first_copies(item, t - 1, 1, 0)

    for s in range(STEPS):
        for f in (K, V, W, U):
            own_copy(s, f).wait()

    @pl.when(t > 0)
    def _():
        for item in order[DIRECT:LEAD]:
            @pl.when(t == n - 1)
            def _(item=item):
                far_copy(item).start()
            down_copy(item).start()

    def outward(make, i):
        for k in range(PARTS):
            make(k, i).start()

    greet(2, t < n - 1)
    greet(3, t == 0)

    @pl.when(t < n - 1)
    def _():
        for item in order[:LEAD]:
            @pl.when(t == 0)
            def _(item=item):
                far_copy(item).start()
            up_copy(item).start()

    pl.when((la > 0) & (la != 2))(lambda: outward(start_rows, NORTH))
    pl.when(la == 2)(lambda: outward(detour, NORTH))
    greet(4, la == 1)
    pl.when(la == 1)(lambda: outward(detour, SOUTH))
    greet(0, la < n_lat - 1)
    pl.when((la < n_lat - 1) & (la != 1))(lambda: outward(start_rows, SOUTH))
    for side, own in ((NORTH, 0), (SOUTH, n - 1)):
        @pl.when(sides[side][0] & (t == own))
        def _(side=side):
            for s in range(EARLY):
                for k in range(PARTS):
                    flow_rows(s, k, side).start()

    pl.when(lo > 0)(lambda: strip(0, WEST).start())
    greet(1, lo < n_lon - 1)
    pl.when(lo < n_lon - 1)(lambda: strip(0, EAST).start())

    def send_own(item):
        @pl.when(t > 0)
        def _():
            down_copy(item).start()

        @pl.when(t < n - 1)
        def _():
            up_copy(item).start()

    @pl.when(ends)
    def _():
        for item in order[LEAD:]:
            far_copy(item).start()
            send_own(item)

    square = (cols, cols)
    eye = lax.broadcasted_iota(jnp.int32, square, 0) == lax.broadcasted_iota(jnp.int32, square, 1)
    level = lax.broadcasted_iota(jnp.int32, (cols, levels), 1).astype(jnp.float32)

    def upright(row):
        return jnp.sum(jnp.where(eye, jnp.broadcast_to(row, square), 0.0), axis=1, keepdims=True)

    def fill_fraction(slot, r, row):
        wet, share, deepest = (
            upright(info[slot, 8 * i + r:8 * i + r + 1, 0:cols]) for i in range(3)
        )
        frac[row, inner, :] = jnp.where(
            level < deepest, wet, jnp.where(level == deepest, share, 0.0)
        )

    for copy in columns:
        copy.wait()
    wet = mask_ref[...].astype(jnp.float32)
    info[0] = jnp.zeros(info.shape[1:], jnp.float32)
    info[0, 0:rows, 0:cols] = wet
    info[0, 8:8 + rows, 0:cols] = wet * part_ref[...]
    info[0, 16:16 + rows, 0:cols] = level_ref[...].astype(jnp.float32) - 1.0
    on_sides(info_copy, lat_sides)
    for r in range(rows):
        fill_fraction(0, r, 1 + r)
    on_sides(frac_strip, lon_sides)

    @pl.when(la == 0)
    def _():
        for field in (c0, c1):
            field[:, 0:2] = jnp.zeros((tracer_count, 2) + field.shape[2:], jnp.float32)
        frac[0] = jnp.zeros(frac.shape[1:], jnp.float32)
        flow[:, K:, 0] = jnp.zeros((STEPS, 2) + flow.shape[3:], jnp.float32)

    @pl.when(la == n_lat - 1)
    def _():
        for field in (c0, c1):
            field[:, rows + 2:] = jnp.zeros((tracer_count, 2) + field.shape[2:], jnp.float32)
        frac[rows + 1] = jnp.zeros(frac.shape[1:], jnp.float32)
        flow[:, K:, rows + 1] = jnp.zeros((STEPS, 2) + flow.shape[3:], jnp.float32)

    for at_edge, halo in ((lo == 0, left_halo), (lo == n_lon - 1, right_halo)):
        @pl.when(at_edge)
        def _(halo=halo):
            for field in (c0, c1):
                field[:, 2:2 + rows, halo] = jnp.zeros(
                    (tracer_count, rows, PAD, levels), jnp.float32)
            frac[1:1 + rows, halo] = jnp.zeros((rows, PAD, levels), jnp.float32)
            flow[:, U:U + 2, 1:1 + rows, halo] = jnp.zeros(
                (STEPS, 2, rows, PAD, levels), jnp.float32)

    def prepare():
        receive(info_copy, lat_sides)
        for side, r, row in ((SOUTH, rows - 1, 0), (NORTH, 0, rows + 1)):
            @pl.when(sides[opposite[side]][0])
            def _(side=side, r=r, row=row):
                fill_fraction(1 + side, r, row)
        own_field.wait()
        receive(frac_strip, lon_sides)
        receive(functools.partial(strip, 0), lon_sides)

    last_level = lax.broadcasted_iota(jnp.int32, (TILE, levels), 1) == levels - 1

    def faces(s, src, first, count):
        @pl.loop(0, count)
        def _(i):
            base = pl.multiple_of(TILE * (first + i), TILE)
            p, q = pl.ds(base + PAD - 1, TILE), pl.ds(base + PAD, TILE)
            for r in range(rows):
                terms = face_terms(
                    flow[s, U, r + 1, p], flow[s, U, r + 1, q],
                    flow[s, K, r + 1, p], flow[s, K, r + 1, q], frac[r + 1, p], frac[r + 1, q],
                )
                for a in range(tracer_count):
                    xflux[a, r, pl.ds(base, TILE)] = limited_flux(
                        src[a, r + 2, pl.ds(base + PAD - 2, TILE)], src[a, r + 2, p],
                        src[a, r + 2, q], src[a, r + 2, pl.ds(base + PAD + 1, TILE)], *terms,
                    )

    def cells(s, src, dst, row_shift, shift, first, count):
        @pl.loop(0, count)
        def _(i):
            base = pl.multiple_of(TILE * (first + i), TILE)
            at = pl.ds(base + PAD, TILE)

            def row_flux(r):
                terms = face_terms(
                    flow[s, V, r, at], flow[s, V, r + 1, at],
                    flow[s, K, r, at], flow[s, K, r + 1, at], frac[r, at], frac[r + 1, at],
                )
                return [
                    limited_flux(
                        src[a, r, at], src[a, r + 1, at], src[a, r + 2, at], src[a, r + 3, at],
                        *terms)
                    for a in range(tracer_count)
                ]

            lower = row_flux(0)
            for r in range(rows):
                upper = row_flux(r + 1)
                share = frac[r + 1, at]
                rise = flow[s, W, r + 1, at]
                area = jnp.where(
                    last_level, 0.0, jnp.minimum(share, pltpu.roll(share, levels - 1, 1))
                )
                lifted = area * rise
                upward = rise >= 0.0
                inverse = 1.0 / jnp.maximum(share, fraction_floor)
                for a in range(tracer_count):
                    centre = src[a, r + 2, at]
                    vertical = lifted * jnp.where(
                        upward, centre, pltpu.roll(centre, levels - 1, 1)
                    )
                    net = (
                        (upper[a] - lower[a])
                        + (xflux[a, r, pl.ds(base + 1, TILE)] - xflux[a, r, pl.ds(base, TILE)])
                        + (vertical - pltpu.roll(vertical, 1, 1))
                    )
                    dst[a, r + row_shift, pl.ds(base + shift, TILE)] = centre - net * inverse
                lower = upper

    def arrive(item):
        @pl.when(t > 0)
        def _():
            group_copy(item, t - 1, 1, t, 0, 1).wait_recv()

        @pl.when(t < n - 1)
        def _():
            group_copy(item, t + 1, 1, t, 0, 0).wait_recv()

        @pl.when(middle)
        def _():
            group_copy(item, far_row, 1, t, 0, 2).wait_recv()
            relay_copy(item).start()

        @pl.when(ends)
        def _():
            group_copy(item, far_pair, 2, t, 0, 2).wait_recv()

    def after(i):
        s, f, k = order[i]
        if i + LEAD < len(order):
            pl.when(middle)(lambda: send_own(order[i + LEAD]))
        if f == K:
            for side, own in ((NORTH, 0), (SOUTH, n - 1)):
                @pl.when(sides[side][0] & ((t != own) | (s >= EARLY)))
                def _(side=side):
                    flow_rows(s, k, side).start()
        elif k == 0:
            on_sides(functools.partial(flow_strip, s), lon_sides)

    def window(s, k):
        src = (c0, c1)[s]
        if s == 0 and k == 0:
            prepare()
        if k == 0:
            receive(functools.partial(flow_strip, s), lon_sides)
            if s == 1:
                receive(functools.partial(strip, 1), lon_sides)
        at = first_tile[k]
        low = jnp.where(west, at, at + (1 if k > 0 else 0))
        count = WINDOWS[k] + (1 if k == 0 else 0)
        faces(s, src, low, count)
        receive(functools.partial(start_rows if s == 0 else step_rows, k), lat_sides)
        receive(functools.partial(flow_rows, s, k), lat_sides)
        if s == 0:
            cells(s, src, c1, 2, PAD, at, WINDOWS[k])
            on_sides(functools.partial(step_rows, k), lat_sides)
            if k == 0:
                on_sides(functools.partial(strip, 1), lon_sides)
        else:
            cells(s, src, out_ref, 0, 0, at, WINDOWS[k])

    due = {}
    for s in range(STEPS):
        for k in range(PARTS):
            i = order.index((s, W, k)) + LAG
            due.setdefault(min(i, len(order) - 1), []).append((s, k))
    for i, item in enumerate(order):
        arrive(item)
        after(i)
        pass_all(PASSES.get(i, ()))
        for s, k in due.get(i, ()):
            window(s, k)

    for s in range(STEPS):
        for f in (K, W):
            item = (s, f, 0)

            @pl.when(t < n - 1)
            def _(item=item):
                up_copy(item, wide=True).wait_send()

            @pl.when(t > 0)
            def _(item=item):
                down_copy(item, wide=True).wait_send()

            @pl.when(ends)
            def _(item=item):
                far_copy(item, wide=True).wait_send()

            @pl.when(middle)
            def _(item=item):
                relay_copy(item, wide=True).wait_send()

        on_sides(functools.partial(strip, s), lon_sides, "wait_send")
        on_sides(functools.partial(flow_strip, s), lon_sides, "wait_send")
        for i in lat_sides:
            @pl.when(sides[i][0])
            def _(i=i, s=s):
                kv, two = pl.ds(K, 2), pl.ds(0, 2)
                field = (c0, c1)[s].at[:, two, inner]
                side_copy(flow.at[s, kv, 1, inner], flow.at[s, kv, 1, inner],
                          kvs.at[s, i], kvr.at[s, i, 0], i).wait_send()
                side_copy(field, field, (c0s, c1s)[s].at[i], (c0r, c1r)[s].at[i, 0], i).wait_send()
    on_sides(frac_strip, lon_sides, "wait_send")
    on_sides(info_copy, lat_sides, "wait_send")

    @pl.when((la == 0) | (la == n_lat - 1))
    def _():
        pltpu.make_async_copy(passing, passing, rbs).wait()


def fused_body(counts, tracers, land_mask, bottom_level, bottom_part, velocity, upwelling,
               diffusivity):
    tracer_count, rows, cols, levels = tracers.shape
    wide = cols + 2 * PAD
    row = (cols, levels)
    dma = pltpu.SemaphoreType.DMA
    hbm, vmem = pl.BlockSpec(memory_space=pltpu.HBM), pl.BlockSpec(memory_space=pltpu.VMEM)
    return pl.pallas_call(
        functools.partial(transport_kernel, counts),
        out_shape=pltpu.VMEM(tracers.shape, jnp.float32),
        in_specs=[hbm] * 7,
        out_specs=vmem,
        scratch_shapes=[
            pltpu.VMEM((tracer_count, rows + 4, wide + PAD, levels), jnp.float32),
            pltpu.VMEM((tracer_count, rows + 4, wide + PAD, levels), jnp.float32),
            pltpu.VMEM((STEPS, 4, rows + 2, wide, levels), jnp.float32),
            pltpu.VMEM((rows + 2, wide, levels), jnp.float32),
            pltpu.VMEM((tracer_count, rows, cols + 16, levels), jnp.float32),
            pltpu.VMEM((3, 24, 128), jnp.float32),
            pltpu.VMEM((rows, cols), jnp.int32),
            pltpu.VMEM((rows, cols), jnp.int32),
            pltpu.VMEM((rows, cols), jnp.float32),
            dma((STEPS, 4)), dma, dma((3,)),
            dma((STEPS, 2, 3)), dma((STEPS, 2, PARTS, 3)),
            dma((2,)), dma((2, PARTS)), dma((2,)), dma((2, PARTS)),
            dma((STEPS, 2)), dma((STEPS, 2)),
            dma((STEPS, 2)), dma((STEPS, 2, PARTS)),
            dma((STEPS, 2)), dma((STEPS, 2)),
            dma((2,)), dma((2,)), dma((2,)), dma((2,)),
            dma, dma((PARTS,)), pltpu.SemaphoreType.REGULAR((5,)),
            pltpu.VMEM((tracer_count, 2, cols, levels), jnp.float32),
        ],
        compiler_params=pltpu.CompilerParams(
            collective_id=0, has_side_effects=True, vmem_limit_bytes=60 * 1024 * 1024
        ),
    )(
        tracers,
        velocity.reshape((STEPS, 2) + row),
        upwelling.reshape((STEPS,) + row),
        diffusivity.reshape((STEPS,) + row),
        land_mask, bottom_level, bottom_part,
    )


def solution(mesh):
    placed = (
        P("trc", "lat", "lon", None),
        P("lat", "lon"),
        P("lat", "lon"),
        P("lat", "lon"),
        P(None, None, ("lat", "lon"), "trc"),
        P(None, ("lat", "lon"), "trc"),
        P(None, ("lat", "lon"), "trc"),
    )
    counts = tuple(mesh.shape[axis] for axis in ("trc", "lat", "lon"))

    def body(*arrays):
        tracers, velocity = arrays[0], arrays[4]
        one_row = velocity.shape[3] == tracers.shape[2] * tracers.shape[3]
        blocks = tracers.shape[1] == 4 and tracers.shape[2] == 64 and tracers.shape[3] == 128
        if counts == (4, 4, 2) and blocks and one_row:
            return fused_body(counts, *arrays)
        return gathered_body(*arrays)

    return jax.shard_map(
        body, mesh=mesh, in_specs=placed, out_specs=P("trc", "lat", "lon", None), check_vma=False
    )
```

```python
import functools

import jax
import jax.numpy as jnp
from jax import lax
from jax.experimental import pallas as pl
from jax.experimental.pallas import tpu as pltpu
from jax.sharding import PartitionSpec as P

STEPS = 2
MESH = pl.DeviceIdType.MESH


fraction_floor = 0.25


def with_halo(block, sides, width):
    for axis, dim in sides:
        count = lax.axis_size(axis)
        forward = [(i, i + 1) for i in range(count - 1)]
        backward = [(target, source) for source, target in forward]
        low = lax.ppermute(
            lax.slice_in_dim(block, block.shape[dim] - width, None, axis=dim), axis, forward
        )
        high = lax.ppermute(lax.slice_in_dim(block, 0, width, axis=dim), axis, backward)
        block = jnp.concatenate([low, block, high], axis=dim)
    return block


def minmod(first, second):
    return 0.5 * (jnp.sign(first) + jnp.sign(second)) * jnp.minimum(jnp.abs(first), jnp.abs(second))


def window(array, start, stop, offset):
    return lax.slice_in_dim(array, start, stop, axis=array.ndim + offset)


def face_divergence(field, speed, mixing, fraction, offset):
    extent = field.shape[field.ndim + offset]
    before = window(field, 0, extent - 3, offset)
    lower = window(field, 1, extent - 2, offset)
    upper = window(field, 2, extent - 1, offset)
    after = window(field, 3, extent, offset)
    face_speed = 0.5 * (window(speed, 1, extent - 2, offset) + window(speed, 2, extent - 1, offset))
    face_area = jnp.minimum(
        window(fraction, 1, extent - 2, offset), window(fraction, 2, extent - 1, offset)
    )
    face_mixing = 0.5 * (
        window(mixing, 1, extent - 2, offset) + window(mixing, 2, extent - 1, offset)
    )
    jump = upper - lower
    damping = 0.5 * (1.0 - jnp.abs(face_speed))
    from_lower = lower + damping * minmod(lower - before, jump)
    from_upper = upper - damping * minmod(jump, after - upper)
    face_value = jnp.where(face_speed >= 0.0, from_lower, from_upper)
    face_flux = face_area * (face_speed * face_value - face_mixing * jump)
    return window(face_flux, 1, extent - 3, offset) - window(face_flux, 0, extent - 4, offset)


def substep(field, fraction, eastward, northward, mixing, rising):
    across_rows = face_divergence(field, northward, mixing, fraction, -3)[..., 2:-2, :]
    across_cols = face_divergence(field, eastward, mixing, fraction, -2)[..., 2:-2, :, :]
    centre = field[..., 2:-2, 2:-2, :]
    wet_share = fraction[2:-2, 2:-2, :]
    top_area = jnp.minimum(wet_share[:, :, :-1], wet_share[:, :, 1:])
    lifting = rising[:, :, :-1]
    carried = jnp.where(lifting >= 0.0, centre[..., :-1], centre[..., 1:])
    vertical = top_area * lifting * carried
    closed = jnp.zeros(vertical.shape[:-1] + (1,), jnp.float32)
    across_levels = jnp.concatenate([vertical, closed], axis=-1) - jnp.concatenate(
        [closed, vertical], axis=-1
    )
    return centre - (across_rows + across_cols + across_levels) / jnp.maximum(
        wet_share, fraction_floor
    )


def cell_fraction(land_mask, bottom_level, bottom_part, levels):
    level_index = lax.broadcasted_iota(jnp.int32, land_mask.shape + (levels,), 2)
    deepest = bottom_level[:, :, None] - 1
    full_cell = (level_index < deepest).astype(jnp.float32)
    last_cell = (level_index == deepest).astype(jnp.float32) * bottom_part[:, :, None]
    return land_mask.astype(jnp.float32)[:, :, None] * (full_cell + last_cell)


def gathered_body(tracers, land_mask, bottom_level, bottom_part, velocity, upwelling, diffusivity):
    levels = tracers.shape[3]
    block_shape = (tracers.shape[1], tracers.shape[2], levels)
    fraction = cell_fraction(land_mask, bottom_level, bottom_part, levels)
    tracer_count = tracers.shape[0]
    moved = (
        lax.all_gather(velocity, "trc", axis=3, tiled=True),
        lax.all_gather(upwelling, "trc", axis=2, tiled=True),
        lax.all_gather(diffusivity, "trc", axis=2, tiled=True),
    )
    speeds = moved[0].reshape((STEPS, 2) + block_shape)
    rises = moved[1].reshape((STEPS,) + block_shape)
    mixes = moved[2].reshape((STEPS,) + block_shape)
    field = tracers
    wide_frac = fraction
    for number in range(STEPS):
        extras = [fraction[None]] if number == 0 else []
        stack = jnp.concatenate(
            [field] + extras + [jnp.stack([speeds[number, 0], speeds[number, 1], mixes[number]])],
            axis=0,
        )
        widened = with_halo(stack, (("lat", 1), ("lon", 2)), 2)
        if number == 0:
            wide_frac = widened[tracer_count]
        flows = widened[-3:]
        field = substep(
            widened[:tracer_count], wide_frac, flows[0], flows[1], flows[2], rises[number]
        )
    return field


W, U, K, V = range(4)
PAD = 8
TILE = 8
SHARES = (2, 2, 2, 2)
PARTS = len(SHARES)
LEAD = 12
END_LAGS = (1, 1)
MIDDLE_LAGS = (1, 1)
AHEAD = 2
DIRECT = 3
SETTLE = 2
PREPARED = 3
LATER = -1
PASSES = {0: (0,), 1: (1,), 2: tuple(range(2, PARTS))}
WINDOWS = tuple(share - (k == 0) + (k == PARTS - 1) for k, share in enumerate(SHARES))


def limited_flux(before, lower, upper, after, east, scale, area_speed, area_mix):
    jump = upper - lower
    base = jnp.where(east, lower, upper)
    slope = jnp.where(east, lower - before, after - upper)
    limited = jnp.maximum(jnp.minimum(slope, jump), 0.0) + jnp.minimum(
        jnp.maximum(slope, jump), 0.0
    )
    return area_speed * (base + scale * limited) - area_mix * jump


def face_terms(speed_p, speed_q, mix_p, mix_q, frac_p, frac_q):
    speed = 0.5 * (speed_p + speed_q)
    area = jnp.minimum(frac_p, frac_q)
    east = speed >= 0.0
    damping = 0.5 * (1.0 - jnp.abs(speed))
    return east, jnp.where(east, damping, -damping), area * speed, area * (0.5 * (mix_p + mix_q))


def arrival_order():
    flat = [(s, k) for s in range(STEPS) for k in range(PARTS)]
    order = [(0, K, 0)]
    ahead = 1
    for i, (s, k) in enumerate(flat):
        while ahead < len(flat) and ahead <= i + (AHEAD if flat[ahead][0] else 1):
            order.append((flat[ahead][0], K, flat[ahead][1]))
            ahead += 1
        order.append((s, W, k))
    return order


def transport_kernel(
    counts, tr_hbm, vel_hbm, up_hbm, dif_hbm, mask_hbm, level_hbm, part_hbm, out_ref,
    c0, c1, flow, frac, xflux, info, mask_ref, level_ref, part_ref,
    own_sem, in_sem, column_sem, zs, zr, c0s, c0r, c1s, c1r, ss, sr, kvs, kvr, uks, ukr,
    frs, frr, ifs, ifr, rbs, rbr, ready, passing, share_inverse, lid,
):
    n, n_lat, n_lon = counts
    tracer_count, rows, cols, levels = tr_hbm.shape
    tiles = cols // TILE
    t, la, lo = lax.axis_index("trc"), lax.axis_index("lat"), lax.axis_index("lon")
    west = lo == 0
    inner = pl.ds(PAD, cols)
    body = pl.ds(1, rows)
    left_halo, right_halo = pl.ds(0, PAD), pl.ds(PAD + cols, PAD)
    left_edge, right_edge = pl.ds(PAD, PAD), pl.ds(cols, PAD)
    middle = (t == 1) | (t == n - 2)
    ends = jnp.logical_not(middle)
    far_end = jnp.where(t == 1, 0, n - 1)
    far_row = jnp.where(t == 1, n - 1, 0)
    far_pair = jnp.where(t < 2, 2, 0)

    sides = (
        (la > 0, {"lat": la - 1}),
        (la < n_lat - 1, {"lat": la + 1}),
        (lo > 0, {"lon": lo - 1}),
        (lo < n_lon - 1, {"lon": lo + 1}),
    )
    opposite = (1, 0, 3, 2)
    NORTH, SOUTH, WEST, EAST = range(4)
    later = (sides[SOUTH], sides[EAST], (t < n - 1, {"trc": t + 1}), (t < n - 2, {"trc": t + 2}),
             (la < n_lat - 2, {"lat": la + 2}))
    earlier = (sides[NORTH], sides[WEST], (t > 0, {"trc": t - 1}), (t == 2, {"trc": t - 2}),
               (la == n_lat - 1, {"lat": la - 2}))
    awaited = (la > 0, lo > 0, t > 0, t > 1, la > 1)

    columns = [
        pltpu.make_async_copy(src, dst, column_sem.at[i])
        for i, (src, dst) in enumerate(
            ((mask_hbm, mask_ref), (level_hbm, level_ref), (part_hbm, part_ref)))
    ]
    barrier = pltpu.get_barrier_semaphore()
    for there, device in later:
        @pl.when(there)
        def _(device=device):
            pl.semaphore_signal(barrier, inc=1, device_id=device, device_id_type=MESH)

    def source(s, f):
        return {
            U: lambda: vel_hbm.at[s, 0], V: lambda: vel_hbm.at[s, 1],
            K: lambda: dif_hbm.at[s], W: lambda: up_hbm.at[s],
        }[f]()

    def own_copy(s, f):
        return pltpu.make_async_copy(
            source(s, f), flow.at[s, f, 1 + t, inner], own_sem.at[s, f]
        )

    for f in (K, V, W, U):
        own_copy(0, f).start()
    own_field = pltpu.make_async_copy(tr_hbm, c0.at[:, pl.ds(2, rows), inner], in_sem)

    def part(k, base):
        before, share = sum(SHARES[:k]), SHARES[k]
        at = TILE * jnp.where(west, tiles - before - share, before)
        return pl.ds(pl.multiple_of(base + at, TILE), TILE * share)

    first_tile = [
        jnp.where(west, tiles - sum(WINDOWS[:k + 1]), sum(WINDOWS[:k])) for k in range(PARTS)
    ]

    def window_columns(k):
        return pl.ds(pl.multiple_of(PAD + TILE * first_tile[k], TILE), TILE * WINDOWS[k])

    def group_copy(item, row, count, target, sent, landed, wide=False):
        s, f, k = item
        at = inner if wide else part(k, PAD)
        ref = flow.at[s, pl.ds(f, 2), pl.ds(1 + row, count), at]
        return pltpu.make_async_remote_copy(
            src_ref=ref, dst_ref=ref, send_sem=zs.at[s, f // 2, sent],
            recv_sem=zr.at[s, f // 2, k, landed],
            device_id={"trc": target}, device_id_type=MESH,
        )

    def up_copy(item, **kw):
        return group_copy(item, t, 1, t + 1, 0, 1, **kw)

    def down_copy(item, **kw):
        return group_copy(item, t, 1, t - 1, 1, 0, **kw)

    def far_copy(item, **kw):
        return group_copy(item, t, 1, jnp.where(t == 0, 2, 1), 2, 2, **kw)

    def relay_copy(item, **kw):
        return group_copy(item, far_pair, 2, far_end, 2, 2, **kw)

    def side_copy(src, dst, send, recv, i):
        return pltpu.make_async_remote_copy(
            src_ref=src, dst_ref=dst, send_sem=send, recv_sem=recv,
            device_id=sides[i][1], device_id_type=MESH,
        )

    def start_rows(k, i):
        src = pl.ds(0 if i == NORTH else rows - 2, 2)
        dst = pl.ds(rows + 2 if i == NORTH else 0, 2)
        return side_copy(
            tr_hbm.at[:, src, part(k, 0)], c0.at[:, dst, part(k, PAD)],
            c0s.at[i], c0r.at[i, k], i)

    def detour(k, i):
        src = pl.ds(0 if i == NORTH else rows - 2, 2)
        return pltpu.make_async_remote_copy(
            src_ref=tr_hbm.at[:, src, part(k, 0)], dst_ref=passing.at[:, :, part(k, 0)],
            send_sem=c0s.at[i], recv_sem=rbr.at[k],
            device_id={"lat": 0 if i == NORTH else n_lat - 1}, device_id_type=MESH,
        )

    def pass_on(k, i):
        dst = pl.ds(rows + 2 if i == NORTH else 0, 2)
        return pltpu.make_async_remote_copy(
            src_ref=passing.at[:, :, part(k, 0)], dst_ref=c0.at[:, dst, part(k, PAD)],
            send_sem=rbs, recv_sem=c0r.at[i, k],
            device_id={"lat": 1 if i == NORTH else n_lat - 2}, device_id_type=MESH,
        )

    def pass_all(ks):
        for at, i in ((0, NORTH), (n_lat - 1, SOUTH)):
            @pl.when(la == at)
            def _(i=i):
                for k in ks:
                    detour(k, i).wait_recv()
                    pass_on(k, i).start()

    def step_rows(k, i):
        src = pl.ds(2 if i == NORTH else rows, 2)
        dst = pl.ds(rows + 2 if i == NORTH else 0, 2)
        at = window_columns(k)
        return side_copy(c1.at[:, src, at], c1.at[:, dst, at], c1s.at[i], c1r.at[i, k], i)

    def strip(s, i):
        if s == 0:
            edge = pl.ds(0, PAD) if i == WEST else pl.ds(cols - PAD, PAD)
            src = tr_hbm.at[:, :, edge]
        else:
            src = c1.at[:, pl.ds(2, rows), left_edge if i == WEST else right_edge]
        halo = right_halo if i == WEST else left_halo
        dst = (c0, c1)[s].at[:, pl.ds(2, rows), halo]
        return side_copy(src, dst, ss.at[s, i - 2], sr.at[s, i - 2], i)

    def flow_rows(s, k, i):
        kv = pl.ds(K, 2)
        src, dst = (1, rows + 1) if i == NORTH else (rows, 0)
        at = part(k, PAD)
        return side_copy(flow.at[s, kv, src, at], flow.at[s, kv, dst, at],
                         kvs.at[s, i], kvr.at[s, i, k], i)

    def flow_strip(s, i):
        uk = pl.ds(U, 2)
        src, dst = (left_edge, right_halo) if i == WEST else (right_edge, left_halo)
        return side_copy(flow.at[s, uk, body, src], flow.at[s, uk, body, dst],
                         uks.at[s, i - 2], ukr.at[s, i - 2], i)

    def frac_strip(i):
        src, dst = (left_edge, right_halo) if i == WEST else (right_edge, left_halo)
        return side_copy(frac.at[body, src], frac.at[body, dst], frs.at[i - 2], frr.at[i - 2], i)

    def info_copy(i):
        return side_copy(info.at[0], info.at[1 + i], ifs.at[i], ifr.at[i], i)

    lat_sides, lon_sides = (NORTH, SOUTH), (WEST, EAST)

    def on_sides(make, which, act="start"):
        for i in which:
            @pl.when(sides[i][0])
            def _(i=i):
                getattr(make(i), act)()

    def receive(make, which):
        for i in which:
            @pl.when(sides[opposite[i]][0])
            def _(i=i):
                make(i).wait_recv()

    order = arrival_order()

    total = 0
    for there in awaited:
        total = total + jnp.where(there, 1, 0)
    pl.when(total > 0)(lambda: pl.semaphore_wait(barrier, total))
    for i, (there, device) in enumerate(earlier):
        @pl.when(there)
        def _(i=i, device=device):
            pl.semaphore_signal(ready.at[i], inc=1, device_id=device, device_id_type=MESH)

    def greet(i, there):
        @pl.when(there)
        def _():
            pl.semaphore_wait(ready.at[i], 1)

    def first_copies(item, target, sent, landed):
        s, f, k = item
        for field in (f, f + 1):
            pltpu.make_async_remote_copy(
                src_ref=source(s, field).at[part(k, 0)],
                dst_ref=flow.at[s, field, 1 + t, part(k, PAD)],
                send_sem=zs.at[s, f // 2, sent], recv_sem=zr.at[s, f // 2, k, landed],
                device_id={"trc": target}, device_id_type=MESH,
            ).start()

    @pl.when(t > 0)
    def _():
        for item in order[:DIRECT]:
            @pl.when(t == n - 1)
            def _(item=item):
                first_copies(item, 1, 2, 2)
            first_copies(item, t - 1, 1, 0)

    for f in (K, V, W, U):
        own_copy(1, f).start()
    for copy in columns:
        copy.start()
    own_field.start()
    for s in range(STEPS):
        for f in (K, V, W, U):
            own_copy(s, f).wait()

    @pl.when(t > 0)
    def _():
        for item in order[DIRECT:LEAD]:
            @pl.when(t == n - 1)
            def _(item=item):
                far_copy(item).start()
            down_copy(item).start()

    def outward(make, i):
        for k in range(PARTS):
            make(k, i).start()

    greet(2, t < n - 1)
    greet(3, t == 0)

    @pl.when(t < n - 1)
    def _():
        for item in order[:LEAD]:
            @pl.when(t == 0)
            def _(item=item):
                far_copy(item).start()
            up_copy(item).start()

    pl.when((la > 0) & (la != 2))(lambda: outward(start_rows, NORTH))
    pl.when(la == 2)(lambda: outward(detour, NORTH))
    greet(4, la == 1)
    pl.when(la == 1)(lambda: outward(detour, SOUTH))
    greet(0, la < n_lat - 1)
    pl.when((la < n_lat - 1) & (la != 1))(lambda: outward(start_rows, SOUTH))
    for side, own in ((NORTH, 0), (SOUTH, n - 1)):
        @pl.when(sides[side][0] & (t == own))
        def _(side=side):
            for k in range(PARTS):
                flow_rows(0, k, side).start()

    def early_rows():
        for side, own in ((NORTH, 0), (SOUTH, n - 1)):
            @pl.when(sides[side][0] & (t == own))
            def _(side=side):
                for k in range(PARTS):
                    flow_rows(1, k, side).start()

    if LATER < 0:
        early_rows()
    else:
        pl.when(lo == 0)(early_rows)

    pl.when(lo > 0)(lambda: strip(0, WEST).start())
    greet(1, lo < n_lon - 1)
    pl.when(lo < n_lon - 1)(lambda: strip(0, EAST).start())

    def send_own(item):
        @pl.when(t > 0)
        def _():
            down_copy(item).start()

        @pl.when(t < n - 1)
        def _():
            up_copy(item).start()

    @pl.when(ends)
    def _():
        for item in order[LEAD:]:
            far_copy(item).start()
            send_own(item)

    square = (cols, cols)
    eye = lax.broadcasted_iota(jnp.int32, square, 0) == lax.broadcasted_iota(jnp.int32, square, 1)
    level = lax.broadcasted_iota(jnp.int32, (cols, levels), 1).astype(jnp.float32)

    def upright(row):
        return jnp.sum(jnp.where(eye, jnp.broadcast_to(row, square), 0.0), axis=1, keepdims=True)

    def fill_fraction(slot, r, row):
        wet, share, deepest = (
            upright(info[slot, 8 * i + r:8 * i + r + 1, 0:cols]) for i in range(3)
        )
        cells_of = jnp.where(level < deepest, wet, jnp.where(level == deepest, share, 0.0))
        frac[row, inner, :] = cells_of
        return cells_of

    for copy in columns:
        copy.wait()
    wet = mask_ref[...].astype(jnp.float32)
    info[0] = jnp.zeros(info.shape[1:], jnp.float32)
    info[0, 0:rows, 0:cols] = wet
    info[0, 8:8 + rows, 0:cols] = wet * part_ref[...]
    info[0, 16:16 + rows, 0:cols] = level_ref[...].astype(jnp.float32) - 1.0
    on_sides(info_copy, lat_sides)
    for r in range(rows):
        share = fill_fraction(0, r, 1 + r)
        share_inverse[r] = 1.0 / jnp.maximum(share, fraction_floor)
        lid[r] = jnp.where(
            level == levels - 1, 0.0, jnp.minimum(share, pltpu.roll(share, levels - 1, 1))
        )
    on_sides(frac_strip, lon_sides)

    @pl.when(la == 0)
    def _():
        for field in (c0, c1):
            field[:, 0:2] = jnp.zeros((tracer_count, 2) + field.shape[2:], jnp.float32)
        frac[0] = jnp.zeros(frac.shape[1:], jnp.float32)
        flow[:, K:, 0] = jnp.zeros((STEPS, 2) + flow.shape[3:], jnp.float32)

    @pl.when(la == n_lat - 1)
    def _():
        for field in (c0, c1):
            field[:, rows + 2:] = jnp.zeros((tracer_count, 2) + field.shape[2:], jnp.float32)
        frac[rows + 1] = jnp.zeros(frac.shape[1:], jnp.float32)
        flow[:, K:, rows + 1] = jnp.zeros((STEPS, 2) + flow.shape[3:], jnp.float32)

    for at_edge, halo in ((lo == 0, left_halo), (lo == n_lon - 1, right_halo)):
        @pl.when(at_edge)
        def _(halo=halo):
            for field in (c0, c1):
                field[:, 2:2 + rows, halo] = jnp.zeros(
                    (tracer_count, rows, PAD, levels), jnp.float32)
            frac[1:1 + rows, halo] = jnp.zeros((rows, PAD, levels), jnp.float32)
            flow[:, U:U + 2, 1:1 + rows, halo] = jnp.zeros(
                (STEPS, 2, rows, PAD, levels), jnp.float32)

    def prepare():
        receive(info_copy, lat_sides)
        for side, r, row in ((SOUTH, rows - 1, 0), (NORTH, 0, rows + 1)):
            @pl.when(sides[opposite[side]][0])
            def _(side=side, r=r, row=row):
                fill_fraction(1 + side, r, row)
        own_field.wait()
        receive(frac_strip, lon_sides)
        receive(functools.partial(strip, 0), lon_sides)

    def faces(s, src, first, count):
        for i in range(count):
            base = pl.multiple_of(TILE * (first + i), TILE)
            p, q = pl.ds(base + PAD - 1, TILE), pl.ds(base + PAD, TILE)
            for r in range(rows):
                terms = face_terms(
                    flow[s, U, r + 1, p], flow[s, U, r + 1, q],
                    flow[s, K, r + 1, p], flow[s, K, r + 1, q], frac[r + 1, p], frac[r + 1, q],
                )
                for a in range(tracer_count):
                    xflux[a, r, pl.ds(base, TILE)] = limited_flux(
                        src[a, r + 2, pl.ds(base + PAD - 2, TILE)], src[a, r + 2, p],
                        src[a, r + 2, q], src[a, r + 2, pl.ds(base + PAD + 1, TILE)], *terms,
                    )

    def cells(s, src, dst, row_shift, shift, first, count):
        for i in range(count):
            base = pl.multiple_of(TILE * (first + i), TILE)
            at = pl.ds(base + PAD, TILE)

            def row_flux(r):
                terms = face_terms(
                    flow[s, V, r, at], flow[s, V, r + 1, at],
                    flow[s, K, r, at], flow[s, K, r + 1, at], frac[r, at], frac[r + 1, at],
                )
                return [
                    limited_flux(
                        src[a, r, at], src[a, r + 1, at], src[a, r + 2, at], src[a, r + 3, at],
                        *terms)
                    for a in range(tracer_count)
                ]

            lower = row_flux(0)
            for r in range(rows):
                upper = row_flux(r + 1)
                rise = flow[s, W, r + 1, at]
                lifted = lid[r, pl.ds(base, TILE)] * rise
                upward = rise >= 0.0
                inverse = share_inverse[r, pl.ds(base, TILE)]
                for a in range(tracer_count):
                    centre = src[a, r + 2, at]
                    vertical = lifted * jnp.where(
                        upward, centre, pltpu.roll(centre, levels - 1, 1)
                    )
                    net = (
                        (upper[a] - lower[a])
                        + (xflux[a, r, pl.ds(base + 1, TILE)] - xflux[a, r, pl.ds(base, TILE)])
                        + (vertical - pltpu.roll(vertical, 1, 1))
                    )
                    dst[a, r + row_shift, pl.ds(base + shift, TILE)] = centre - net * inverse
                lower = upper

    def arrive(item):
        @pl.when(t > 0)
        def _():
            group_copy(item, t - 1, 1, t, 0, 1).wait_recv()

        @pl.when(t < n - 1)
        def _():
            group_copy(item, t + 1, 1, t, 0, 0).wait_recv()

        @pl.when(middle)
        def _():
            group_copy(item, far_row, 1, t, 0, 2).wait_recv()
            relay_copy(item).start()

        @pl.when(ends)
        def _():
            group_copy(item, far_pair, 2, t, 0, 2).wait_recv()

    def after(i):
        s, f, k = order[i]
        if i + LEAD < len(order):
            pl.when(middle)(lambda: send_own(order[i + LEAD]))
        if f == K:
            for side, own in ((NORTH, 0), (SOUTH, n - 1)):
                @pl.when(sides[side][0] & (t != own))
                def _(side=side):
                    flow_rows(s, k, side).start()
        elif k == 0:
            on_sides(functools.partial(flow_strip, s), lon_sides)

    def window(s, k):
        src = (c0, c1)[s]
        if k == 0:
            receive(functools.partial(flow_strip, s), lon_sides)
            if s == 1:
                receive(functools.partial(strip, 1), lon_sides)
        at = first_tile[k]
        low = jnp.where(west, at, at + (1 if k > 0 else 0))
        count = WINDOWS[k] + (1 if k == 0 else 0)
        faces(s, src, low, count)
        receive(functools.partial(start_rows if s == 0 else step_rows, k), lat_sides)
        receive(functools.partial(flow_rows, s, k), lat_sides)
        if s == 0:
            cells(s, src, c1, 2, PAD, at, WINDOWS[k])
            on_sides(functools.partial(step_rows, k), lat_sides)
            if k == 0:
                on_sides(functools.partial(strip, 1), lon_sides)
        else:
            cells(s, src, out_ref, 0, 0, at, WINDOWS[k])

    def finish(s):
        for f in (K, W):
            item = (s, f, 0)

            @pl.when(t < n - 1)
            def _(item=item):
                up_copy(item, wide=True).wait_send()

            @pl.when(t > 0)
            def _(item=item):
                down_copy(item, wide=True).wait_send()

            @pl.when(ends)
            def _(item=item):
                far_copy(item, wide=True).wait_send()

            @pl.when(middle)
            def _(item=item):
                relay_copy(item, wide=True).wait_send()

        on_sides(functools.partial(strip, s), lon_sides, "wait_send")
        on_sides(functools.partial(flow_strip, s), lon_sides, "wait_send")
        for i in lat_sides:
            @pl.when(sides[i][0])
            def _(i=i):
                kv, two = pl.ds(K, 2), pl.ds(0, 2)
                field = (c0, c1)[s].at[:, two, inner]
                side_copy(flow.at[s, kv, 1, inner], flow.at[s, kv, 1, inner],
                          kvs.at[s, i], kvr.at[s, i, 0], i).wait_send()
                side_copy(field, field, (c0s, c1s)[s].at[i], (c0r, c1r)[s].at[i, 0], i).wait_send()
    def finish_start():
        on_sides(frac_strip, lon_sides, "wait_send")
        on_sides(info_copy, lat_sides, "wait_send")

        @pl.when((la == 0) | (la == n_lat - 1))
        def _():
            pltpu.make_async_copy(passing, passing, rbs).wait()

    for i, item in enumerate(order):
        if i == len(order) - SETTLE:
            finish_start()
            finish(0)
        arrive(item)
        after(i)
        pass_all(PASSES.get(i, ()))
        if i == PREPARED:
            prepare()
        if i == LATER:
            pl.when(lo != 0)(early_rows)
        due = [
            {(s, k) for s in range(STEPS) for k in range(PARTS)
             if i == min(order.index((s, W, k)) + lags[s], len(order) - 1)}
            for lags in (END_LAGS, MIDDLE_LAGS)
        ]
        for s, k in sorted(due[0] | due[1]):
            here = [(s, k) in those for those in due]
            if all(here):
                window(s, k)
            else:
                pl.when(ends if here[0] else middle)(functools.partial(window, s, k))

    finish(STEPS - 1)


def fused_body(counts, tracers, land_mask, bottom_level, bottom_part, velocity, upwelling,
               diffusivity):
    tracer_count, rows, cols, levels = tracers.shape
    wide = cols + 2 * PAD
    row = (cols, levels)
    dma = pltpu.SemaphoreType.DMA
    hbm, vmem = pl.BlockSpec(memory_space=pltpu.HBM), pl.BlockSpec(memory_space=pltpu.VMEM)
    return pl.pallas_call(
        functools.partial(transport_kernel, counts),
        out_shape=pltpu.VMEM(tracers.shape, jnp.float32),
        in_specs=[hbm] * 7,
        out_specs=vmem,
        scratch_shapes=[
            pltpu.VMEM((tracer_count, rows + 4, wide + PAD, levels), jnp.float32),
            pltpu.VMEM((tracer_count, rows + 4, wide + PAD, levels), jnp.float32),
            pltpu.VMEM((STEPS, 4, rows + 2, wide, levels), jnp.float32),
            pltpu.VMEM((rows + 2, wide, levels), jnp.float32),
            pltpu.VMEM((tracer_count, rows, cols + 16, levels), jnp.float32),
            pltpu.VMEM((3, 24, 128), jnp.float32),
            pltpu.VMEM((rows, cols), jnp.int32),
            pltpu.VMEM((rows, cols), jnp.int32),
            pltpu.VMEM((rows, cols), jnp.float32),
            dma((STEPS, 4)), dma, dma((3,)),
            dma((STEPS, 2, 3)), dma((STEPS, 2, PARTS, 3)),
            dma((2,)), dma((2, PARTS)), dma((2,)), dma((2, PARTS)),
            dma((STEPS, 2)), dma((STEPS, 2)),
            dma((STEPS, 2)), dma((STEPS, 2, PARTS)),
            dma((STEPS, 2)), dma((STEPS, 2)),
            dma((2,)), dma((2,)), dma((2,)), dma((2,)),
            dma, dma((PARTS,)), pltpu.SemaphoreType.REGULAR((5,)),
            pltpu.VMEM((tracer_count, 2, cols, levels), jnp.float32),
            pltpu.VMEM((rows, cols, levels), jnp.float32),
            pltpu.VMEM((rows, cols, levels), jnp.float32),
        ],
        compiler_params=pltpu.CompilerParams(
            collective_id=0, has_side_effects=True, vmem_limit_bytes=60 * 1024 * 1024
        ),
    )(
        tracers,
        velocity.reshape((STEPS, 2) + row),
        upwelling.reshape((STEPS,) + row),
        diffusivity.reshape((STEPS,) + row),
        land_mask, bottom_level, bottom_part,
    )


def solution(mesh):
    placed = (
        P("trc", "lat", "lon", None),
        P("lat", "lon"),
        P("lat", "lon"),
        P("lat", "lon"),
        P(None, None, ("lat", "lon"), "trc"),
        P(None, ("lat", "lon"), "trc"),
        P(None, ("lat", "lon"), "trc"),
    )
    counts = tuple(mesh.shape[axis] for axis in ("trc", "lat", "lon"))

    def body(*arrays):
        tracers, velocity = arrays[0], arrays[4]
        one_row = velocity.shape[3] == tracers.shape[2] * tracers.shape[3]
        blocks = tracers.shape[1] == 4 and tracers.shape[2] == 64 and tracers.shape[3] == 128
        if counts == (4, 4, 2) and blocks and one_row:
            return fused_body(counts, *arrays)
        return gathered_body(*arrays)

    return jax.shard_map(
        body, mesh=mesh, in_specs=placed, out_specs=P("trc", "lat", "lon", None), check_vma=False
    )
```

```python
import functools

import jax
import jax.numpy as jnp
from jax import lax
from jax.experimental import pallas as pl
from jax.experimental.pallas import tpu as pltpu
from jax.sharding import PartitionSpec as P

STEPS = 2
MESH = pl.DeviceIdType.MESH


fraction_floor = 0.25


def with_halo(block, sides, width):
    for axis, dim in sides:
        count = lax.axis_size(axis)
        forward = [(i, i + 1) for i in range(count - 1)]
        backward = [(target, source) for source, target in forward]
        low = lax.ppermute(
            lax.slice_in_dim(block, block.shape[dim] - width, None, axis=dim), axis, forward
        )
        high = lax.ppermute(lax.slice_in_dim(block, 0, width, axis=dim), axis, backward)
        block = jnp.concatenate([low, block, high], axis=dim)
    return block


def minmod(first, second):
    return 0.5 * (jnp.sign(first) + jnp.sign(second)) * jnp.minimum(jnp.abs(first), jnp.abs(second))


def window(array, start, stop, offset):
    return lax.slice_in_dim(array, start, stop, axis=array.ndim + offset)


def face_divergence(field, speed, mixing, fraction, offset):
    extent = field.shape[field.ndim + offset]
    before = window(field, 0, extent - 3, offset)
    lower = window(field, 1, extent - 2, offset)
    upper = window(field, 2, extent - 1, offset)
    after = window(field, 3, extent, offset)
    face_speed = 0.5 * (window(speed, 1, extent - 2, offset) + window(speed, 2, extent - 1, offset))
    face_area = jnp.minimum(
        window(fraction, 1, extent - 2, offset), window(fraction, 2, extent - 1, offset)
    )
    face_mixing = 0.5 * (
        window(mixing, 1, extent - 2, offset) + window(mixing, 2, extent - 1, offset)
    )
    jump = upper - lower
    damping = 0.5 * (1.0 - jnp.abs(face_speed))
    from_lower = lower + damping * minmod(lower - before, jump)
    from_upper = upper - damping * minmod(jump, after - upper)
    face_value = jnp.where(face_speed >= 0.0, from_lower, from_upper)
    face_flux = face_area * (face_speed * face_value - face_mixing * jump)
    return window(face_flux, 1, extent - 3, offset) - window(face_flux, 0, extent - 4, offset)


def substep(field, fraction, eastward, northward, mixing, rising):
    across_rows = face_divergence(field, northward, mixing, fraction, -3)[..., 2:-2, :]
    across_cols = face_divergence(field, eastward, mixing, fraction, -2)[..., 2:-2, :, :]
    centre = field[..., 2:-2, 2:-2, :]
    wet_share = fraction[2:-2, 2:-2, :]
    top_area = jnp.minimum(wet_share[:, :, :-1], wet_share[:, :, 1:])
    lifting = rising[:, :, :-1]
    carried = jnp.where(lifting >= 0.0, centre[..., :-1], centre[..., 1:])
    vertical = top_area * lifting * carried
    closed = jnp.zeros(vertical.shape[:-1] + (1,), jnp.float32)
    across_levels = jnp.concatenate([vertical, closed], axis=-1) - jnp.concatenate(
        [closed, vertical], axis=-1
    )
    return centre - (across_rows + across_cols + across_levels) / jnp.maximum(
        wet_share, fraction_floor
    )


def cell_fraction(land_mask, bottom_level, bottom_part, levels):
    level_index = lax.broadcasted_iota(jnp.int32, land_mask.shape + (levels,), 2)
    deepest = bottom_level[:, :, None] - 1
    full_cell = (level_index < deepest).astype(jnp.float32)
    last_cell = (level_index == deepest).astype(jnp.float32) * bottom_part[:, :, None]
    return land_mask.astype(jnp.float32)[:, :, None] * (full_cell + last_cell)


def gathered_body(tracers, land_mask, bottom_level, bottom_part, velocity, upwelling, diffusivity):
    levels = tracers.shape[3]
    block_shape = (tracers.shape[1], tracers.shape[2], levels)
    fraction = cell_fraction(land_mask, bottom_level, bottom_part, levels)
    tracer_count = tracers.shape[0]
    moved = (
        lax.all_gather(velocity, "trc", axis=3, tiled=True),
        lax.all_gather(upwelling, "trc", axis=2, tiled=True),
        lax.all_gather(diffusivity, "trc", axis=2, tiled=True),
    )
    speeds = moved[0].reshape((STEPS, 2) + block_shape)
    rises = moved[1].reshape((STEPS,) + block_shape)
    mixes = moved[2].reshape((STEPS,) + block_shape)
    field = tracers
    wide_frac = fraction
    for number in range(STEPS):
        extras = [fraction[None]] if number == 0 else []
        stack = jnp.concatenate(
            [field] + extras + [jnp.stack([speeds[number, 0], speeds[number, 1], mixes[number]])],
            axis=0,
        )
        widened = with_halo(stack, (("lat", 1), ("lon", 2)), 2)
        if number == 0:
            wide_frac = widened[tracer_count]
        flows = widened[-3:]
        field = substep(
            widened[:tracer_count], wide_frac, flows[0], flows[1], flows[2], rises[number]
        )
    return field


W, U, K, V = range(4)
PAD = 8
TILE = 8
SHARES = (2, 2, 2, 2)
PARTS = len(SHARES)
LEAD = 11
END_LAGS = (1, 1)
MIDDLE_LAGS = (1, 1)
AHEAD = 2
DIRECT = 3
SETTLE = 2
PREPARED = 3
LATER = -1
PASSES = {0: (0,), 1: (1,), 2: tuple(range(2, PARTS))}
WINDOWS = tuple(share - (k == 0) + (k == PARTS - 1) for k, share in enumerate(SHARES))


def limited_flux(before, lower, upper, after, east, scale, area_speed, area_mix):
    jump = upper - lower
    base = jnp.where(east, lower, upper)
    slope = jnp.where(east, lower - before, after - upper)
    limited = jnp.maximum(jnp.minimum(slope, jump), 0.0) + jnp.minimum(
        jnp.maximum(slope, jump), 0.0
    )
    return area_speed * (base + scale * limited) - area_mix * jump


def face_terms(speed_p, speed_q, mix_p, mix_q, frac_p, frac_q):
    speed = 0.5 * (speed_p + speed_q)
    area = jnp.minimum(frac_p, frac_q)
    east = speed >= 0.0
    damping = 0.5 * (1.0 - jnp.abs(speed))
    return east, jnp.where(east, damping, -damping), area * speed, area * (0.5 * (mix_p + mix_q))


def arrival_order():
    flat = [(s, k) for s in range(STEPS) for k in range(PARTS)]
    order = [(0, K, 0)]
    ahead = 1
    for i, (s, k) in enumerate(flat):
        while ahead < len(flat) and ahead <= i + (AHEAD if flat[ahead][0] else 1):
            order.append((flat[ahead][0], K, flat[ahead][1]))
            ahead += 1
        order.append((s, W, k))
    return order


def transport_kernel(
    counts, tr_hbm, vel_hbm, up_hbm, dif_hbm, mask_hbm, level_hbm, part_hbm, out_ref,
    c0, c1, flow, frac, xflux, info, mask_ref, level_ref, part_ref,
    own_sem, in_sem, column_sem, zs, zr, c0s, c0r, c1s, c1r, ss, sr, kvs, kvr, uks, ukr,
    frs, frr, ifs, ifr, rbs, rbr, ready, passing, share_inverse, lid,
):
    n, n_lat, n_lon = counts
    tracer_count, rows, cols, levels = tr_hbm.shape
    tiles = cols // TILE
    t, la, lo = lax.axis_index("trc"), lax.axis_index("lat"), lax.axis_index("lon")
    west = lo == 0
    inner = pl.ds(PAD, cols)
    body = pl.ds(1, rows)
    left_halo, right_halo = pl.ds(0, PAD), pl.ds(PAD + cols, PAD)
    left_edge, right_edge = pl.ds(PAD, PAD), pl.ds(cols, PAD)
    middle = (t == 1) | (t == n - 2)
    ends = jnp.logical_not(middle)
    far_end = jnp.where(t == 1, 0, n - 1)
    far_row = jnp.where(t == 1, n - 1, 0)
    far_pair = jnp.where(t < 2, 2, 0)

    sides = (
        (la > 0, {"lat": la - 1}),
        (la < n_lat - 1, {"lat": la + 1}),
        (lo > 0, {"lon": lo - 1}),
        (lo < n_lon - 1, {"lon": lo + 1}),
    )
    opposite = (1, 0, 3, 2)
    NORTH, SOUTH, WEST, EAST = range(4)
    later = (sides[SOUTH], sides[EAST], (t < n - 1, {"trc": t + 1}), (t < n - 2, {"trc": t + 2}),
             (la < n_lat - 2, {"lat": la + 2}))
    earlier = (sides[NORTH], sides[WEST], (t > 0, {"trc": t - 1}), (t == 2, {"trc": t - 2}),
               (la == n_lat - 1, {"lat": la - 2}))
    awaited = (la > 0, lo > 0, t > 0, t > 1, la > 1)

    columns = [
        pltpu.make_async_copy(src, dst, column_sem.at[i])
        for i, (src, dst) in enumerate(
            ((mask_hbm, mask_ref), (level_hbm, level_ref), (part_hbm, part_ref)))
    ]
    barrier = pltpu.get_barrier_semaphore()
    for there, device in later:
        @pl.when(there)
        def _(device=device):
            pl.semaphore_signal(barrier, inc=1, device_id=device, device_id_type=MESH)

    def source(s, f):
        return {
            U: lambda: vel_hbm.at[s, 0], V: lambda: vel_hbm.at[s, 1],
            K: lambda: dif_hbm.at[s], W: lambda: up_hbm.at[s],
        }[f]()

    def own_copy(s, f):
        return pltpu.make_async_copy(
            source(s, f), flow.at[s, f, 1 + t, inner], own_sem.at[s, f]
        )

    for f in (K, V, W, U):
        own_copy(0, f).start()
    own_field = pltpu.make_async_copy(tr_hbm, c0.at[:, pl.ds(2, rows), inner], in_sem)

    def part(k, base):
        before, share = sum(SHARES[:k]), SHARES[k]
        at = TILE * jnp.where(west, tiles - before - share, before)
        return pl.ds(pl.multiple_of(base + at, TILE), TILE * share)

    first_tile = [
        jnp.where(west, tiles - sum(WINDOWS[:k + 1]), sum(WINDOWS[:k])) for k in range(PARTS)
    ]

    def window_columns(k):
        return pl.ds(pl.multiple_of(PAD + TILE * first_tile[k], TILE), TILE * WINDOWS[k])

    def group_copy(item, row, count, target, sent, landed, wide=False):
        s, f, k = item
        at = inner if wide else part(k, PAD)
        ref = flow.at[s, pl.ds(f, 2), pl.ds(1 + row, count), at]
        return pltpu.make_async_remote_copy(
            src_ref=ref, dst_ref=ref, send_sem=zs.at[s, f // 2, sent],
            recv_sem=zr.at[s, f // 2, k, landed],
            device_id={"trc": target}, device_id_type=MESH,
        )

    def up_copy(item, **kw):
        return group_copy(item, t, 1, t + 1, 0, 1, **kw)

    def down_copy(item, **kw):
        return group_copy(item, t, 1, t - 1, 1, 0, **kw)

    def far_copy(item, **kw):
        return group_copy(item, t, 1, jnp.where(t == 0, 2, 1), 2, 2, **kw)

    def relay_copy(item, **kw):
        return group_copy(item, far_pair, 2, far_end, 2, 2, **kw)

    def side_copy(src, dst, send, recv, i):
        return pltpu.make_async_remote_copy(
            src_ref=src, dst_ref=dst, send_sem=send, recv_sem=recv,
            device_id=sides[i][1], device_id_type=MESH,
        )

    def start_rows(k, i):
        src = pl.ds(0 if i == NORTH else rows - 2, 2)
        dst = pl.ds(rows + 2 if i == NORTH else 0, 2)
        return side_copy(
            tr_hbm.at[:, src, part(k, 0)], c0.at[:, dst, part(k, PAD)],
            c0s.at[i], c0r.at[i, k], i)

    def detour(k, i):
        src = pl.ds(0 if i == NORTH else rows - 2, 2)
        return pltpu.make_async_remote_copy(
            src_ref=tr_hbm.at[:, src, part(k, 0)], dst_ref=passing.at[:, :, part(k, 0)],
            send_sem=c0s.at[i], recv_sem=rbr.at[k],
            device_id={"lat": 0 if i == NORTH else n_lat - 1}, device_id_type=MESH,
        )

    def pass_on(k, i):
        dst = pl.ds(rows + 2 if i == NORTH else 0, 2)
        return pltpu.make_async_remote_copy(
            src_ref=passing.at[:, :, part(k, 0)], dst_ref=c0.at[:, dst, part(k, PAD)],
            send_sem=rbs, recv_sem=c0r.at[i, k],
            device_id={"lat": 1 if i == NORTH else n_lat - 2}, device_id_type=MESH,
        )

    def pass_all(ks):
        for at, i in ((0, NORTH), (n_lat - 1, SOUTH)):
            @pl.when(la == at)
            def _(i=i):
                for k in ks:
                    detour(k, i).wait_recv()
                    pass_on(k, i).start()

    def step_rows(k, i):
        src = pl.ds(2 if i == NORTH else rows, 2)
        dst = pl.ds(rows + 2 if i == NORTH else 0, 2)
        at = window_columns(k)
        return side_copy(c1.at[:, src, at], c1.at[:, dst, at], c1s.at[i], c1r.at[i, k], i)

    def strip(s, i):
        if s == 0:
            edge = pl.ds(0, PAD) if i == WEST else pl.ds(cols - PAD, PAD)
            src = tr_hbm.at[:, :, edge]
        else:
            src = c1.at[:, pl.ds(2, rows), left_edge if i == WEST else right_edge]
        halo = right_halo if i == WEST else left_halo
        dst = (c0, c1)[s].at[:, pl.ds(2, rows), halo]
        return side_copy(src, dst, ss.at[s, i - 2], sr.at[s, i - 2], i)

    def flow_rows(s, k, i):
        kv = pl.ds(K, 2)
        src, dst = (1, rows + 1) if i == NORTH else (rows, 0)
        at = part(k, PAD)
        return side_copy(flow.at[s, kv, src, at], flow.at[s, kv, dst, at],
                         kvs.at[s, i], kvr.at[s, i, k], i)

    def flow_strip(s, i):
        uk = pl.ds(U, 2)
        src, dst = (left_edge, right_halo) if i == WEST else (right_edge, left_halo)
        return side_copy(flow.at[s, uk, body, src], flow.at[s, uk, body, dst],
                         uks.at[s, i - 2], ukr.at[s, i - 2], i)

    def frac_strip(i):
        src, dst = (left_edge, right_halo) if i == WEST else (right_edge, left_halo)
        return side_copy(frac.at[body, src], frac.at[body, dst], frs.at[i - 2], frr.at[i - 2], i)

    def info_copy(i):
        return side_copy(info.at[0], info.at[1 + i], ifs.at[i], ifr.at[i], i)

    lat_sides, lon_sides = (NORTH, SOUTH), (WEST, EAST)

    def on_sides(make, which, act="start"):
        for i in which:
            @pl.when(sides[i][0])
            def _(i=i):
                getattr(make(i), act)()

    def receive(make, which):
        for i in which:
            @pl.when(sides[opposite[i]][0])
            def _(i=i):
                make(i).wait_recv()

    order = arrival_order()

    total = 0
    for there in awaited:
        total = total + jnp.where(there, 1, 0)
    pl.when(total > 0)(lambda: pl.semaphore_wait(barrier, total))
    for i, (there, device) in enumerate(earlier):
        @pl.when(there)
        def _(i=i, device=device):
            pl.semaphore_signal(ready.at[i], inc=1, device_id=device, device_id_type=MESH)

    def greet(i, there):
        @pl.when(there)
        def _():
            pl.semaphore_wait(ready.at[i], 1)

    def first_copies(item, target, sent, landed):
        s, f, k = item
        for field in (f, f + 1):
            pltpu.make_async_remote_copy(
                src_ref=source(s, field).at[part(k, 0)],
                dst_ref=flow.at[s, field, 1 + t, part(k, PAD)],
                send_sem=zs.at[s, f // 2, sent], recv_sem=zr.at[s, f // 2, k, landed],
                device_id={"trc": target}, device_id_type=MESH,
            ).start()

    @pl.when(t > 0)
    def _():
        for item in order[:DIRECT]:
            @pl.when(t == n - 1)
            def _(item=item):
                first_copies(item, 1, 2, 2)
            first_copies(item, t - 1, 1, 0)

    for f in (K, V, W, U):
        own_copy(1, f).start()
    for copy in columns:
        copy.start()
    own_field.start()
    for s in range(STEPS):
        for f in (K, V, W, U):
            own_copy(s, f).wait()

    @pl.when(t > 0)
    def _():
        for item in order[DIRECT:LEAD]:
            @pl.when(t == n - 1)
            def _(item=item):
                far_copy(item).start()
            down_copy(item).start()

    def outward(make, i):
        for k in range(PARTS):
            make(k, i).start()

    greet(2, t < n - 1)
    greet(3, t == 0)

    @pl.when(t < n - 1)
    def _():
        for item in order[:LEAD]:
            @pl.when(t == 0)
            def _(item=item):
                far_copy(item).start()
            up_copy(item).start()

    pl.when((la > 0) & (la != 2))(lambda: outward(start_rows, NORTH))
    pl.when(la == 2)(lambda: outward(detour, NORTH))
    greet(4, la == 1)
    pl.when(la == 1)(lambda: outward(detour, SOUTH))
    greet(0, la < n_lat - 1)
    pl.when((la < n_lat - 1) & (la != 1))(lambda: outward(start_rows, SOUTH))
    for side, own in ((NORTH, 0), (SOUTH, n - 1)):
        @pl.when(sides[side][0] & (t == own))
        def _(side=side):
            for k in range(PARTS):
                flow_rows(0, k, side).start()

    def early_rows():
        for side, own in ((NORTH, 0), (SOUTH, n - 1)):
            @pl.when(sides[side][0] & (t == own))
            def _(side=side):
                for k in range(PARTS):
                    flow_rows(1, k, side).start()

    if LATER < 0:
        early_rows()
    else:
        pl.when(lo == 0)(early_rows)

    pl.when(lo > 0)(lambda: strip(0, WEST).start())
    greet(1, lo < n_lon - 1)
    pl.when(lo < n_lon - 1)(lambda: strip(0, EAST).start())

    def send_own(item):
        @pl.when(t > 0)
        def _():
            down_copy(item).start()

        @pl.when(t < n - 1)
        def _():
            up_copy(item).start()

    @pl.when(ends)
    def _():
        for item in order[LEAD:]:
            far_copy(item).start()
            send_own(item)

    square = (cols, cols)
    eye = lax.broadcasted_iota(jnp.int32, square, 0) == lax.broadcasted_iota(jnp.int32, square, 1)
    level = lax.broadcasted_iota(jnp.int32, (cols, levels), 1).astype(jnp.float32)

    def upright(row):
        return jnp.sum(jnp.where(eye, jnp.broadcast_to(row, square), 0.0), axis=1, keepdims=True)

    def fill_fraction(slot, r, row):
        wet, share, deepest = (
            upright(info[slot, 8 * i + r:8 * i + r + 1, 0:cols]) for i in range(3)
        )
        cells_of = jnp.where(level < deepest, wet, jnp.where(level == deepest, share, 0.0))
        frac[row, inner, :] = cells_of
        return cells_of

    for copy in columns:
        copy.wait()
    wet = mask_ref[...].astype(jnp.float32)
    info[0] = jnp.zeros(info.shape[1:], jnp.float32)
    info[0, 0:rows, 0:cols] = wet
    info[0, 8:8 + rows, 0:cols] = wet * part_ref[...]
    info[0, 16:16 + rows, 0:cols] = level_ref[...].astype(jnp.float32) - 1.0
    on_sides(info_copy, lat_sides)
    for r in range(rows):
        share = fill_fraction(0, r, 1 + r)
        share_inverse[r] = 1.0 / jnp.maximum(share, fraction_floor)
        lid[r] = jnp.where(
            level == levels - 1, 0.0, jnp.minimum(share, pltpu.roll(share, levels - 1, 1))
        )
    on_sides(frac_strip, lon_sides)

    @pl.when(la == 0)
    def _():
        for field in (c0, c1):
            field[:, 0:2] = jnp.zeros((tracer_count, 2) + field.shape[2:], jnp.float32)
        frac[0] = jnp.zeros(frac.shape[1:], jnp.float32)
        flow[:, K:, 0] = jnp.zeros((STEPS, 2) + flow.shape[3:], jnp.float32)

    @pl.when(la == n_lat - 1)
    def _():
        for field in (c0, c1):
            field[:, rows + 2:] = jnp.zeros((tracer_count, 2) + field.shape[2:], jnp.float32)
        frac[rows + 1] = jnp.zeros(frac.shape[1:], jnp.float32)
        flow[:, K:, rows + 1] = jnp.zeros((STEPS, 2) + flow.shape[3:], jnp.float32)

    for at_edge, halo in ((lo == 0, left_halo), (lo == n_lon - 1, right_halo)):
        @pl.when(at_edge)
        def _(halo=halo):
            for field in (c0, c1):
                field[:, 2:2 + rows, halo] = jnp.zeros(
                    (tracer_count, rows, PAD, levels), jnp.float32)
            frac[1:1 + rows, halo] = jnp.zeros((rows, PAD, levels), jnp.float32)
            flow[:, U:U + 2, 1:1 + rows, halo] = jnp.zeros(
                (STEPS, 2, rows, PAD, levels), jnp.float32)

    def prepare():
        receive(info_copy, lat_sides)
        for side, r, row in ((SOUTH, rows - 1, 0), (NORTH, 0, rows + 1)):
            @pl.when(sides[opposite[side]][0])
            def _(side=side, r=r, row=row):
                fill_fraction(1 + side, r, row)
        own_field.wait()
        receive(frac_strip, lon_sides)
        receive(functools.partial(strip, 0), lon_sides)

    def faces(s, src, first, count):
        for i in range(count):
            base = pl.multiple_of(TILE * (first + i), TILE)
            p, q = pl.ds(base + PAD - 1, TILE), pl.ds(base + PAD, TILE)
            for r in range(rows):
                terms = face_terms(
                    flow[s, U, r + 1, p], flow[s, U, r + 1, q],
                    flow[s, K, r + 1, p], flow[s, K, r + 1, q], frac[r + 1, p], frac[r + 1, q],
                )
                for a in range(tracer_count):
                    xflux[a, r, pl.ds(base, TILE)] = limited_flux(
                        src[a, r + 2, pl.ds(base + PAD - 2, TILE)], src[a, r + 2, p],
                        src[a, r + 2, q], src[a, r + 2, pl.ds(base + PAD + 1, TILE)], *terms,
                    )

    def cells(s, src, dst, row_shift, shift, first, count):
        for i in range(count):
            base = pl.multiple_of(TILE * (first + i), TILE)
            at = pl.ds(base + PAD, TILE)

            def row_flux(r):
                terms = face_terms(
                    flow[s, V, r, at], flow[s, V, r + 1, at],
                    flow[s, K, r, at], flow[s, K, r + 1, at], frac[r, at], frac[r + 1, at],
                )
                return [
                    limited_flux(
                        src[a, r, at], src[a, r + 1, at], src[a, r + 2, at], src[a, r + 3, at],
                        *terms)
                    for a in range(tracer_count)
                ]

            lower = row_flux(0)
            for r in range(rows):
                upper = row_flux(r + 1)
                rise = flow[s, W, r + 1, at]
                lifted = lid[r, pl.ds(base, TILE)] * rise
                upward = rise >= 0.0
                inverse = share_inverse[r, pl.ds(base, TILE)]
                for a in range(tracer_count):
                    centre = src[a, r + 2, at]
                    vertical = lifted * jnp.where(
                        upward, centre, pltpu.roll(centre, levels - 1, 1)
                    )
                    net = (
                        (upper[a] - lower[a])
                        + (xflux[a, r, pl.ds(base + 1, TILE)] - xflux[a, r, pl.ds(base, TILE)])
                        + (vertical - pltpu.roll(vertical, 1, 1))
                    )
                    dst[a, r + row_shift, pl.ds(base + shift, TILE)] = centre - net * inverse
                lower = upper

    def arrive(item):
        @pl.when(t > 0)
        def _():
            group_copy(item, t - 1, 1, t, 0, 1).wait_recv()

        @pl.when(t < n - 1)
        def _():
            group_copy(item, t + 1, 1, t, 0, 0).wait_recv()

        @pl.when(middle)
        def _():
            group_copy(item, far_row, 1, t, 0, 2).wait_recv()
            relay_copy(item).start()

        @pl.when(ends)
        def _():
            group_copy(item, far_pair, 2, t, 0, 2).wait_recv()

    def after(i):
        s, f, k = order[i]
        if i + LEAD < len(order):
            pl.when(middle)(lambda: send_own(order[i + LEAD]))
        if f == K:
            for side, own in ((NORTH, 0), (SOUTH, n - 1)):
                @pl.when(sides[side][0] & (t != own))
                def _(side=side):
                    flow_rows(s, k, side).start()
        elif k == 0:
            on_sides(functools.partial(flow_strip, s), lon_sides)

    def window(s, k):
        src = (c0, c1)[s]
        if k == 0:
            receive(functools.partial(flow_strip, s), lon_sides)
            if s == 1:
                receive(functools.partial(strip, 1), lon_sides)
        at = first_tile[k]
        low = jnp.where(west, at, at + (1 if k > 0 else 0))
        count = WINDOWS[k] + (1 if k == 0 else 0)
        faces(s, src, low, count)
        receive(functools.partial(start_rows if s == 0 else step_rows, k), lat_sides)
        receive(functools.partial(flow_rows, s, k), lat_sides)
        if s == 0:
            cells(s, src, c1, 2, PAD, at, WINDOWS[k])
            on_sides(functools.partial(step_rows, k), lat_sides)
            if k == 0:
                on_sides(functools.partial(strip, 1), lon_sides)
        else:
            cells(s, src, out_ref, 0, 0, at, WINDOWS[k])

    def finish(s):
        for f in (K, W):
            item = (s, f, 0)

            @pl.when(t < n - 1)
            def _(item=item):
                up_copy(item, wide=True).wait_send()

            @pl.when(t > 0)
            def _(item=item):
                down_copy(item, wide=True).wait_send()

            @pl.when(ends)
            def _(item=item):
                far_copy(item, wide=True).wait_send()

            @pl.when(middle)
            def _(item=item):
                relay_copy(item, wide=True).wait_send()

        on_sides(functools.partial(strip, s), lon_sides, "wait_send")
        on_sides(functools.partial(flow_strip, s), lon_sides, "wait_send")
        for i in lat_sides:
            @pl.when(sides[i][0])
            def _(i=i):
                kv, two = pl.ds(K, 2), pl.ds(0, 2)
                field = (c0, c1)[s].at[:, two, inner]
                side_copy(flow.at[s, kv, 1, inner], flow.at[s, kv, 1, inner],
                          kvs.at[s, i], kvr.at[s, i, 0], i).wait_send()
                side_copy(field, field, (c0s, c1s)[s].at[i], (c0r, c1r)[s].at[i, 0], i).wait_send()
    def finish_start():
        on_sides(frac_strip, lon_sides, "wait_send")
        on_sides(info_copy, lat_sides, "wait_send")

        @pl.when((la == 0) | (la == n_lat - 1))
        def _():
            pltpu.make_async_copy(passing, passing, rbs).wait()

    for i, item in enumerate(order):
        if i == len(order) - SETTLE:
            finish_start()
            finish(0)
        arrive(item)
        after(i)
        pass_all(PASSES.get(i, ()))
        if i == PREPARED:
            prepare()
        if i == LATER:
            pl.when(lo != 0)(early_rows)
        due = [
            {(s, k) for s in range(STEPS) for k in range(PARTS)
             if i == min(order.index((s, W, k)) + lags[s], len(order) - 1)}
            for lags in (END_LAGS, MIDDLE_LAGS)
        ]
        for s, k in sorted(due[0] | due[1]):
            here = [(s, k) in those for those in due]
            if all(here):
                window(s, k)
            else:
                pl.when(ends if here[0] else middle)(functools.partial(window, s, k))

    finish(STEPS - 1)


def fused_body(counts, tracers, land_mask, bottom_level, bottom_part, velocity, upwelling,
               diffusivity):
    tracer_count, rows, cols, levels = tracers.shape
    wide = cols + 2 * PAD
    row = (cols, levels)
    dma = pltpu.SemaphoreType.DMA
    hbm, vmem = pl.BlockSpec(memory_space=pltpu.HBM), pl.BlockSpec(memory_space=pltpu.VMEM)
    return pl.pallas_call(
        functools.partial(transport_kernel, counts),
        out_shape=pltpu.VMEM(tracers.shape, jnp.float32),
        in_specs=[hbm] * 7,
        out_specs=vmem,
        scratch_shapes=[
            pltpu.VMEM((tracer_count, rows + 4, wide + PAD, levels), jnp.float32),
            pltpu.VMEM((tracer_count, rows + 4, wide + PAD, levels), jnp.float32),
            pltpu.VMEM((STEPS, 4, rows + 2, wide, levels), jnp.float32),
            pltpu.VMEM((rows + 2, wide, levels), jnp.float32),
            pltpu.VMEM((tracer_count, rows, cols + 16, levels), jnp.float32),
            pltpu.VMEM((3, 24, 128), jnp.float32),
            pltpu.VMEM((rows, cols), jnp.int32),
            pltpu.VMEM((rows, cols), jnp.int32),
            pltpu.VMEM((rows, cols), jnp.float32),
            dma((STEPS, 4)), dma, dma((3,)),
            dma((STEPS, 2, 3)), dma((STEPS, 2, PARTS, 3)),
            dma((2,)), dma((2, PARTS)), dma((2,)), dma((2, PARTS)),
            dma((STEPS, 2)), dma((STEPS, 2)),
            dma((STEPS, 2)), dma((STEPS, 2, PARTS)),
            dma((STEPS, 2)), dma((STEPS, 2)),
            dma((2,)), dma((2,)), dma((2,)), dma((2,)),
            dma, dma((PARTS,)), pltpu.SemaphoreType.REGULAR((5,)),
            pltpu.VMEM((tracer_count, 2, cols, levels), jnp.float32),
            pltpu.VMEM((rows, cols, levels), jnp.float32),
            pltpu.VMEM((rows, cols, levels), jnp.float32),
        ],
        compiler_params=pltpu.CompilerParams(
            collective_id=0, has_side_effects=True, vmem_limit_bytes=60 * 1024 * 1024
        ),
    )(
        tracers,
        velocity.reshape((STEPS, 2) + row),
        upwelling.reshape((STEPS,) + row),
        diffusivity.reshape((STEPS,) + row),
        land_mask, bottom_level, bottom_part,
    )


def solution(mesh):
    placed = (
        P("trc", "lat", "lon", None),
        P("lat", "lon"),
        P("lat", "lon"),
        P("lat", "lon"),
        P(None, None, ("lat", "lon"), "trc"),
        P(None, ("lat", "lon"), "trc"),
        P(None, ("lat", "lon"), "trc"),
    )
    counts = tuple(mesh.shape[axis] for axis in ("trc", "lat", "lon"))

    def body(*arrays):
        tracers, velocity = arrays[0], arrays[4]
        one_row = velocity.shape[3] == tracers.shape[2] * tracers.shape[3]
        blocks = tracers.shape[1] == 4 and tracers.shape[2] == 64 and tracers.shape[3] == 128
        if counts == (4, 4, 2) and blocks and one_row:
            return fused_body(counts, *arrays)
        return gathered_body(*arrays)

    return jax.shard_map(
        body, mesh=mesh, in_specs=placed, out_specs=P("trc", "lat", "lon", None), check_vma=False
    )
```

```python
import functools

import jax
import jax.numpy as jnp
from jax import lax
from jax.experimental import pallas as pl
from jax.experimental.pallas import tpu as pltpu
from jax.sharding import PartitionSpec as P

STEPS = 2
MESH = pl.DeviceIdType.MESH


fraction_floor = 0.25


def with_halo(block, sides, width):
    for axis, dim in sides:
        count = lax.axis_size(axis)
        forward = [(i, i + 1) for i in range(count - 1)]
        backward = [(target, source) for source, target in forward]
        low = lax.ppermute(
            lax.slice_in_dim(block, block.shape[dim] - width, None, axis=dim), axis, forward
        )
        high = lax.ppermute(lax.slice_in_dim(block, 0, width, axis=dim), axis, backward)
        block = jnp.concatenate([low, block, high], axis=dim)
    return block


def minmod(first, second):
    return 0.5 * (jnp.sign(first) + jnp.sign(second)) * jnp.minimum(jnp.abs(first), jnp.abs(second))


def window(array, start, stop, offset):
    return lax.slice_in_dim(array, start, stop, axis=array.ndim + offset)


def face_divergence(field, speed, mixing, fraction, offset):
    extent = field.shape[field.ndim + offset]
    before = window(field, 0, extent - 3, offset)
    lower = window(field, 1, extent - 2, offset)
    upper = window(field, 2, extent - 1, offset)
    after = window(field, 3, extent, offset)
    face_speed = 0.5 * (window(speed, 1, extent - 2, offset) + window(speed, 2, extent - 1, offset))
    face_area = jnp.minimum(
        window(fraction, 1, extent - 2, offset), window(fraction, 2, extent - 1, offset)
    )
    face_mixing = 0.5 * (
        window(mixing, 1, extent - 2, offset) + window(mixing, 2, extent - 1, offset)
    )
    jump = upper - lower
    damping = 0.5 * (1.0 - jnp.abs(face_speed))
    from_lower = lower + damping * minmod(lower - before, jump)
    from_upper = upper - damping * minmod(jump, after - upper)
    face_value = jnp.where(face_speed >= 0.0, from_lower, from_upper)
    face_flux = face_area * (face_speed * face_value - face_mixing * jump)
    return window(face_flux, 1, extent - 3, offset) - window(face_flux, 0, extent - 4, offset)


def substep(field, fraction, eastward, northward, mixing, rising):
    across_rows = face_divergence(field, northward, mixing, fraction, -3)[..., 2:-2, :]
    across_cols = face_divergence(field, eastward, mixing, fraction, -2)[..., 2:-2, :, :]
    centre = field[..., 2:-2, 2:-2, :]
    wet_share = fraction[2:-2, 2:-2, :]
    top_area = jnp.minimum(wet_share[:, :, :-1], wet_share[:, :, 1:])
    lifting = rising[:, :, :-1]
    carried = jnp.where(lifting >= 0.0, centre[..., :-1], centre[..., 1:])
    vertical = top_area * lifting * carried
    closed = jnp.zeros(vertical.shape[:-1] + (1,), jnp.float32)
    across_levels = jnp.concatenate([vertical, closed], axis=-1) - jnp.concatenate(
        [closed, vertical], axis=-1
    )
    return centre - (across_rows + across_cols + across_levels) / jnp.maximum(
        wet_share, fraction_floor
    )


def cell_fraction(land_mask, bottom_level, bottom_part, levels):
    level_index = lax.broadcasted_iota(jnp.int32, land_mask.shape + (levels,), 2)
    deepest = bottom_level[:, :, None] - 1
    full_cell = (level_index < deepest).astype(jnp.float32)
    last_cell = (level_index == deepest).astype(jnp.float32) * bottom_part[:, :, None]
    return land_mask.astype(jnp.float32)[:, :, None] * (full_cell + last_cell)


def gathered_body(tracers, land_mask, bottom_level, bottom_part, velocity, upwelling, diffusivity):
    levels = tracers.shape[3]
    block_shape = (tracers.shape[1], tracers.shape[2], levels)
    fraction = cell_fraction(land_mask, bottom_level, bottom_part, levels)
    tracer_count = tracers.shape[0]
    moved = (
        lax.all_gather(velocity, "trc", axis=3, tiled=True),
        lax.all_gather(upwelling, "trc", axis=2, tiled=True),
        lax.all_gather(diffusivity, "trc", axis=2, tiled=True),
    )
    speeds = moved[0].reshape((STEPS, 2) + block_shape)
    rises = moved[1].reshape((STEPS,) + block_shape)
    mixes = moved[2].reshape((STEPS,) + block_shape)
    field = tracers
    wide_frac = fraction
    for number in range(STEPS):
        extras = [fraction[None]] if number == 0 else []
        stack = jnp.concatenate(
            [field] + extras + [jnp.stack([speeds[number, 0], speeds[number, 1], mixes[number]])],
            axis=0,
        )
        widened = with_halo(stack, (("lat", 1), ("lon", 2)), 2)
        if number == 0:
            wide_frac = widened[tracer_count]
        flows = widened[-3:]
        field = substep(
            widened[:tracer_count], wide_frac, flows[0], flows[1], flows[2], rises[number]
        )
    return field


W, U, K, V = range(4)
PAD = 8
TILE = 8
SHARES = (2, 2, 2, 2)
PARTS = len(SHARES)
LEAD = 11
INWARD = 13
END_LAGS = (1, 1)
MIDDLE_LAGS = (1, 1)
AHEAD = 2
DIRECT = 3
SETTLE = 2
PREPARED = 3
LATER = -1
PASSES = {0: (0,), 1: (1,), 2: tuple(range(2, PARTS))}
WINDOWS = tuple(share - (k == 0) + (k == PARTS - 1) for k, share in enumerate(SHARES))


def limited_flux(before, lower, upper, after, east, scale, area_speed, area_mix):
    jump = upper - lower
    base = jnp.where(east, lower, upper)
    slope = jnp.where(east, lower - before, after - upper)
    limited = jnp.maximum(jnp.minimum(slope, jump), 0.0) + jnp.minimum(
        jnp.maximum(slope, jump), 0.0
    )
    return area_speed * (base + scale * limited) - area_mix * jump


def face_terms(speed_p, speed_q, mix_p, mix_q, frac_p, frac_q):
    speed = 0.5 * (speed_p + speed_q)
    area = jnp.minimum(frac_p, frac_q)
    east = speed >= 0.0
    damping = 0.5 * (1.0 - jnp.abs(speed))
    return east, jnp.where(east, damping, -damping), area * speed, area * (0.5 * (mix_p + mix_q))


def arrival_order():
    flat = [(s, k) for s in range(STEPS) for k in range(PARTS)]
    order = [(0, K, 0)]
    ahead = 1
    for i, (s, k) in enumerate(flat):
        while ahead < len(flat) and ahead <= i + (AHEAD if flat[ahead][0] else 1):
            order.append((flat[ahead][0], K, flat[ahead][1]))
            ahead += 1
        order.append((s, W, k))
    return order


def transport_kernel(
    counts, tr_hbm, vel_hbm, up_hbm, dif_hbm, mask_hbm, level_hbm, part_hbm, out_ref,
    c0, c1, flow, frac, xflux, info, mask_ref, level_ref, part_ref,
    own_sem, in_sem, column_sem, zs, zr, c0s, c0r, c1s, c1r, ss, sr, kvs, kvr, uks, ukr,
    frs, frr, ifs, ifr, rbs, rbr, ready, passing, share_inverse, lid,
):
    n, n_lat, n_lon = counts
    tracer_count, rows, cols, levels = tr_hbm.shape
    tiles = cols // TILE
    t, la, lo = lax.axis_index("trc"), lax.axis_index("lat"), lax.axis_index("lon")
    west = lo == 0
    inner = pl.ds(PAD, cols)
    body = pl.ds(1, rows)
    left_halo, right_halo = pl.ds(0, PAD), pl.ds(PAD + cols, PAD)
    left_edge, right_edge = pl.ds(PAD, PAD), pl.ds(cols, PAD)
    middle = (t == 1) | (t == n - 2)
    ends = jnp.logical_not(middle)
    far_end = jnp.where(t == 1, 0, n - 1)
    far_row = jnp.where(t == 1, n - 1, 0)
    far_pair = jnp.where(t < 2, 2, 0)

    sides = (
        (la > 0, {"lat": la - 1}),
        (la < n_lat - 1, {"lat": la + 1}),
        (lo > 0, {"lon": lo - 1}),
        (lo < n_lon - 1, {"lon": lo + 1}),
    )
    opposite = (1, 0, 3, 2)
    NORTH, SOUTH, WEST, EAST = range(4)
    later = (sides[SOUTH], sides[EAST], (t < n - 1, {"trc": t + 1}), (t < n - 2, {"trc": t + 2}),
             (la < n_lat - 2, {"lat": la + 2}))
    earlier = (sides[NORTH], sides[WEST], (t > 0, {"trc": t - 1}), (t == 2, {"trc": t - 2}),
               (la == n_lat - 1, {"lat": la - 2}))
    awaited = (la > 0, lo > 0, t > 0, t > 1, la > 1)

    columns = [
        pltpu.make_async_copy(src, dst, column_sem.at[i])
        for i, (src, dst) in enumerate(
            ((mask_hbm, mask_ref), (level_hbm, level_ref), (part_hbm, part_ref)))
    ]
    barrier = pltpu.get_barrier_semaphore()
    for there, device in later:
        @pl.when(there)
        def _(device=device):
            pl.semaphore_signal(barrier, inc=1, device_id=device, device_id_type=MESH)

    def source(s, f):
        return {
            U: lambda: vel_hbm.at[s, 0], V: lambda: vel_hbm.at[s, 1],
            K: lambda: dif_hbm.at[s], W: lambda: up_hbm.at[s],
        }[f]()

    def own_copy(s, f):
        return pltpu.make_async_copy(
            source(s, f), flow.at[s, f, 1 + t, inner], own_sem.at[s, f]
        )

    for f in (K, V, W, U):
        own_copy(0, f).start()
    own_field = pltpu.make_async_copy(tr_hbm, c0.at[:, pl.ds(2, rows), inner], in_sem)

    def part(k, base):
        before, share = sum(SHARES[:k]), SHARES[k]
        at = TILE * jnp.where(west, tiles - before - share, before)
        return pl.ds(pl.multiple_of(base + at, TILE), TILE * share)

    first_tile = [
        jnp.where(west, tiles - sum(WINDOWS[:k + 1]), sum(WINDOWS[:k])) for k in range(PARTS)
    ]

    def window_columns(k):
        return pl.ds(pl.multiple_of(PAD + TILE * first_tile[k], TILE), TILE * WINDOWS[k])

    def group_copy(item, row, count, target, sent, landed, wide=False):
        s, f, k = item
        at = inner if wide else part(k, PAD)
        ref = flow.at[s, pl.ds(f, 2), pl.ds(1 + row, count), at]
        return pltpu.make_async_remote_copy(
            src_ref=ref, dst_ref=ref, send_sem=zs.at[s, f // 2, sent],
            recv_sem=zr.at[s, f // 2, k, landed],
            device_id={"trc": target}, device_id_type=MESH,
        )

    def up_copy(item, **kw):
        return group_copy(item, t, 1, t + 1, 0, 1, **kw)

    def down_copy(item, **kw):
        return group_copy(item, t, 1, t - 1, 1, 0, **kw)

    def far_copy(item, **kw):
        return group_copy(item, t, 1, jnp.where(t == 0, 2, 1), 2, 2, **kw)

    def relay_copy(item, **kw):
        return group_copy(item, far_pair, 2, far_end, 2, 2, **kw)

    def side_copy(src, dst, send, recv, i):
        return pltpu.make_async_remote_copy(
            src_ref=src, dst_ref=dst, send_sem=send, recv_sem=recv,
            device_id=sides[i][1], device_id_type=MESH,
        )

    def start_rows(k, i):
        src = pl.ds(0 if i == NORTH else rows - 2, 2)
        dst = pl.ds(rows + 2 if i == NORTH else 0, 2)
        return side_copy(
            tr_hbm.at[:, src, part(k, 0)], c0.at[:, dst, part(k, PAD)],
            c0s.at[i], c0r.at[i, k], i)

    def detour(k, i):
        src = pl.ds(0 if i == NORTH else rows - 2, 2)
        return pltpu.make_async_remote_copy(
            src_ref=tr_hbm.at[:, src, part(k, 0)], dst_ref=passing.at[:, :, part(k, 0)],
            send_sem=c0s.at[i], recv_sem=rbr.at[k],
            device_id={"lat": 0 if i == NORTH else n_lat - 1}, device_id_type=MESH,
        )

    def pass_on(k, i):
        dst = pl.ds(rows + 2 if i == NORTH else 0, 2)
        return pltpu.make_async_remote_copy(
            src_ref=passing.at[:, :, part(k, 0)], dst_ref=c0.at[:, dst, part(k, PAD)],
            send_sem=rbs, recv_sem=c0r.at[i, k],
            device_id={"lat": 1 if i == NORTH else n_lat - 2}, device_id_type=MESH,
        )

    def pass_all(ks):
        for at, i in ((0, NORTH), (n_lat - 1, SOUTH)):
            @pl.when(la == at)
            def _(i=i):
                for k in ks:
                    detour(k, i).wait_recv()
                    pass_on(k, i).start()

    def step_rows(k, i):
        src = pl.ds(2 if i == NORTH else rows, 2)
        dst = pl.ds(rows + 2 if i == NORTH else 0, 2)
        at = window_columns(k)
        return side_copy(c1.at[:, src, at], c1.at[:, dst, at], c1s.at[i], c1r.at[i, k], i)

    def strip(s, i):
        if s == 0:
            edge = pl.ds(0, PAD) if i == WEST else pl.ds(cols - PAD, PAD)
            src = tr_hbm.at[:, :, edge]
        else:
            src = c1.at[:, pl.ds(2, rows), left_edge if i == WEST else right_edge]
        halo = right_halo if i == WEST else left_halo
        dst = (c0, c1)[s].at[:, pl.ds(2, rows), halo]
        return side_copy(src, dst, ss.at[s, i - 2], sr.at[s, i - 2], i)

    def flow_rows(s, k, i):
        kv = pl.ds(K, 2)
        src, dst = (1, rows + 1) if i == NORTH else (rows, 0)
        at = part(k, PAD)
        return side_copy(flow.at[s, kv, src, at], flow.at[s, kv, dst, at],
                         kvs.at[s, i], kvr.at[s, i, k], i)

    def flow_strip(s, i):
        uk = pl.ds(U, 2)
        src, dst = (left_edge, right_halo) if i == WEST else (right_edge, left_halo)
        return side_copy(flow.at[s, uk, body, src], flow.at[s, uk, body, dst],
                         uks.at[s, i - 2], ukr.at[s, i - 2], i)

    def frac_strip(i):
        src, dst = (left_edge, right_halo) if i == WEST else (right_edge, left_halo)
        return side_copy(frac.at[body, src], frac.at[body, dst], frs.at[i - 2], frr.at[i - 2], i)

    def info_copy(i):
        return side_copy(info.at[0], info.at[1 + i], ifs.at[i], ifr.at[i], i)

    lat_sides, lon_sides = (NORTH, SOUTH), (WEST, EAST)

    def on_sides(make, which, act="start"):
        for i in which:
            @pl.when(sides[i][0])
            def _(i=i):
                getattr(make(i), act)()

    def receive(make, which):
        for i in which:
            @pl.when(sides[opposite[i]][0])
            def _(i=i):
                make(i).wait_recv()

    order = arrival_order()

    total = 0
    for there in awaited:
        total = total + jnp.where(there, 1, 0)
    pl.when(total > 0)(lambda: pl.semaphore_wait(barrier, total))
    for i, (there, device) in enumerate(earlier):
        @pl.when(there)
        def _(i=i, device=device):
            pl.semaphore_signal(ready.at[i], inc=1, device_id=device, device_id_type=MESH)

    def greet(i, there):
        @pl.when(there)
        def _():
            pl.semaphore_wait(ready.at[i], 1)

    def first_copies(item, target, sent, landed):
        s, f, k = item
        for field in (f, f + 1):
            pltpu.make_async_remote_copy(
                src_ref=source(s, field).at[part(k, 0)],
                dst_ref=flow.at[s, field, 1 + t, part(k, PAD)],
                send_sem=zs.at[s, f // 2, sent], recv_sem=zr.at[s, f // 2, k, landed],
                device_id={"trc": target}, device_id_type=MESH,
            ).start()

    @pl.when(t > 0)
    def _():
        for item in order[:DIRECT]:
            @pl.when(t == n - 1)
            def _(item=item):
                first_copies(item, 1, 2, 2)
            first_copies(item, t - 1, 1, 0)

    for f in (K, V, W, U):
        own_copy(1, f).start()
    for copy in columns:
        copy.start()
    own_field.start()
    for s in range(STEPS):
        for f in (K, V, W, U):
            own_copy(s, f).wait()

    @pl.when(t > 0)
    def _():
        for item in order[DIRECT:LEAD]:
            @pl.when(t == n - 1)
            def _(item=item):
                far_copy(item).start()
            down_copy(item).start()

    def outward(make, i):
        for k in range(PARTS):
            make(k, i).start()

    greet(2, t < n - 1)
    greet(3, t == 0)

    @pl.when(t < n - 1)
    def _():
        for item in order[:LEAD]:
            @pl.when(t == 0)
            def _(item=item):
                far_copy(item).start()
            up_copy(item).start()

    @pl.when(t == 2)
    def _():
        for item in order[LEAD:INWARD]:
            down_copy(item).start()

    @pl.when(t == 1)
    def _():
        for item in order[LEAD:INWARD]:
            up_copy(item).start()

    pl.when((la > 0) & (la != 2))(lambda: outward(start_rows, NORTH))
    pl.when(la == 2)(lambda: outward(detour, NORTH))
    greet(4, la == 1)
    pl.when(la == 1)(lambda: outward(detour, SOUTH))
    greet(0, la < n_lat - 1)
    pl.when((la < n_lat - 1) & (la != 1))(lambda: outward(start_rows, SOUTH))
    for side, own in ((NORTH, 0), (SOUTH, n - 1)):
        @pl.when(sides[side][0] & (t == own))
        def _(side=side):
            for k in range(PARTS):
                flow_rows(0, k, side).start()

    def early_rows():
        for side, own in ((NORTH, 0), (SOUTH, n - 1)):
            @pl.when(sides[side][0] & (t == own))
            def _(side=side):
                for k in range(PARTS):
                    flow_rows(1, k, side).start()

    if LATER < 0:
        early_rows()
    else:
        pl.when(lo == 0)(early_rows)

    pl.when(lo > 0)(lambda: strip(0, WEST).start())
    greet(1, lo < n_lon - 1)
    pl.when(lo < n_lon - 1)(lambda: strip(0, EAST).start())

    def send_own(item):
        @pl.when(t > 0)
        def _():
            down_copy(item).start()

        @pl.when(t < n - 1)
        def _():
            up_copy(item).start()

    @pl.when(ends)
    def _():
        for item in order[LEAD:]:
            far_copy(item).start()
            send_own(item)

    square = (cols, cols)
    eye = lax.broadcasted_iota(jnp.int32, square, 0) == lax.broadcasted_iota(jnp.int32, square, 1)
    level = lax.broadcasted_iota(jnp.int32, (cols, levels), 1).astype(jnp.float32)

    def upright(row):
        return jnp.sum(jnp.where(eye, jnp.broadcast_to(row, square), 0.0), axis=1, keepdims=True)

    def fill_fraction(slot, r, row):
        wet, share, deepest = (
            upright(info[slot, 8 * i + r:8 * i + r + 1, 0:cols]) for i in range(3)
        )
        cells_of = jnp.where(level < deepest, wet, jnp.where(level == deepest, share, 0.0))
        frac[row, inner, :] = cells_of
        return cells_of

    for copy in columns:
        copy.wait()
    wet = mask_ref[...].astype(jnp.float32)
    info[0] = jnp.zeros(info.shape[1:], jnp.float32)
    info[0, 0:rows, 0:cols] = wet
    info[0, 8:8 + rows, 0:cols] = wet * part_ref[...]
    info[0, 16:16 + rows, 0:cols] = level_ref[...].astype(jnp.float32) - 1.0
    on_sides(info_copy, lat_sides)
    for r in range(rows):
        share = fill_fraction(0, r, 1 + r)
        share_inverse[r] = 1.0 / jnp.maximum(share, fraction_floor)
        lid[r] = jnp.where(
            level == levels - 1, 0.0, jnp.minimum(share, pltpu.roll(share, levels - 1, 1))
        )
    on_sides(frac_strip, lon_sides)

    @pl.when(la == 0)
    def _():
        for field in (c0, c1):
            field[:, 0:2] = jnp.zeros((tracer_count, 2) + field.shape[2:], jnp.float32)
        frac[0] = jnp.zeros(frac.shape[1:], jnp.float32)
        flow[:, K:, 0] = jnp.zeros((STEPS, 2) + flow.shape[3:], jnp.float32)

    @pl.when(la == n_lat - 1)
    def _():
        for field in (c0, c1):
            field[:, rows + 2:] = jnp.zeros((tracer_count, 2) + field.shape[2:], jnp.float32)
        frac[rows + 1] = jnp.zeros(frac.shape[1:], jnp.float32)
        flow[:, K:, rows + 1] = jnp.zeros((STEPS, 2) + flow.shape[3:], jnp.float32)

    for at_edge, halo in ((lo == 0, left_halo), (lo == n_lon - 1, right_halo)):
        @pl.when(at_edge)
        def _(halo=halo):
            for field in (c0, c1):
                field[:, 2:2 + rows, halo] = jnp.zeros(
                    (tracer_count, rows, PAD, levels), jnp.float32)
            frac[1:1 + rows, halo] = jnp.zeros((rows, PAD, levels), jnp.float32)
            flow[:, U:U + 2, 1:1 + rows, halo] = jnp.zeros(
                (STEPS, 2, rows, PAD, levels), jnp.float32)

    def prepare():
        receive(info_copy, lat_sides)
        for side, r, row in ((SOUTH, rows - 1, 0), (NORTH, 0, rows + 1)):
            @pl.when(sides[opposite[side]][0])
            def _(side=side, r=r, row=row):
                fill_fraction(1 + side, r, row)
        own_field.wait()
        receive(frac_strip, lon_sides)
        receive(functools.partial(strip, 0), lon_sides)

    def faces(s, src, first, count):
        for i in range(count):
            base = pl.multiple_of(TILE * (first + i), TILE)
            p, q = pl.ds(base + PAD - 1, TILE), pl.ds(base + PAD, TILE)
            for r in range(rows):
                terms = face_terms(
                    flow[s, U, r + 1, p], flow[s, U, r + 1, q],
                    flow[s, K, r + 1, p], flow[s, K, r + 1, q], frac[r + 1, p], frac[r + 1, q],
                )
                for a in range(tracer_count):
                    xflux[a, r, pl.ds(base, TILE)] = limited_flux(
                        src[a, r + 2, pl.ds(base + PAD - 2, TILE)], src[a, r + 2, p],
                        src[a, r + 2, q], src[a, r + 2, pl.ds(base + PAD + 1, TILE)], *terms,
                    )

    def cells(s, src, dst, row_shift, shift, first, count):
        for i in range(count):
            base = pl.multiple_of(TILE * (first + i), TILE)
            at = pl.ds(base + PAD, TILE)

            def row_flux(r):
                terms = face_terms(
                    flow[s, V, r, at], flow[s, V, r + 1, at],
                    flow[s, K, r, at], flow[s, K, r + 1, at], frac[r, at], frac[r + 1, at],
                )
                return [
                    limited_flux(
                        src[a, r, at], src[a, r + 1, at], src[a, r + 2, at], src[a, r + 3, at],
                        *terms)
                    for a in range(tracer_count)
                ]

            lower = row_flux(0)
            for r in range(rows):
                upper = row_flux(r + 1)
                rise = flow[s, W, r + 1, at]
                lifted = lid[r, pl.ds(base, TILE)] * rise
                upward = rise >= 0.0
                inverse = share_inverse[r, pl.ds(base, TILE)]
                for a in range(tracer_count):
                    centre = src[a, r + 2, at]
                    vertical = lifted * jnp.where(
                        upward, centre, pltpu.roll(centre, levels - 1, 1)
                    )
                    net = (
                        (upper[a] - lower[a])
                        + (xflux[a, r, pl.ds(base + 1, TILE)] - xflux[a, r, pl.ds(base, TILE)])
                        + (vertical - pltpu.roll(vertical, 1, 1))
                    )
                    dst[a, r + row_shift, pl.ds(base + shift, TILE)] = centre - net * inverse
                lower = upper

    def arrive(item):
        @pl.when(t > 0)
        def _():
            group_copy(item, t - 1, 1, t, 0, 1).wait_recv()

        @pl.when(t < n - 1)
        def _():
            group_copy(item, t + 1, 1, t, 0, 0).wait_recv()

        @pl.when(middle)
        def _():
            group_copy(item, far_row, 1, t, 0, 2).wait_recv()
            relay_copy(item).start()

        @pl.when(ends)
        def _():
            group_copy(item, far_pair, 2, t, 0, 2).wait_recv()

    def after(i):
        s, f, k = order[i]
        if i + LEAD < len(order):
            late = order[i + LEAD]
            pl.when(t == 1)(lambda: down_copy(late).start())
            pl.when(t == 2)(lambda: up_copy(late).start())
            if i + LEAD >= INWARD:
                pl.when(t == 2)(lambda: down_copy(late).start())
                pl.when(t == 1)(lambda: up_copy(late).start())
        if f == K:
            for side, own in ((NORTH, 0), (SOUTH, n - 1)):
                @pl.when(sides[side][0] & (t != own))
                def _(side=side):
                    flow_rows(s, k, side).start()
        elif k == 0:
            on_sides(functools.partial(flow_strip, s), lon_sides)

    def window(s, k):
        src = (c0, c1)[s]
        if k == 0:
            receive(functools.partial(flow_strip, s), lon_sides)
            if s == 1:
                receive(functools.partial(strip, 1), lon_sides)
        at = first_tile[k]
        low = jnp.where(west, at, at + (1 if k > 0 else 0))
        count = WINDOWS[k] + (1 if k == 0 else 0)
        faces(s, src, low, count)
        receive(functools.partial(start_rows if s == 0 else step_rows, k), lat_sides)
        receive(functools.partial(flow_rows, s, k), lat_sides)
        if s == 0:
            cells(s, src, c1, 2, PAD, at, WINDOWS[k])
            on_sides(functools.partial(step_rows, k), lat_sides)
            if k == 0:
                on_sides(functools.partial(strip, 1), lon_sides)
        else:
            cells(s, src, out_ref, 0, 0, at, WINDOWS[k])

    def finish(s):
        for f in (K, W):
            item = (s, f, 0)

            @pl.when(t < n - 1)
            def _(item=item):
                up_copy(item, wide=True).wait_send()

            @pl.when(t > 0)
            def _(item=item):
                down_copy(item, wide=True).wait_send()

            @pl.when(ends)
            def _(item=item):
                far_copy(item, wide=True).wait_send()

            @pl.when(middle)
            def _(item=item):
                relay_copy(item, wide=True).wait_send()

        on_sides(functools.partial(strip, s), lon_sides, "wait_send")
        on_sides(functools.partial(flow_strip, s), lon_sides, "wait_send")
        for i in lat_sides:
            @pl.when(sides[i][0])
            def _(i=i):
                kv, two = pl.ds(K, 2), pl.ds(0, 2)
                field = (c0, c1)[s].at[:, two, inner]
                side_copy(flow.at[s, kv, 1, inner], flow.at[s, kv, 1, inner],
                          kvs.at[s, i], kvr.at[s, i, 0], i).wait_send()
                side_copy(field, field, (c0s, c1s)[s].at[i], (c0r, c1r)[s].at[i, 0], i).wait_send()
    def finish_start():
        on_sides(frac_strip, lon_sides, "wait_send")
        on_sides(info_copy, lat_sides, "wait_send")

        @pl.when((la == 0) | (la == n_lat - 1))
        def _():
            pltpu.make_async_copy(passing, passing, rbs).wait()

    for i, item in enumerate(order):
        if i == len(order) - SETTLE:
            finish_start()
            finish(0)
        arrive(item)
        after(i)
        pass_all(PASSES.get(i, ()))
        if i == PREPARED:
            prepare()
        if i == LATER:
            pl.when(lo != 0)(early_rows)
        due = [
            {(s, k) for s in range(STEPS) for k in range(PARTS)
             if i == min(order.index((s, W, k)) + lags[s], len(order) - 1)}
            for lags in (END_LAGS, MIDDLE_LAGS)
        ]
        for s, k in sorted(due[0] | due[1]):
            here = [(s, k) in those for those in due]
            if all(here):
                window(s, k)
            else:
                pl.when(ends if here[0] else middle)(functools.partial(window, s, k))

    finish(STEPS - 1)


def fused_body(counts, tracers, land_mask, bottom_level, bottom_part, velocity, upwelling,
               diffusivity):
    tracer_count, rows, cols, levels = tracers.shape
    wide = cols + 2 * PAD
    row = (cols, levels)
    dma = pltpu.SemaphoreType.DMA
    hbm, vmem = pl.BlockSpec(memory_space=pltpu.HBM), pl.BlockSpec(memory_space=pltpu.VMEM)
    return pl.pallas_call(
        functools.partial(transport_kernel, counts),
        out_shape=pltpu.VMEM(tracers.shape, jnp.float32),
        in_specs=[hbm] * 7,
        out_specs=vmem,
        scratch_shapes=[
            pltpu.VMEM((tracer_count, rows + 4, wide + PAD, levels), jnp.float32),
            pltpu.VMEM((tracer_count, rows + 4, wide + PAD, levels), jnp.float32),
            pltpu.VMEM((STEPS, 4, rows + 2, wide, levels), jnp.float32),
            pltpu.VMEM((rows + 2, wide, levels), jnp.float32),
            pltpu.VMEM((tracer_count, rows, cols + 16, levels), jnp.float32),
            pltpu.VMEM((3, 24, 128), jnp.float32),
            pltpu.VMEM((rows, cols), jnp.int32),
            pltpu.VMEM((rows, cols), jnp.int32),
            pltpu.VMEM((rows, cols), jnp.float32),
            dma((STEPS, 4)), dma, dma((3,)),
            dma((STEPS, 2, 3)), dma((STEPS, 2, PARTS, 3)),
            dma((2,)), dma((2, PARTS)), dma((2,)), dma((2, PARTS)),
            dma((STEPS, 2)), dma((STEPS, 2)),
            dma((STEPS, 2)), dma((STEPS, 2, PARTS)),
            dma((STEPS, 2)), dma((STEPS, 2)),
            dma((2,)), dma((2,)), dma((2,)), dma((2,)),
            dma, dma((PARTS,)), pltpu.SemaphoreType.REGULAR((5,)),
            pltpu.VMEM((tracer_count, 2, cols, levels), jnp.float32),
            pltpu.VMEM((rows, cols, levels), jnp.float32),
            pltpu.VMEM((rows, cols, levels), jnp.float32),
        ],
        compiler_params=pltpu.CompilerParams(
            collective_id=0, has_side_effects=True, vmem_limit_bytes=60 * 1024 * 1024
        ),
    )(
        tracers,
        velocity.reshape((STEPS, 2) + row),
        upwelling.reshape((STEPS,) + row),
        diffusivity.reshape((STEPS,) + row),
        land_mask, bottom_level, bottom_part,
    )


def solution(mesh):
    placed = (
        P("trc", "lat", "lon", None),
        P("lat", "lon"),
        P("lat", "lon"),
        P("lat", "lon"),
        P(None, None, ("lat", "lon"), "trc"),
        P(None, ("lat", "lon"), "trc"),
        P(None, ("lat", "lon"), "trc"),
    )
    counts = tuple(mesh.shape[axis] for axis in ("trc", "lat", "lon"))

    def body(*arrays):
        tracers, velocity = arrays[0], arrays[4]
        one_row = velocity.shape[3] == tracers.shape[2] * tracers.shape[3]
        blocks = tracers.shape[1] == 4 and tracers.shape[2] == 64 and tracers.shape[3] == 128
        if counts == (4, 4, 2) and blocks and one_row:
            return fused_body(counts, *arrays)
        return gathered_body(*arrays)

    return jax.shard_map(
        body, mesh=mesh, in_specs=placed, out_specs=P("trc", "lat", "lon", None), check_vma=False
    )
```

```python
import functools

import jax
import jax.numpy as jnp
from jax import lax
from jax.experimental import pallas as pl
from jax.experimental.pallas import tpu as pltpu
from jax.sharding import PartitionSpec as P

STEPS = 2
MESH = pl.DeviceIdType.MESH


fraction_floor = 0.25


def with_halo(block, sides, width):
    for axis, dim in sides:
        count = lax.axis_size(axis)
        forward = [(i, i + 1) for i in range(count - 1)]
        backward = [(target, source) for source, target in forward]
        low = lax.ppermute(
            lax.slice_in_dim(block, block.shape[dim] - width, None, axis=dim), axis, forward
        )
        high = lax.ppermute(lax.slice_in_dim(block, 0, width, axis=dim), axis, backward)
        block = jnp.concatenate([low, block, high], axis=dim)
    return block


def minmod(first, second):
    return 0.5 * (jnp.sign(first) + jnp.sign(second)) * jnp.minimum(jnp.abs(first), jnp.abs(second))


def window(array, start, stop, offset):
    return lax.slice_in_dim(array, start, stop, axis=array.ndim + offset)


def face_divergence(field, speed, mixing, fraction, offset):
    extent = field.shape[field.ndim + offset]
    before = window(field, 0, extent - 3, offset)
    lower = window(field, 1, extent - 2, offset)
    upper = window(field, 2, extent - 1, offset)
    after = window(field, 3, extent, offset)
    face_speed = 0.5 * (window(speed, 1, extent - 2, offset) + window(speed, 2, extent - 1, offset))
    face_area = jnp.minimum(
        window(fraction, 1, extent - 2, offset), window(fraction, 2, extent - 1, offset)
    )
    face_mixing = 0.5 * (
        window(mixing, 1, extent - 2, offset) + window(mixing, 2, extent - 1, offset)
    )
    jump = upper - lower
    damping = 0.5 * (1.0 - jnp.abs(face_speed))
    from_lower = lower + damping * minmod(lower - before, jump)
    from_upper = upper - damping * minmod(jump, after - upper)
    face_value = jnp.where(face_speed >= 0.0, from_lower, from_upper)
    face_flux = face_area * (face_speed * face_value - face_mixing * jump)
    return window(face_flux, 1, extent - 3, offset) - window(face_flux, 0, extent - 4, offset)


def substep(field, fraction, eastward, northward, mixing, rising):
    across_rows = face_divergence(field, northward, mixing, fraction, -3)[..., 2:-2, :]
    across_cols = face_divergence(field, eastward, mixing, fraction, -2)[..., 2:-2, :, :]
    centre = field[..., 2:-2, 2:-2, :]
    wet_share = fraction[2:-2, 2:-2, :]
    top_area = jnp.minimum(wet_share[:, :, :-1], wet_share[:, :, 1:])
    lifting = rising[:, :, :-1]
    carried = jnp.where(lifting >= 0.0, centre[..., :-1], centre[..., 1:])
    vertical = top_area * lifting * carried
    closed = jnp.zeros(vertical.shape[:-1] + (1,), jnp.float32)
    across_levels = jnp.concatenate([vertical, closed], axis=-1) - jnp.concatenate(
        [closed, vertical], axis=-1
    )
    return centre - (across_rows + across_cols + across_levels) / jnp.maximum(
        wet_share, fraction_floor
    )


def cell_fraction(land_mask, bottom_level, bottom_part, levels):
    level_index = lax.broadcasted_iota(jnp.int32, land_mask.shape + (levels,), 2)
    deepest = bottom_level[:, :, None] - 1
    full_cell = (level_index < deepest).astype(jnp.float32)
    last_cell = (level_index == deepest).astype(jnp.float32) * bottom_part[:, :, None]
    return land_mask.astype(jnp.float32)[:, :, None] * (full_cell + last_cell)


def gathered_body(tracers, land_mask, bottom_level, bottom_part, velocity, upwelling, diffusivity):
    levels = tracers.shape[3]
    block_shape = (tracers.shape[1], tracers.shape[2], levels)
    fraction = cell_fraction(land_mask, bottom_level, bottom_part, levels)
    tracer_count = tracers.shape[0]
    moved = (
        lax.all_gather(velocity, "trc", axis=3, tiled=True),
        lax.all_gather(upwelling, "trc", axis=2, tiled=True),
        lax.all_gather(diffusivity, "trc", axis=2, tiled=True),
    )
    speeds = moved[0].reshape((STEPS, 2) + block_shape)
    rises = moved[1].reshape((STEPS,) + block_shape)
    mixes = moved[2].reshape((STEPS,) + block_shape)
    field = tracers
    wide_frac = fraction
    for number in range(STEPS):
        extras = [fraction[None]] if number == 0 else []
        stack = jnp.concatenate(
            [field] + extras + [jnp.stack([speeds[number, 0], speeds[number, 1], mixes[number]])],
            axis=0,
        )
        widened = with_halo(stack, (("lat", 1), ("lon", 2)), 2)
        if number == 0:
            wide_frac = widened[tracer_count]
        flows = widened[-3:]
        field = substep(
            widened[:tracer_count], wide_frac, flows[0], flows[1], flows[2], rises[number]
        )
    return field


W, U, K, V = range(4)
PAD = 8
TILE = 8
SHARES = (2, 2, 2, 2)
PARTS = len(SHARES)
LEAD = 11
INWARD = 13
END_LAGS = (1, 1)
MIDDLE_LAGS = (1, 2)
AHEAD = 2
DIRECT = 3
SETTLE = 2
PREPARED = 3
LATER = -1
PASSES = {0: (0,), 1: (1,), 2: tuple(range(2, PARTS))}
WINDOWS = tuple(share - (k == 0) + (k == PARTS - 1) for k, share in enumerate(SHARES))


def limited_flux(before, lower, upper, after, east, scale, area_speed, area_mix):
    jump = upper - lower
    base = jnp.where(east, lower, upper)
    slope = jnp.where(east, lower - before, after - upper)
    limited = jnp.maximum(jnp.minimum(slope, jump), 0.0) + jnp.minimum(
        jnp.maximum(slope, jump), 0.0
    )
    return area_speed * (base + scale * limited) - area_mix * jump


def face_terms(speed_p, speed_q, mix_p, mix_q, frac_p, frac_q):
    speed = 0.5 * (speed_p + speed_q)
    area = jnp.minimum(frac_p, frac_q)
    east = speed >= 0.0
    damping = 0.5 * (1.0 - jnp.abs(speed))
    return east, jnp.where(east, damping, -damping), area * speed, area * (0.5 * (mix_p + mix_q))


def arrival_order():
    flat = [(s, k) for s in range(STEPS) for k in range(PARTS)]
    order = [(0, K, 0)]
    ahead = 1
    for i, (s, k) in enumerate(flat):
        while ahead < len(flat) and ahead <= i + (AHEAD if flat[ahead][0] else 1):
            order.append((flat[ahead][0], K, flat[ahead][1]))
            ahead += 1
        order.append((s, W, k))
    return order


def transport_kernel(
    counts, tr_hbm, vel_hbm, up_hbm, dif_hbm, mask_hbm, level_hbm, part_hbm, out_ref,
    c0, c1, flow, frac, xflux, info, mask_ref, level_ref, part_ref,
    own_sem, in_sem, column_sem, zs, zr, c0s, c0r, c1s, c1r, ss, sr, kvs, kvr, uks, ukr,
    frs, frr, ifs, ifr, rbs, rbr, ready, passing, share_inverse, lid,
):
    n, n_lat, n_lon = counts
    tracer_count, rows, cols, levels = tr_hbm.shape
    tiles = cols // TILE
    t, la, lo = lax.axis_index("trc"), lax.axis_index("lat"), lax.axis_index("lon")
    west = lo == 0
    inner = pl.ds(PAD, cols)
    body = pl.ds(1, rows)
    left_halo, right_halo = pl.ds(0, PAD), pl.ds(PAD + cols, PAD)
    left_edge, right_edge = pl.ds(PAD, PAD), pl.ds(cols, PAD)
    middle = (t == 1) | (t == n - 2)
    ends = jnp.logical_not(middle)
    far_end = jnp.where(t == 1, 0, n - 1)
    far_row = jnp.where(t == 1, n - 1, 0)
    far_pair = jnp.where(t < 2, 2, 0)

    sides = (
        (la > 0, {"lat": la - 1}),
        (la < n_lat - 1, {"lat": la + 1}),
        (lo > 0, {"lon": lo - 1}),
        (lo < n_lon - 1, {"lon": lo + 1}),
    )
    opposite = (1, 0, 3, 2)
    NORTH, SOUTH, WEST, EAST = range(4)
    later = (sides[SOUTH], sides[EAST], (t < n - 1, {"trc": t + 1}), (t < n - 2, {"trc": t + 2}),
             (la < n_lat - 2, {"lat": la + 2}))
    earlier = (sides[NORTH], sides[WEST], (t > 0, {"trc": t - 1}), (t == 2, {"trc": t - 2}),
               (la == n_lat - 1, {"lat": la - 2}))
    awaited = (la > 0, lo > 0, t > 0, t > 1, la > 1)

    columns = [
        pltpu.make_async_copy(src, dst, column_sem.at[i])
        for i, (src, dst) in enumerate(
            ((mask_hbm, mask_ref), (level_hbm, level_ref), (part_hbm, part_ref)))
    ]
    barrier = pltpu.get_barrier_semaphore()
    for there, device in later:
        @pl.when(there)
        def _(device=device):
            pl.semaphore_signal(barrier, inc=1, device_id=device, device_id_type=MESH)

    def source(s, f):
        return {
            U: lambda: vel_hbm.at[s, 0], V: lambda: vel_hbm.at[s, 1],
            K: lambda: dif_hbm.at[s], W: lambda: up_hbm.at[s],
        }[f]()

    def own_copy(s, f):
        return pltpu.make_async_copy(
            source(s, f), flow.at[s, f, 1 + t, inner], own_sem.at[s, f]
        )

    for f in (K, V, W, U):
        own_copy(0, f).start()
    own_field = pltpu.make_async_copy(tr_hbm, c0.at[:, pl.ds(2, rows), inner], in_sem)

    def part(k, base):
        before, share = sum(SHARES[:k]), SHARES[k]
        at = TILE * jnp.where(west, tiles - before - share, before)
        return pl.ds(pl.multiple_of(base + at, TILE), TILE * share)

    first_tile = [
        jnp.where(west, tiles - sum(WINDOWS[:k + 1]), sum(WINDOWS[:k])) for k in range(PARTS)
    ]

    def window_columns(k):
        return pl.ds(pl.multiple_of(PAD + TILE * first_tile[k], TILE), TILE * WINDOWS[k])

    def group_copy(item, row, count, target, sent, landed, wide=False):
        s, f, k = item
        at = inner if wide else part(k, PAD)
        ref = flow.at[s, pl.ds(f, 2), pl.ds(1 + row, count), at]
        return pltpu.make_async_remote_copy(
            src_ref=ref, dst_ref=ref, send_sem=zs.at[s, f // 2, sent],
            recv_sem=zr.at[s, f // 2, k, landed],
            device_id={"trc": target}, device_id_type=MESH,
        )

    def up_copy(item, **kw):
        return group_copy(item, t, 1, t + 1, 0, 1, **kw)

    def down_copy(item, **kw):
        return group_copy(item, t, 1, t - 1, 1, 0, **kw)

    def far_copy(item, **kw):
        return group_copy(item, t, 1, jnp.where(t == 0, 2, 1), 2, 2, **kw)

    def relay_copy(item, **kw):
        return group_copy(item, far_pair, 2, far_end, 2, 2, **kw)

    def side_copy(src, dst, send, recv, i):
        return pltpu.make_async_remote_copy(
            src_ref=src, dst_ref=dst, send_sem=send, recv_sem=recv,
            device_id=sides[i][1], device_id_type=MESH,
        )

    def start_rows(k, i):
        src = pl.ds(0 if i == NORTH else rows - 2, 2)
        dst = pl.ds(rows + 2 if i == NORTH else 0, 2)
        return side_copy(
            tr_hbm.at[:, src, part(k, 0)], c0.at[:, dst, part(k, PAD)],
            c0s.at[i], c0r.at[i, k], i)

    def detour(k, i):
        src = pl.ds(0 if i == NORTH else rows - 2, 2)
        return pltpu.make_async_remote_copy(
            src_ref=tr_hbm.at[:, src, part(k, 0)], dst_ref=passing.at[:, :, part(k, 0)],
            send_sem=c0s.at[i], recv_sem=rbr.at[k],
            device_id={"lat": 0 if i == NORTH else n_lat - 1}, device_id_type=MESH,
        )

    def pass_on(k, i):
        dst = pl.ds(rows + 2 if i == NORTH else 0, 2)
        return pltpu.make_async_remote_copy(
            src_ref=passing.at[:, :, part(k, 0)], dst_ref=c0.at[:, dst, part(k, PAD)],
            send_sem=rbs, recv_sem=c0r.at[i, k],
            device_id={"lat": 1 if i == NORTH else n_lat - 2}, device_id_type=MESH,
        )

    def pass_all(ks):
        for at, i in ((0, NORTH), (n_lat - 1, SOUTH)):
            @pl.when(la == at)
            def _(i=i):
                for k in ks:
                    detour(k, i).wait_recv()
                    pass_on(k, i).start()

    def step_rows(k, i):
        src = pl.ds(2 if i == NORTH else rows, 2)
        dst = pl.ds(rows + 2 if i == NORTH else 0, 2)
        at = window_columns(k)
        return side_copy(c1.at[:, src, at], c1.at[:, dst, at], c1s.at[i], c1r.at[i, k], i)

    def strip(s, i):
        if s == 0:
            edge = pl.ds(0, PAD) if i == WEST else pl.ds(cols - PAD, PAD)
            src = tr_hbm.at[:, :, edge]
        else:
            src = c1.at[:, pl.ds(2, rows), left_edge if i == WEST else right_edge]
        halo = right_halo if i == WEST else left_halo
        dst = (c0, c1)[s].at[:, pl.ds(2, rows), halo]
        return side_copy(src, dst, ss.at[s, i - 2], sr.at[s, i - 2], i)

    def flow_rows(s, k, i):
        kv = pl.ds(K, 2)
        src, dst = (1, rows + 1) if i == NORTH else (rows, 0)
        at = part(k, PAD)
        return side_copy(flow.at[s, kv, src, at], flow.at[s, kv, dst, at],
                         kvs.at[s, i], kvr.at[s, i, k], i)

    def flow_strip(s, i):
        uk = pl.ds(U, 2)
        src, dst = (left_edge, right_halo) if i == WEST else (right_edge, left_halo)
        return side_copy(flow.at[s, uk, body, src], flow.at[s, uk, body, dst],
                         uks.at[s, i - 2], ukr.at[s, i - 2], i)

    def frac_strip(i):
        src, dst = (left_edge, right_halo) if i == WEST else (right_edge, left_halo)
        return side_copy(frac.at[body, src], frac.at[body, dst], frs.at[i - 2], frr.at[i - 2], i)

    def info_copy(i):
        return side_copy(info.at[0], info.at[1 + i], ifs.at[i], ifr.at[i], i)

    lat_sides, lon_sides = (NORTH, SOUTH), (WEST, EAST)

    def on_sides(make, which, act="start"):
        for i in which:
            @pl.when(sides[i][0])
            def _(i=i):
                getattr(make(i), act)()

    def receive(make, which):
        for i in which:
            @pl.when(sides[opposite[i]][0])
            def _(i=i):
                make(i).wait_recv()

    order = arrival_order()

    total = 0
    for there in awaited:
        total = total + jnp.where(there, 1, 0)
    pl.when(total > 0)(lambda: pl.semaphore_wait(barrier, total))
    for i, (there, device) in enumerate(earlier):
        @pl.when(there)
        def _(i=i, device=device):
            pl.semaphore_signal(ready.at[i], inc=1, device_id=device, device_id_type=MESH)

    def greet(i, there):
        @pl.when(there)
        def _():
            pl.semaphore_wait(ready.at[i], 1)

    def first_copies(item, target, sent, landed):
        s, f, k = item
        for field in (f, f + 1):
            pltpu.make_async_remote_copy(
                src_ref=source(s, field).at[part(k, 0)],
                dst_ref=flow.at[s, field, 1 + t, part(k, PAD)],
                send_sem=zs.at[s, f // 2, sent], recv_sem=zr.at[s, f // 2, k, landed],
                device_id={"trc": target}, device_id_type=MESH,
            ).start()

    @pl.when(t > 0)
    def _():
        for item in order[:DIRECT]:
            @pl.when(t == n - 1)
            def _(item=item):
                first_copies(item, 1, 2, 2)
            first_copies(item, t - 1, 1, 0)

    for f in (K, V, W, U):
        own_copy(1, f).start()
    for copy in columns:
        copy.start()
    own_field.start()
    for s in range(STEPS):
        for f in (K, V, W, U):
            own_copy(s, f).wait()

    @pl.when(t > 0)
    def _():
        for item in order[DIRECT:LEAD]:
            @pl.when(t == n - 1)
            def _(item=item):
                far_copy(item).start()
            down_copy(item).start()

    def outward(make, i):
        for k in range(PARTS):
            make(k, i).start()

    greet(2, t < n - 1)
    greet(3, t == 0)

    @pl.when(t < n - 1)
    def _():
        for item in order[:LEAD]:
            @pl.when(t == 0)
            def _(item=item):
                far_copy(item).start()
            up_copy(item).start()

    @pl.when(t == 2)
    def _():
        for item in order[LEAD:INWARD]:
            down_copy(item).start()

    @pl.when(t == 1)
    def _():
        for item in order[LEAD:INWARD]:
            up_copy(item).start()

    pl.when((la > 0) & (la != 2))(lambda: outward(start_rows, NORTH))
    pl.when(la == 2)(lambda: outward(detour, NORTH))
    greet(4, la == 1)
    pl.when(la == 1)(lambda: outward(detour, SOUTH))
    greet(0, la < n_lat - 1)
    pl.when((la < n_lat - 1) & (la != 1))(lambda: outward(start_rows, SOUTH))
    for side, own in ((NORTH, 0), (SOUTH, n - 1)):
        @pl.when(sides[side][0] & (t == own))
        def _(side=side):
            for k in range(PARTS):
                flow_rows(0, k, side).start()

    def early_rows():
        for side, own in ((NORTH, 0), (SOUTH, n - 1)):
            @pl.when(sides[side][0] & (t == own))
            def _(side=side):
                for k in range(PARTS):
                    flow_rows(1, k, side).start()

    if LATER < 0:
        early_rows()
    else:
        pl.when(lo == 0)(early_rows)

    pl.when(lo > 0)(lambda: strip(0, WEST).start())
    greet(1, lo < n_lon - 1)
    pl.when(lo < n_lon - 1)(lambda: strip(0, EAST).start())

    def send_own(item):
        @pl.when(t > 0)
        def _():
            down_copy(item).start()

        @pl.when(t < n - 1)
        def _():
            up_copy(item).start()

    @pl.when(ends)
    def _():
        for item in order[LEAD:]:
            far_copy(item).start()
            send_own(item)

    square = (cols, cols)
    eye = lax.broadcasted_iota(jnp.int32, square, 0) == lax.broadcasted_iota(jnp.int32, square, 1)
    level = lax.broadcasted_iota(jnp.int32, (cols, levels), 1).astype(jnp.float32)

    def upright(row):
        return jnp.sum(jnp.where(eye, jnp.broadcast_to(row, square), 0.0), axis=1, keepdims=True)

    def fill_fraction(slot, r, row):
        wet, share, deepest = (
            upright(info[slot, 8 * i + r:8 * i + r + 1, 0:cols]) for i in range(3)
        )
        cells_of = jnp.where(level < deepest, wet, jnp.where(level == deepest, share, 0.0))
        frac[row, inner, :] = cells_of
        return cells_of

    for copy in columns:
        copy.wait()
    wet = mask_ref[...].astype(jnp.float32)
    info[0] = jnp.zeros(info.shape[1:], jnp.float32)
    info[0, 0:rows, 0:cols] = wet
    info[0, 8:8 + rows, 0:cols] = wet * part_ref[...]
    info[0, 16:16 + rows, 0:cols] = level_ref[...].astype(jnp.float32) - 1.0
    on_sides(info_copy, lat_sides)
    for r in range(rows):
        share = fill_fraction(0, r, 1 + r)
        share_inverse[r] = 1.0 / jnp.maximum(share, fraction_floor)
        lid[r] = jnp.where(
            level == levels - 1, 0.0, jnp.minimum(share, pltpu.roll(share, levels - 1, 1))
        )
    on_sides(frac_strip, lon_sides)

    @pl.when(la == 0)
    def _():
        for field in (c0, c1):
            field[:, 0:2] = jnp.zeros((tracer_count, 2) + field.shape[2:], jnp.float32)
        frac[0] = jnp.zeros(frac.shape[1:], jnp.float32)
        flow[:, K:, 0] = jnp.zeros((STEPS, 2) + flow.shape[3:], jnp.float32)

    @pl.when(la == n_lat - 1)
    def _():
        for field in (c0, c1):
            field[:, rows + 2:] = jnp.zeros((tracer_count, 2) + field.shape[2:], jnp.float32)
        frac[rows + 1] = jnp.zeros(frac.shape[1:], jnp.float32)
        flow[:, K:, rows + 1] = jnp.zeros((STEPS, 2) + flow.shape[3:], jnp.float32)

    for at_edge, halo in ((lo == 0, left_halo), (lo == n_lon - 1, right_halo)):
        @pl.when(at_edge)
        def _(halo=halo):
            for field in (c0, c1):
                field[:, 2:2 + rows, halo] = jnp.zeros(
                    (tracer_count, rows, PAD, levels), jnp.float32)
            frac[1:1 + rows, halo] = jnp.zeros((rows, PAD, levels), jnp.float32)
            flow[:, U:U + 2, 1:1 + rows, halo] = jnp.zeros(
                (STEPS, 2, rows, PAD, levels), jnp.float32)

    def prepare():
        receive(info_copy, lat_sides)
        for side, r, row in ((SOUTH, rows - 1, 0), (NORTH, 0, rows + 1)):
            @pl.when(sides[opposite[side]][0])
            def _(side=side, r=r, row=row):
                fill_fraction(1 + side, r, row)
        own_field.wait()
        receive(frac_strip, lon_sides)
        receive(functools.partial(strip, 0), lon_sides)

    def faces(s, src, first, count):
        for i in range(count):
            base = pl.multiple_of(TILE * (first + i), TILE)
            p, q = pl.ds(base + PAD - 1, TILE), pl.ds(base + PAD, TILE)
            for r in range(rows):
                terms = face_terms(
                    flow[s, U, r + 1, p], flow[s, U, r + 1, q],
                    flow[s, K, r + 1, p], flow[s, K, r + 1, q], frac[r + 1, p], frac[r + 1, q],
                )
                for a in range(tracer_count):
                    xflux[a, r, pl.ds(base, TILE)] = limited_flux(
                        src[a, r + 2, pl.ds(base + PAD - 2, TILE)], src[a, r + 2, p],
                        src[a, r + 2, q], src[a, r + 2, pl.ds(base + PAD + 1, TILE)], *terms,
                    )

    def cells(s, src, dst, row_shift, shift, first, count):
        for i in range(count):
            base = pl.multiple_of(TILE * (first + i), TILE)
            at = pl.ds(base + PAD, TILE)

            def row_flux(r):
                terms = face_terms(
                    flow[s, V, r, at], flow[s, V, r + 1, at],
                    flow[s, K, r, at], flow[s, K, r + 1, at], frac[r, at], frac[r + 1, at],
                )
                return [
                    limited_flux(
                        src[a, r, at], src[a, r + 1, at], src[a, r + 2, at], src[a, r + 3, at],
                        *terms)
                    for a in range(tracer_count)
                ]

            lower = row_flux(0)
            for r in range(rows):
                upper = row_flux(r + 1)
                rise = flow[s, W, r + 1, at]
                lifted = lid[r, pl.ds(base, TILE)] * rise
                upward = rise >= 0.0
                inverse = share_inverse[r, pl.ds(base, TILE)]
                for a in range(tracer_count):
                    centre = src[a, r + 2, at]
                    vertical = lifted * jnp.where(
                        upward, centre, pltpu.roll(centre, levels - 1, 1)
                    )
                    net = (
                        (upper[a] - lower[a])
                        + (xflux[a, r, pl.ds(base + 1, TILE)] - xflux[a, r, pl.ds(base, TILE)])
                        + (vertical - pltpu.roll(vertical, 1, 1))
                    )
                    dst[a, r + row_shift, pl.ds(base + shift, TILE)] = centre - net * inverse
                lower = upper

    def arrive(item):
        @pl.when(t > 0)
        def _():
            group_copy(item, t - 1, 1, t, 0, 1).wait_recv()

        @pl.when(t < n - 1)
        def _():
            group_copy(item, t + 1, 1, t, 0, 0).wait_recv()

        @pl.when(middle)
        def _():
            group_copy(item, far_row, 1, t, 0, 2).wait_recv()
            relay_copy(item).start()

        @pl.when(ends)
        def _():
            group_copy(item, far_pair, 2, t, 0, 2).wait_recv()

    def after(i):
        s, f, k = order[i]
        if i + LEAD < len(order):
            late = order[i + LEAD]
            pl.when(t == 1)(lambda: down_copy(late).start())
            pl.when(t == 2)(lambda: up_copy(late).start())
            if i + LEAD >= INWARD:
                pl.when(t == 2)(lambda: down_copy(late).start())
                pl.when(t == 1)(lambda: up_copy(late).start())
        if f == K:
            for side, own in ((NORTH, 0), (SOUTH, n - 1)):
                @pl.when(sides[side][0] & (t != own))
                def _(side=side):
                    flow_rows(s, k, side).start()
        elif k == 0:
            on_sides(functools.partial(flow_strip, s), lon_sides)

    def window(s, k):
        src = (c0, c1)[s]
        if k == 0:
            receive(functools.partial(flow_strip, s), lon_sides)
            if s == 1:
                receive(functools.partial(strip, 1), lon_sides)
        at = first_tile[k]
        low = jnp.where(west, at, at + (1 if k > 0 else 0))
        count = WINDOWS[k] + (1 if k == 0 else 0)
        faces(s, src, low, count)
        receive(functools.partial(start_rows if s == 0 else step_rows, k), lat_sides)
        receive(functools.partial(flow_rows, s, k), lat_sides)
        if s == 0:
            cells(s, src, c1, 2, PAD, at, WINDOWS[k])
            on_sides(functools.partial(step_rows, k), lat_sides)
            if k == 0:
                on_sides(functools.partial(strip, 1), lon_sides)
        else:
            cells(s, src, out_ref, 0, 0, at, WINDOWS[k])

    def finish(s):
        for f in (K, W):
            item = (s, f, 0)

            @pl.when(t < n - 1)
            def _(item=item):
                up_copy(item, wide=True).wait_send()

            @pl.when(t > 0)
            def _(item=item):
                down_copy(item, wide=True).wait_send()

            @pl.when(ends)
            def _(item=item):
                far_copy(item, wide=True).wait_send()

            @pl.when(middle)
            def _(item=item):
                relay_copy(item, wide=True).wait_send()

        on_sides(functools.partial(strip, s), lon_sides, "wait_send")
        on_sides(functools.partial(flow_strip, s), lon_sides, "wait_send")
        for i in lat_sides:
            @pl.when(sides[i][0])
            def _(i=i):
                kv, two = pl.ds(K, 2), pl.ds(0, 2)
                field = (c0, c1)[s].at[:, two, inner]
                side_copy(flow.at[s, kv, 1, inner], flow.at[s, kv, 1, inner],
                          kvs.at[s, i], kvr.at[s, i, 0], i).wait_send()
                side_copy(field, field, (c0s, c1s)[s].at[i], (c0r, c1r)[s].at[i, 0], i).wait_send()
    def finish_start():
        on_sides(frac_strip, lon_sides, "wait_send")
        on_sides(info_copy, lat_sides, "wait_send")

        @pl.when((la == 0) | (la == n_lat - 1))
        def _():
            pltpu.make_async_copy(passing, passing, rbs).wait()

    for i, item in enumerate(order):
        if i == len(order) - SETTLE:
            finish_start()
            finish(0)
        arrive(item)
        after(i)
        pass_all(PASSES.get(i, ()))
        if i == PREPARED:
            prepare()
        if i == LATER:
            pl.when(lo != 0)(early_rows)
        due = [
            {(s, k) for s in range(STEPS) for k in range(PARTS)
             if i == min(order.index((s, W, k)) + lags[s], len(order) - 1)}
            for lags in (END_LAGS, MIDDLE_LAGS)
        ]
        for s, k in sorted(due[0] | due[1]):
            here = [(s, k) in those for those in due]
            if all(here):
                window(s, k)
            else:
                pl.when(ends if here[0] else middle)(functools.partial(window, s, k))

    finish(STEPS - 1)


def fused_body(counts, tracers, land_mask, bottom_level, bottom_part, velocity, upwelling,
               diffusivity):
    tracer_count, rows, cols, levels = tracers.shape
    wide = cols + 2 * PAD
    row = (cols, levels)
    dma = pltpu.SemaphoreType.DMA
    hbm, vmem = pl.BlockSpec(memory_space=pltpu.HBM), pl.BlockSpec(memory_space=pltpu.VMEM)
    return pl.pallas_call(
        functools.partial(transport_kernel, counts),
        out_shape=pltpu.VMEM(tracers.shape, jnp.float32),
        in_specs=[hbm] * 7,
        out_specs=vmem,
        scratch_shapes=[
            pltpu.VMEM((tracer_count, rows + 4, wide + PAD, levels), jnp.float32),
            pltpu.VMEM((tracer_count, rows + 4, wide + PAD, levels), jnp.float32),
            pltpu.VMEM((STEPS, 4, rows + 2, wide, levels), jnp.float32),
            pltpu.VMEM((rows + 2, wide, levels), jnp.float32),
            pltpu.VMEM((tracer_count, rows, cols + 16, levels), jnp.float32),
            pltpu.VMEM((3, 24, 128), jnp.float32),
            pltpu.VMEM((rows, cols), jnp.int32),
            pltpu.VMEM((rows, cols), jnp.int32),
            pltpu.VMEM((rows, cols), jnp.float32),
            dma((STEPS, 4)), dma, dma((3,)),
            dma((STEPS, 2, 3)), dma((STEPS, 2, PARTS, 3)),
            dma((2,)), dma((2, PARTS)), dma((2,)), dma((2, PARTS)),
            dma((STEPS, 2)), dma((STEPS, 2)),
            dma((STEPS, 2)), dma((STEPS, 2, PARTS)),
            dma((STEPS, 2)), dma((STEPS, 2)),
            dma((2,)), dma((2,)), dma((2,)), dma((2,)),
            dma, dma((PARTS,)), pltpu.SemaphoreType.REGULAR((5,)),
            pltpu.VMEM((tracer_count, 2, cols, levels), jnp.float32),
            pltpu.VMEM((rows, cols, levels), jnp.float32),
            pltpu.VMEM((rows, cols, levels), jnp.float32),
        ],
        compiler_params=pltpu.CompilerParams(
            collective_id=0, has_side_effects=True, vmem_limit_bytes=60 * 1024 * 1024
        ),
    )(
        tracers,
        velocity.reshape((STEPS, 2) + row),
        upwelling.reshape((STEPS,) + row),
        diffusivity.reshape((STEPS,) + row),
        land_mask, bottom_level, bottom_part,
    )


def solution(mesh):
    placed = (
        P("trc", "lat", "lon", None),
        P("lat", "lon"),
        P("lat", "lon"),
        P("lat", "lon"),
        P(None, None, ("lat", "lon"), "trc"),
        P(None, ("lat", "lon"), "trc"),
        P(None, ("lat", "lon"), "trc"),
    )
    counts = tuple(mesh.shape[axis] for axis in ("trc", "lat", "lon"))

    def body(*arrays):
        tracers, velocity = arrays[0], arrays[4]
        one_row = velocity.shape[3] == tracers.shape[2] * tracers.shape[3]
        blocks = tracers.shape[1] == 4 and tracers.shape[2] == 64 and tracers.shape[3] == 128
        if counts == (4, 4, 2) and blocks and one_row:
            return fused_body(counts, *arrays)
        return gathered_body(*arrays)

    return jax.shard_map(
        body, mesh=mesh, in_specs=placed, out_specs=P("trc", "lat", "lon", None), check_vma=False
    )
```
